32 devices in a mesh: dp: 16 (over z, y, core), tensor: 2 (over x).
Axes of the slice: x: 2, y: 2, z: 4, core: 2. Of those that a mesh axis runs over, the one named last changes fastest.
Arguments:
- block_input: bfloat16 [16384, 1024], P(('dp', 'tensor'))
- positions: int32 [16384], P('dp'), may hold values from 0 to 1023, as said below
- expert_ids: int32 [16384, 8], P('dp'), may hold values from 0 to 31, all different within a row
- attn_gain: float32 [1024], replicated, may hold values from 0.1 to 1.9
- query_weight: bfloat16 [1024, 1024], P('dp', 'tensor'), may hold values from -2 to 2
- kv_weight: bfloat16 [1024, 8, 128], P('dp', 'tensor'), may hold values from -0.1875 to 0.1875
- out_weight: bfloat16 [1024, 1024], P('tensor', 'dp'), may hold values from -6 to 6
- ffn_gain: float32 [1024], replicated, may hold values from 0.1 to 1.9
- router_weight: bfloat16 [1024, 32], replicated, may hold values from -0.09375 to 0.09375
- gate_weight: bfloat16 [32, 1024, 512], P('tensor', 'dp'), may hold values from -0.1875 to 0.1875
- up_weight: bfloat16 [32, 1024, 512], P('tensor', 'dp'), may hold values from -0.1875 to 0.1875
- down_weight: bfloat16 [32, 512, 1024], P('tensor', 'dp'), may hold values from -4 to 4
- out_grad: bfloat16 [16384, 1024], P(('dp', 'tensor')), may hold values from -6 to 6
Outputs:
- block_output: bfloat16 [16384, 1024], P(('dp', 'tensor'))
- input_grad: bfloat16 [16384, 1024], P(('dp', 'tensor'))
- attn_gain_grad: float32 [1024], replicated
- query_grad: float32 [1024, 1024], P('dp', 'tensor')
- kv_grad: float32 [1024, 8, 128], P('dp', 'tensor')
- out_weight_grad: float32 [1024, 1024], P('tensor', 'dp')
- ffn_gain_grad: float32 [1024], replicated
- router_grad: float32 [1024, 32], replicated
- gate_grad: float32 [32, 1024, 512], P('tensor', 'dp')
- up_grad: float32 [32, 1024, 512], P('tensor', 'dp')
- down_grad: float32 [32, 512, 1024], P('tensor', 'dp')
The draws below stay inside these ranges and needn't reach their ends.
Inputs may be any that keep to these rules, and one draw needn't show every extreme that they name: `expert_ids`: each row names 8 different experts. Within each sequence of 1024 tokens, positions count up by one from 0 at the first token of each packed document; every sequence's first token begins a document, and the first sequence is one whole document.
All inputs are finite; a program needn't handle non-finite values.
Results may differ from the reference program's by a relative error of at most 0.02.
Values may be sent and summed in bfloat16 or wider, within the bound.
No kernel may reach another device: no remote copies, remote signals or barrier semaphores. Data moves between devices by JAX's collectives and lax.ppermute only.
A program may use at most 320 MiB of HBM per device.

```python
import jax
import jax.numpy as jnp
from jax import lax

D = 1024
HEADS = 16
KV_HEADS = 8
HEAD_DIM = 64
FF = 512
EXPERTS = 32
TOP = 8
SEQ = 1024
CAP = 320
TOKENS = 16384
N_DP = 16


def draw_block_input(key, part):
    key_base, key_rows, key_cols = jax.random.split(key, 3)
    row_place = jnp.arange(TOKENS, dtype=jnp.float32) / TOKENS
    row_scales = jnp.exp(1.1 * (row_place - 0.5) + jax.random.uniform(key_rows, (TOKENS,), minval=-0.6, maxval=0.6))
    col_scales = jnp.exp(jax.random.uniform(key_cols, (D,), minval=-1.15, maxval=1.15))
    base_vals = jax.random.normal(key_base, (TOKENS, D))
    return (base_vals * row_scales[:, None] * col_scales[None, :]).astype(jnp.bfloat16)


def draw_positions(key, part):
    token_ids = jnp.arange(TOKENS, dtype=jnp.int32)
    random_begin = (jax.random.randint(key, (TOKENS,), 0, max(SEQ // 4, 2)) == 0) & (token_ids >= SEQ)
    begins = random_begin | (token_ids % SEQ == 0)
    last_begin = lax.cummax(jnp.where(begins, token_ids, 0), axis=0)
    return token_ids - last_begin


def steps_of(own_key, extent, shards, low, top_value):
    loudness, own = 1.0, jax.random.fold_in(own_key, 6)
    for axis_at, shards_of in shards:
        draws = jnp.exp(jax.random.uniform(jax.random.fold_in(own, axis_at), (shards_of,), jnp.float32, low / len(shards), top_value / len(shards)))
        loudness = loudness * jnp.repeat(draws, extent[axis_at] // shards_of).reshape([-1 if axis == axis_at else 1 for axis in range(len(extent))])
    return loudness


def distinct(stream_key, rows, number_of, top, lift):
    ranking = jax.random.permutation(jax.random.fold_in(stream_key, 1), number_of)
    favour = ranking
    for power in range(3):
        favour = favour * favour // number_of
    favour = favour * lift // number_of
    lots = jax.random.randint(jax.random.fold_in(stream_key, 2), (rows, number_of), 0, 4096) + favour
    holders = jax.random.permutation(jax.random.fold_in(stream_key, 3), rows)[jnp.arange(number_of) % rows]
    lots = jnp.where(jnp.arange(rows)[:, None] == holders[None, :], 1 << 14, lots)
    merit = lots * number_of + jnp.arange(number_of)
    return lax.top_k(merit.astype(jnp.int32), top)[1].astype(jnp.int32)


def gaussian(key, shape, deviation, bound, shards=(), held_as=jnp.bfloat16):
    entries = deviation * jax.random.normal(key, shape, jnp.float32)
    if shards:
        entries = entries * steps_of(key, shape, shards, -0.22, 0.18)
    return jnp.clip(entries, -bound, bound).astype(held_as)


def setup_inputs(seed: int = 0) -> dict:
    key_of = jax.random.split(jax.random.key(seed), 14)
    block_input = draw_block_input(jax.random.fold_in(key_of[13], 71), 0)
    positions = draw_positions(jax.random.fold_in(key_of[13], 71), 0)
    expert_ids = distinct(key_of[2], TOKENS, EXPERTS, TOP, 2048)
    attn_gain = jnp.clip(1.0 + 0.18 * jax.random.normal(key_of[3], (D,), jnp.float32), 0.1, 1.9)
    query_weight = gaussian(key_of[4], (D, HEADS * HEAD_DIM), (12 / D ** 0.5), 2.0, ((0, 16), (1, 2)))
    kv_weight = gaussian(key_of[5], (D, KV_HEADS, 2 * HEAD_DIM), D ** -0.5, 0.1875, ((0, 16), (1, 2)))
    out_weight = gaussian(key_of[6], (HEADS * HEAD_DIM, D), 1.0, 6.0, ((0, 2), (1, 16)))
    ffn_gain = jnp.clip(1.0 + 0.18 * jax.random.normal(key_of[7], (D,), jnp.float32), 0.1, 1.9)
    router_weight = gaussian(key_of[8], (D, EXPERTS), (0.5 / D ** 0.5), 0.09375)
    gate_weight = gaussian(key_of[9], (EXPERTS, D, FF), D ** -0.5, 0.1875, ((0, 2), (1, 16)))
    up_weight = gaussian(key_of[10], (EXPERTS, D, FF), D ** -0.5, 0.1875, ((0, 2), (1, 16)))
    down_weight = gaussian(key_of[11], (EXPERTS, FF, D), (16 / FF ** 0.5), 4.0, ((0, 2), (1, 16)))
    out_grad = gaussian(key_of[12], (TOKENS, D), 1.0, 6.0, ((0, 32),))
    return dict(block_input=block_input, positions=positions, expert_ids=expert_ids, attn_gain=attn_gain, query_weight=query_weight, kv_weight=kv_weight, out_weight=out_weight, ffn_gain=ffn_gain, router_weight=router_weight, gate_weight=gate_weight, up_weight=up_weight, down_weight=down_weight, out_grad=out_grad)


norm_eps = 1e-06
attn_scale = 0.015625
residual_scale = 0.22
rope_base = 10000.0
masked_score = -1e+30
highest = lax.Precision.HIGHEST

@jax.custom_vjp
def low(v):
    return lax.optimization_barrier(v.astype(jnp.bfloat16)).astype(jnp.float32)

@jax.custom_vjp
def low_back(v):
    return v

def low_keep(v):
    return (low(v), None)

def low_pass(kept, grad):
    return (grad,)

def back_keep(v):
    return (v, None)

def back_low(kept, grad):
    return (low(grad),)
low.defvjp(low_keep, low_pass)
low_back.defvjp(back_keep, back_low)

def row_scale(values):
    return lax.rsqrt(lax.optimization_barrier(jnp.mean(values * values, axis=-1, keepdims=True)) + norm_eps)

def rotary(values, positions, direction):
    head_dim = values.shape[-1]
    half_dim = head_dim // 2
    frequency = rope_base ** (-(jnp.arange(half_dim, dtype=jnp.float32) * 2.0 / head_dim))
    angles = positions.astype(jnp.float32)[:, None] * frequency[None, :]
    cosine = jnp.concatenate([jnp.cos(angles), jnp.cos(angles)], axis=-1)[:, None, :]
    sine_table = jnp.concatenate([jnp.sin(angles), jnp.sin(angles)], axis=-1)[:, None, :]
    rotated = jnp.concatenate([-values[..., half_dim:], values[..., :half_dim]], axis=-1)
    return values * cosine + direction * rotated * sine_table

def pair_rank(expert_ids, expert_count):
    flat_ids = expert_ids.reshape(-1)
    one_hot = (flat_ids[:, None] == jnp.arange(expert_count, dtype=jnp.int32)[None, :]).astype(jnp.int32)
    earlier = jnp.cumsum(one_hot, axis=0) - one_hot
    return lax.optimization_barrier(jnp.sum(earlier * one_hot, axis=1)).reshape(expert_ids.shape).astype(jnp.int32)

def attend(query, keys, values_in):
    seq_len, kv_heads, repeat, head_dim = query.shape
    block_rows = min(512, seq_len)
    key_pos = jnp.arange(seq_len)

    @jax.checkpoint
    def one_block(block_items):
        q_block, first_row = block_items
        row_pos = first_row + jnp.arange(block_rows)
        scores = jnp.einsum('bgrd,sgd->grbs', q_block, keys, precision=highest)
        scores = low_back(attn_scale * scores)
        scores = jnp.where(key_pos[None, None, None, :] <= row_pos[None, None, :, None], scores, masked_score)
        top_score = lax.optimization_barrier(jnp.max(scores, axis=-1, keepdims=True))
        log_total = top_score + jnp.log(lax.optimization_barrier(jnp.sum(jnp.exp(scores - top_score), axis=-1, keepdims=True)))
        prob_vals = jnp.exp(scores - log_total)
        blended = jnp.einsum('grbs,sgd->bgrd', low(prob_vals), values_in, precision=highest)
        return low(low_back(blended))
    q_blocks = query.reshape(seq_len // block_rows, block_rows, kv_heads, repeat, head_dim)
    starts = jnp.arange(seq_len // block_rows) * block_rows
    return lax.map(one_block, (q_blocks, starts)).reshape(seq_len, kv_heads * repeat * head_dim)

def layer(block_in, params, positions, expert_ids):
    attn_gain, query_weight, kv_weight, out_weight, ffn_gain, router_weight, gate_weight, up_weight, down_weight = params
    seq_len = block_in.shape[0]
    kv_heads = kv_weight.shape[1]
    head_dim = kv_weight.shape[2] // 2
    head_count = query_weight.shape[1] // head_dim
    attn_normed = low(block_in * row_scale(block_in) * attn_gain)
    query_pre = low_back(jnp.dot(attn_normed, query_weight, precision=highest))
    kv_pre = low_back(jnp.einsum('sd,dgk->sgk', attn_normed, kv_weight, precision=highest))
    query_rot = low(rotary(query_pre.reshape(seq_len, head_count, head_dim), positions, 1.0))
    key_rot = low(rotary(kv_pre[..., :head_dim], positions, 1.0))
    value_low = low(kv_pre[..., head_dim:])
    attn_mixed = attend(query_rot.reshape(seq_len, kv_heads, head_count // kv_heads, head_dim), key_rot, value_low)
    attn_out = low_back(jnp.dot(attn_mixed, out_weight, precision=highest))
    hidden_state = block_in + residual_scale * attn_out
    ffn_normed = low(hidden_state * row_scale(hidden_state) * ffn_gain)
    logits = low_back(jnp.dot(ffn_normed, router_weight, precision=highest))
    selected = jnp.take_along_axis(logits, expert_ids, axis=1)
    top_logit = lax.optimization_barrier(jnp.max(selected, axis=1, keepdims=True))
    raised = jnp.exp(selected - top_logit)
    gate_vals = raised / lax.optimization_barrier(jnp.sum(raised, axis=1, keepdims=True))
    expert_count = router_weight.shape[1]
    ranks = pair_rank(expert_ids, expert_count)
    slot_index = jnp.where(ranks < CAP, expert_ids * CAP + ranks, expert_count * CAP).astype(jnp.int32)
    token_ids = jnp.broadcast_to(jnp.arange(seq_len, dtype=jnp.int32)[:, None], expert_ids.shape)
    slot_token = jnp.full((expert_count * CAP + 1,), seq_len, jnp.int32).at[slot_index.reshape(-1)].set(token_ids.reshape(-1))[:-1]
    slot_gate = jnp.zeros((expert_count * CAP + 1,), jnp.float32).at[slot_index.reshape(-1)].add(gate_vals.reshape(-1))[:-1]
    padded = jnp.concatenate([ffn_normed, jnp.zeros((1, ffn_normed.shape[1]), jnp.float32)], axis=0)
    expert_in = low_back(padded[slot_token].reshape(expert_count, CAP, -1))
    gate_pre = low_back(jnp.einsum('ecd,edf->ecf', expert_in, gate_weight, precision=highest))
    up_pre = low_back(jnp.einsum('ecd,edf->ecf', expert_in, up_weight, precision=highest))
    hidden_act = low(jax.nn.silu(gate_pre) * up_pre)
    expert_out = low_back(jnp.einsum('ecf,efd->ecd', hidden_act, down_weight, precision=highest))
    weighted = low(slot_gate.reshape(expert_count, CAP, 1) * expert_out)
    stacked = jnp.concatenate([weighted.reshape(expert_count * CAP, -1), jnp.zeros((1, weighted.shape[2]), jnp.float32)], axis=0)
    moe_out = low_back(lax.optimization_barrier(jnp.sum(stacked[slot_index], axis=1)))
    return hidden_state + residual_scale * moe_out

def reference(block_input, positions, expert_ids, attn_gain, query_weight, kv_weight, out_weight, ffn_gain, router_weight, gate_weight, up_weight, down_weight, out_grad):
    weights = tuple((item.astype(jnp.float32) for item in (attn_gain, query_weight, kv_weight, out_weight, ffn_gain, router_weight, gate_weight, up_weight, down_weight)))
    seq_inputs = block_input.astype(jnp.float32).reshape(N_DP, SEQ, D)
    seq_grads = out_grad.astype(jnp.float32).reshape(N_DP, SEQ, D)
    seq_pos = positions.reshape(N_DP, SEQ)
    seq_ids = expert_ids.reshape(N_DP, SEQ, TOP)

    def one_sequence(totals, step_items):
        seq_in, pos_now, ids_now, grad_now = step_items

        def forward(value_in, params):
            return layer(value_in, params, pos_now, ids_now)
        result, pullback = jax.vjp(forward, seq_in, weights)
        input_cot, weight_cot = pullback(grad_now)
        totals = tuple((left + right for left, right in zip(totals, weight_cot)))
        return (totals, (result, input_cot))
    zero_grads = tuple((jnp.zeros_like(item) for item in weights))
    totals, (outputs, input_cots) = lax.scan(one_sequence, zero_grads, (seq_inputs, seq_pos, seq_ids, seq_grads))
    block_output = outputs.reshape(TOKENS, D).astype(jnp.bfloat16)
    input_grad = input_cots.reshape(TOKENS, D).astype(jnp.bfloat16)
    return (block_output, input_grad, totals[0], totals[1], totals[2], totals[3], totals[4], totals[5], totals[6], totals[7], totals[8])
```

```python
import functools

import jax
import jax.numpy as jnp
from jax import lax
from jax.sharding import Mesh, PartitionSpec as P

CAP = 320
norm_eps = 1e-06
attn_scale = 0.015625
residual_scale = 0.22
rope_base = 10000.0
masked_score = -1e30
f32 = jnp.float32
bf16 = jnp.bfloat16


def row_scale(values):
    return lax.rsqrt(jnp.mean(values * values, axis=-1, keepdims=True) + norm_eps)


def rope_tables(positions, head_dim):
    half_dim = head_dim // 2
    frequency = rope_base ** (-(jnp.arange(half_dim, dtype=f32) * 2.0 / head_dim))
    angles = positions.astype(f32)[:, None] * frequency[None, :]
    cosine, sine = jnp.cos(angles), jnp.sin(angles)
    return (
        jnp.concatenate([cosine, cosine], axis=-1)[:, None, :],
        jnp.concatenate([sine, sine], axis=-1)[:, None, :],
    )


def rotary(values, tables, direction):
    half_dim = values.shape[-1] // 2
    cosine, sine = tables
    rotated = jnp.concatenate([-values[..., half_dim:], values[..., :half_dim]], axis=-1)
    return values * cosine + direction * rotated * sine


def contract(left, right, left_dim, right_dim):
    return lax.dot_general(
        left, right, (((left_dim,), (right_dim,)), ((), ())), preferred_element_type=f32
    )


def ein(spec, *operands):
    return jnp.einsum(spec, *operands, preferred_element_type=f32)


def norm_backward(normed_grad, source, gain):
    scale_rows = row_scale(source)
    unit_rows = source * scale_rows
    scaled_grad = normed_grad * gain
    gain_grad = jnp.sum(normed_grad * unit_rows, axis=0)
    source_grad = scale_rows * (
        scaled_grad - unit_rows * jnp.mean(scaled_grad * unit_rows, axis=-1, keepdims=True)
    )
    return (source_grad, gain_grad)


def swap(values, axis):
    return lax.ppermute(values, axis, [(0, 1), (1, 0)])


def butterfly_sum(values, sizes):
    for axis, size in sizes:
        step = 1
        while step < size:
            values = values + lax.ppermute(values, axis, [(i, i ^ step) for i in range(size)])
            step *= 2
    return values


def in_order(mine, theirs, first):
    return jnp.concatenate(
        [jnp.where(first, mine, theirs), jnp.where(first, theirs, mine)], axis=0
    )


def gather_rows(rows, tensor_size):
    if tensor_size != 2:
        return lax.all_gather(rows, "tensor", axis=0, tiled=True)
    return in_order(rows, swap(rows, "tensor"), lax.axis_index("tensor") == 0)


def scatter_rows(values, tensor_size):
    if tensor_size != 2:
        return lax.psum_scatter(
            values.astype(bf16), "tensor", scatter_dimension=0, tiled=True
        ).astype(f32)
    half = values.shape[0] // 2
    me = lax.axis_index("tensor")
    give = lax.dynamic_slice_in_dim(values, (1 - me) * half, half, 0).astype(bf16)
    keep = lax.dynamic_slice_in_dim(values, me * half, half, 0)
    return keep.astype(f32) + swap(give, "tensor").astype(f32)


def gather_group(rows, tensor_size):
    if tensor_size != 2:
        own = gather_rows(rows, tensor_size)
        across = swap(own, "y")
    else:
        first = lax.axis_index("tensor") == 0
        half = rows.shape[0] // 2
        by_tensor, by_y = swap(rows, "tensor"), swap(rows, "y")
        corner = jnp.concatenate(
            [swap(by_y[:half], "tensor"), swap(by_tensor[half:], "y")], axis=0
        )
        own = in_order(rows, by_tensor, first)
        across = in_order(by_y, corner, first)
    return jnp.stack([own, across, swap(own, "core"), swap(across, "core")])


def scatter_group(parts, tensor_size):
    pair = [parts[i].astype(f32) + swap(parts[i + 2].astype(bf16), "core").astype(f32) for i in (0, 1)]
    own, across = pair
    if tensor_size != 2:
        own = own + swap(across.astype(bf16), "y").astype(f32)
        return scatter_rows(own, tensor_size)
    me = lax.axis_index("tensor")
    rows = own.shape[0] // 2
    half = rows // 2

    def take(values, which):
        return lax.dynamic_slice_in_dim(values, which * rows, rows, 0)

    mine, by_tensor = take(own, me), take(own, 1 - me)
    by_y, corner = take(across, me), take(across, 1 - me).astype(bf16)
    low, high = swap(corner[:half], "tensor"), swap(corner[half:], "y")
    by_y = jnp.concatenate([by_y[:half] + low.astype(f32), by_y[half:]], axis=0)
    by_tensor = jnp.concatenate([by_tensor[:half], by_tensor[half:] + high.astype(f32)], axis=0)
    return (
        mine
        + swap(by_tensor.astype(bf16), "tensor").astype(f32)
        + swap(by_y.astype(bf16), "y").astype(f32)
    )


def split_low(values, count):
    pieces = []
    for _ in range(count):
        piece = values.astype(bf16)
        pieces.append(piece)
        values = values - piece.astype(f32)
    return pieces


def attention_forward(query, keys, values_in):
    seq_len = query.shape[0]
    block = min(512, seq_len)
    mixed, log_totals = [], []
    for start in range(0, seq_len, block):
        stop = start + block
        scores = masked_scores(query[start:stop], keys[:stop], start)
        top_score = jnp.max(scores, axis=-1, keepdims=True)
        log_total = top_score + jnp.log(
            jnp.sum(jnp.exp(scores - top_score), axis=-1, keepdims=True)
        )
        prob_vals = jnp.exp(scores - log_total).astype(bf16)
        blended = ein("grbs,sgd->bgrd", prob_vals, values_in[:stop])
        mixed.append(blended.astype(bf16).reshape(block, -1))
        log_totals.append(log_total)
    return jnp.concatenate(mixed, axis=0), log_totals


def masked_scores(q_block, keys, start):
    scores = ein("bgrd,sgd->grbs", q_block, keys) * attn_scale
    row_pos = start + jnp.arange(q_block.shape[0])
    key_pos = jnp.arange(keys.shape[0])
    return jnp.where(
        key_pos[None, None, None, :] <= row_pos[None, None, :, None], scores, masked_score
    )


def attention_backward(query, keys, values_in, log_totals, mixed_grad):
    seq_len = query.shape[0]
    block = min(512, seq_len)
    query_grads = []
    key_grad = value_grad = None
    for index, start in reversed(list(enumerate(range(0, seq_len, block)))):
        stop = start + block
        q_block, g_block = query[start:stop], mixed_grad[start:stop]
        scores = masked_scores(q_block, keys[:stop], start)
        prob_vals = jnp.exp(scores - log_totals[index])
        prob_grad = ein("bgrd,sgd->grbs", g_block, values_in[:stop])
        row_dot = jnp.sum(prob_vals * prob_grad, axis=-1, keepdims=True)
        score_grad = (prob_vals * (prob_grad - row_dot)).astype(bf16)
        query_grads.append(ein("grbs,sgd->bgrd", score_grad, keys[:stop]) * attn_scale)
        key_step = ein("grbs,bgrd->sgd", score_grad, q_block) * attn_scale
        value_step = ein("grbs,bgrd->sgd", prob_vals.astype(bf16), g_block)
        if key_grad is None:
            key_grad, value_grad = key_step, value_step
        else:
            pad = ((0, seq_len - stop), (0, 0), (0, 0))
            key_grad = key_grad + jnp.pad(key_step, pad)
            value_grad = value_grad + jnp.pad(value_step, pad)
    return jnp.concatenate(query_grads[::-1], axis=0), key_grad, value_grad


def shards(
    sizes,
    block_input,
    positions,
    expert_ids,
    attn_gain,
    query_weight,
    kv_weight,
    out_weight,
    ffn_gain,
    router_weight,
    gate_weight,
    up_weight,
    down_weight,
    out_grad,
):
    tensor_size = sizes["tensor"]
    every_dp = ("z", "y", "core")
    seq_len = positions.shape[0]
    width = block_input.shape[1]
    kv_local = kv_weight.shape[1]
    head_dim = kv_weight.shape[2] // 2
    heads_local = query_weight.shape[1] // head_dim
    q_width, kv_width = heads_local * head_dim, kv_local * 2 * head_dim
    expert_count = router_weight.shape[1]
    experts_local = gate_weight.shape[0]
    owned = experts_local // 4
    hidden_width = gate_weight.shape[2]

    packed = jnp.concatenate(
        [query_weight, kv_weight.reshape(kv_weight.shape[0], -1), out_weight.T], axis=1
    )
    packed_full = lax.all_gather(packed, every_dp, axis=0, tiled=True)
    qkv_full = packed_full[:, : q_width + kv_width]
    out_full = packed_full[:, q_width + kv_width :]

    def to_owner(weight):
        return lax.all_to_all(weight, ("y", "core"), 0, 1, tiled=True)

    def from_owner(grad):
        return lax.all_to_all(grad, ("y", "core"), 1, 0, tiled=True)

    both = jnp.concatenate([to_owner(gate_weight), to_owner(up_weight)], axis=2)
    both_full = lax.all_gather(both, "z", axis=1, tiled=True)
    down_full = lax.all_gather(to_owner(down_weight), "z", axis=1, tiled=True)

    grad_rows = out_grad.astype(f32)
    moe_grad = gather_group((residual_scale * grad_rows).astype(bf16), tensor_size)

    ids_t = expert_ids.T
    hits = jnp.zeros((expert_count, seq_len), jnp.bool_)
    for k in range(ids_t.shape[0]):
        hits = hits | (ids_t[k][None, :] == jnp.arange(expert_count)[:, None])
    token_ids = jnp.arange(seq_len)
    earlier = (token_ids[:, None] < token_ids[None, :]).astype(bf16)
    rank = jnp.dot(hits.astype(bf16), earlier, preferred_element_type=f32)
    code = jnp.where(hits, jnp.where(rank < CAP, rank, -1.0), -2.0)
    code_y = swap(code, "y")
    codes = jnp.stack([code, code_y, swap(code, "core"), swap(code_y, "core")])

    input_rows = block_input.astype(f32)
    attn_normed = (input_rows * row_scale(input_rows) * attn_gain).astype(bf16)
    attn_tokens = gather_rows(attn_normed, tensor_size)
    tables = rope_tables(positions, head_dim)
    qkv_pre = jnp.dot(attn_tokens, qkv_full, preferred_element_type=f32)
    query_pre = qkv_pre[:, :q_width].reshape(seq_len, heads_local, head_dim)
    kv_pre = qkv_pre[:, q_width:].reshape(seq_len, kv_local, 2 * head_dim)
    query_rot = (
        rotary(query_pre, tables, 1.0)
        .astype(bf16)
        .reshape(seq_len, kv_local, heads_local // kv_local, head_dim)
    )
    key_rot = rotary(kv_pre[..., :head_dim], tables, 1.0).astype(bf16)
    value_low = kv_pre[..., head_dim:].astype(bf16)
    attn_mixed, log_totals = attention_forward(query_rot, key_rot, value_low)
    attn_out = scatter_rows(contract(attn_mixed, out_full, 1, 1), tensor_size)
    hidden_state = input_rows + residual_scale * attn_out
    ffn_normed = (hidden_state * row_scale(hidden_state) * ffn_gain).astype(bf16)

    tokens = gather_group(ffn_normed, tensor_size)
    logits = ein("dx,std->sxt", router_weight, tokens)
    chosen = codes > -1.5
    top_logit = jnp.max(jnp.where(chosen, logits, -jnp.inf), axis=1, keepdims=True)
    raised = jnp.where(chosen, jnp.exp(jnp.where(chosen, logits - top_logit, 0.0)), 0.0)
    gates = raised / jnp.sum(raised, axis=1, keepdims=True)
    expert_first = (
        lax.axis_index("tensor") * experts_local
        + (lax.axis_index("y") * 2 + lax.axis_index("core")) * owned
    )
    code_own = lax.dynamic_slice_in_dim(codes, expert_first, owned, 1)
    gate_own = lax.dynamic_slice_in_dim(gates, expert_first, owned, 1)
    slot_ids = jnp.arange(CAP, dtype=jnp.int32)
    dispatch = (code_own.astype(jnp.int32)[:, :, None, :] == slot_ids[:, None]).astype(bf16)

    gate_cols = jnp.stack(split_low(gate_own, 3), axis=-1)
    slot_gate = jnp.sum(ein("sect,setk->seck", dispatch, gate_cols), axis=-1)[..., None]
    expert_in = ein("sect,std->secd", dispatch, tokens).astype(bf16)
    both_pre = ein("secd,edf->secf", expert_in, both_full)
    gate_pre, up_pre = both_pre[..., :hidden_width], both_pre[..., hidden_width:]
    hidden_act = (jax.nn.silu(gate_pre) * up_pre).astype(bf16)
    expert_out = ein("secf,efd->secd", hidden_act, down_full)
    weighted = (slot_gate * expert_out).astype(bf16)
    moe_parts = ein("sect,secd->std", dispatch, weighted).astype(bf16)
    moe_out = scatter_group(moe_parts, tensor_size)
    block_output = (hidden_state + residual_scale * moe_out).astype(bf16)

    slot_grad = ein("sect,std->secd", dispatch, moe_grad)
    out_slot_grad = (slot_gate * slot_grad).astype(bf16)
    down_part = ein("secf,secd->efd", hidden_act, out_slot_grad).astype(bf16)
    raw_hidden_grad = ein("secd,efd->secf", slot_grad.astype(bf16), down_full)
    slot_gate_grad = jnp.sum(hidden_act.astype(f32) * raw_hidden_grad, axis=-1)
    hidden_grad = slot_gate * raw_hidden_grad
    sigmoid_gate = jax.nn.sigmoid(gate_pre)
    both_pre_grad = jnp.concatenate(
        [
            hidden_grad * up_pre * sigmoid_gate * (1.0 + gate_pre * (1.0 - sigmoid_gate)),
            hidden_grad * gate_pre * sigmoid_gate,
        ],
        axis=-1,
    ).astype(bf16)
    both_part = ein("secd,secf->edf", expert_in, both_pre_grad).astype(bf16)
    in_grad = ein("secf,edf->secd", both_pre_grad, both_full).astype(bf16)
    normed_parts = ein("sect,secd->std", dispatch, in_grad).astype(bf16)
    grad_cols = jnp.stack(split_low(slot_gate_grad, 3), axis=-1)
    pair_grad = jnp.sum(ein("sect,seck->setk", dispatch, grad_cols), axis=-1)
    gate_dot = jnp.sum(gate_own * pair_grad, axis=1, keepdims=True)
    pair_all = lax.dynamic_update_slice_in_dim(jnp.zeros_like(gates), pair_grad, expert_first, 1)
    logit_parts = jnp.swapaxes(gates * (pair_all - gate_dot), 1, 2).astype(bf16)
    normed_local = scatter_group(normed_parts, tensor_size)
    logit_low = scatter_group(logit_parts, tensor_size).astype(bf16)

    down_sum = from_owner(
        lax.psum_scatter(down_part, "z", scatter_dimension=1, tiled=True)
    ).astype(f32)
    both_sum = lax.psum_scatter(both_part, "z", scatter_dimension=1, tiled=True)
    gate_sum = from_owner(both_sum[..., :hidden_width]).astype(f32)
    up_sum = from_owner(both_sum[..., hidden_width:]).astype(f32)

    normed_local = normed_local + contract(logit_low, router_weight, 1, 1)
    router_part = contract(logit_low, ffn_normed, 0, 0)
    state_grad, ffn_gain_part = norm_backward(normed_local, hidden_state, ffn_gain)
    state_grad = state_grad + grad_rows
    steps = (
        ("core", 2),
        ("y", 2),
        ("tensor", tensor_size),
        ("z", sizes["z"]),
    )
    early_sum = butterfly_sum(
        jnp.concatenate([router_part, ffn_gain_part[None, :]], axis=0), steps
    )
    router_grad, ffn_gain_grad = early_sum[:expert_count].T, early_sum[expert_count]

    attn_grad_all = gather_rows((residual_scale * state_grad).astype(bf16), tensor_size)
    out_part = contract(attn_grad_all, attn_mixed, 0, 0).astype(bf16)
    out_sum = lax.psum_scatter(out_part, every_dp, scatter_dimension=0, tiled=True)
    mixed_grad = jnp.dot(attn_grad_all, out_full, preferred_element_type=f32)
    mixed_grad = mixed_grad.astype(bf16).reshape(query_rot.shape)
    query_grad, key_grad, value_grad = attention_backward(
        query_rot, key_rot, value_low, log_totals, mixed_grad
    )
    query_pre_grad = rotary(
        query_grad.reshape(seq_len, heads_local, head_dim), tables, -1.0
    ).astype(bf16)
    kv_pre_grad = jnp.concatenate(
        [rotary(key_grad, tables, -1.0), value_grad], axis=-1
    ).astype(bf16)
    qkv_pre_grad = jnp.concatenate(
        [query_pre_grad.reshape(seq_len, q_width), kv_pre_grad.reshape(seq_len, kv_width)], axis=1
    )
    qkv_part = contract(attn_tokens, qkv_pre_grad, 0, 0).astype(bf16)
    qkv_sum = lax.psum_scatter(qkv_part, every_dp, scatter_dimension=0, tiled=True)
    attn_normed_grad = scatter_rows(contract(qkv_pre_grad, qkv_full, 1, 1), tensor_size)
    input_part, attn_gain_part = norm_backward(attn_normed_grad, input_rows, attn_gain)
    input_grad = (state_grad + input_part).astype(bf16)
    attn_gain_grad = butterfly_sum(attn_gain_part[None, :], steps)[0]
    return (
        block_output,
        input_grad,
        attn_gain_grad,
        qkv_sum[:, :q_width].astype(f32),
        qkv_sum[:, q_width:].reshape(kv_weight.shape).astype(f32),
        out_sum.T.astype(f32),
        ffn_gain_grad,
        router_grad,
        gate_sum,
        up_sum,
        down_sum,
    )


def solution(mesh):
    dp, tensor = mesh.shape["dp"], mesh.shape["tensor"]
    fine = Mesh(mesh.devices.reshape(dp // 4, 2, 2, tensor), ("z", "y", "core", "tensor"))
    rows = ("z", "y", "core")
    every = rows + ("tensor",)
    experts = P("tensor", rows, None)
    return jax.shard_map(
        functools.partial(shards, dict(fine.shape)),
        mesh=fine,
        in_specs=(
            P(every, None),
            P(rows),
            P(rows, None),
            P(),
            P(rows, "tensor"),
            P(rows, "tensor", None),
            P("tensor", rows),
            P(),
            P(),
            experts,
            experts,
            experts,
            P(every, None),
        ),
        out_specs=(
            P(every, None),
            P(every, None),
            P(),
            P(rows, "tensor"),
            P(rows, "tensor", None),
            P("tensor", rows),
            P(),
            P(),
            experts,
            experts,
            experts,
        ),
        check_vma=False,
    )
```

```python
import functools

import jax
import jax.numpy as jnp
from jax import lax
from jax.experimental import pallas as pl
from jax.experimental.pallas import tpu as pltpu
from jax.sharding import Mesh, PartitionSpec as P

CAP = 320
HEAD = 64
HALF = HEAD // 2
LANES = 2 * HEAD
BLOCK = 256
norm_eps = 1e-06
attn_scale = 0.015625
residual_scale = 0.22
rope_base = 10000.0
masked_score = -1e30
f32 = jnp.float32
bf16 = jnp.bfloat16


def row_scale(values):
    return lax.rsqrt(jnp.mean(values * values, axis=-1, keepdims=True) + norm_eps)


def contract(left, right, left_dim, right_dim):
    return lax.dot_general(
        left, right, (((left_dim,), (right_dim,)), ((), ())), preferred_element_type=f32
    )


def ein(spec, *operands):
    return jnp.einsum(spec, *operands, preferred_element_type=f32)


def norm_backward(normed_grad, source, gain):
    scale_rows = row_scale(source)
    unit_rows = source * scale_rows
    scaled_grad = normed_grad * gain
    gain_grad = jnp.sum(normed_grad * unit_rows, axis=0)
    source_grad = scale_rows * (
        scaled_grad - unit_rows * jnp.mean(scaled_grad * unit_rows, axis=-1, keepdims=True)
    )
    return (source_grad, gain_grad)


def swap(values, axis):
    return lax.ppermute(values, axis, [(0, 1), (1, 0)])


def butterfly_sum(values, sizes):
    for axis, size in sizes:
        step = 1
        while step < size:
            values = values + lax.ppermute(values, axis, [(i, i ^ step) for i in range(size)])
            step *= 2
    return values


def in_order(mine, theirs, first):
    return jnp.concatenate(
        [jnp.where(first, mine, theirs), jnp.where(first, theirs, mine)], axis=0
    )


def gather_rows(rows, tensor_size):
    if tensor_size != 2:
        return lax.all_gather(rows, "tensor", axis=0, tiled=True)
    return in_order(rows, swap(rows, "tensor"), lax.axis_index("tensor") == 0)


def scatter_rows(values, tensor_size):
    if tensor_size != 2:
        return lax.psum_scatter(
            values.astype(bf16), "tensor", scatter_dimension=0, tiled=True
        ).astype(f32)
    half = values.shape[0] // 2
    me = lax.axis_index("tensor")
    give = lax.dynamic_slice_in_dim(values, (1 - me) * half, half, 0).astype(bf16)
    keep = lax.dynamic_slice_in_dim(values, me * half, half, 0)
    return keep.astype(f32) + swap(give, "tensor").astype(f32)


def gather_group(rows, tensor_size):
    if tensor_size != 2:
        own = gather_rows(rows, tensor_size)
        across = swap(own, "y")
    else:
        first = lax.axis_index("tensor") == 0
        half = rows.shape[0] // 2
        by_tensor, by_y = swap(rows, "tensor"), swap(rows, "y")
        corner = jnp.concatenate(
            [swap(by_y[:half], "tensor"), swap(by_tensor[half:], "y")], axis=0
        )
        own = in_order(rows, by_tensor, first)
        across = in_order(by_y, corner, first)
    return jnp.stack([own, across, swap(own, "core"), swap(across, "core")])


def scatter_group(parts, tensor_size):
    pair = [parts[i].astype(f32) + swap(parts[i + 2].astype(bf16), "core").astype(f32) for i in (0, 1)]
    own, across = pair
    if tensor_size != 2:
        own = own + swap(across.astype(bf16), "y").astype(f32)
        return scatter_rows(own, tensor_size)
    me = lax.axis_index("tensor")
    rows = own.shape[0] // 2
    half = rows // 2

    def take(values, which):
        return lax.dynamic_slice_in_dim(values, which * rows, rows, 0)

    mine, by_tensor = take(own, me), take(own, 1 - me)
    by_y, corner = take(across, me), take(across, 1 - me).astype(bf16)
    low, high = swap(corner[:half], "tensor"), swap(corner[half:], "y")
    by_y = jnp.concatenate([by_y[:half] + low.astype(f32), by_y[half:]], axis=0)
    by_tensor = jnp.concatenate([by_tensor[:half], by_tensor[half:] + high.astype(f32)], axis=0)
    return (
        mine
        + swap(by_tensor.astype(bf16), "tensor").astype(f32)
        + swap(by_y.astype(bf16), "y").astype(f32)
    )


def rope_lanes(values, cosine, sine, first, direction):
    lanes = values.shape[1]
    turned = jnp.where(
        first, pltpu.roll(values, lanes - HALF, 1), pltpu.roll(values, HALF, 1)
    )
    return values * cosine + direction * (turned * sine)


def lane_ids(rows):
    return lax.broadcasted_iota(jnp.int32, (rows, LANES), 1)


def attention_forward_kernel(pre_ref, cos_ref, sin_ref, mixed_ref, rot_ref, lse_ref):
    seq_len = pre_ref.shape[0]
    lane = lane_ids(seq_len)
    first = (lane & (2 * HALF - 1)) < HALF
    low = lane < HEAD
    cosine, sine = cos_ref[...], sin_ref[...]
    query = rope_lanes(pre_ref[:, :LANES], cosine, sine, first, 1.0).astype(bf16)
    kv = pre_ref[:, LANES:]
    kv = jnp.where(low, rope_lanes(kv, cosine, sine, first, 1.0), kv)
    rot_ref[:, :LANES] = query
    rot_ref[:, LANES:] = kv.astype(bf16)
    keys, values_in = head_pairs(kv, low)
    block = min(BLOCK, seq_len)
    for start in range(0, seq_len, block):
        stop = start + block
        allowed = causal(block, stop, start)
        total = jnp.zeros((block, LANES), f32)
        lses = []
        for head in (0, 1):
            scores = (
                contract(query[start:stop], keys[head][:stop], 1, 1) * attn_scale
            )
            scores = jnp.where(allowed, scores, masked_score)
            top = jnp.max(scores, axis=1, keepdims=True)
            raised = jnp.exp(scores - top)
            summed = jnp.sum(raised, axis=1, keepdims=True)
            prob = (raised * (1.0 / summed)).astype(bf16)
            total = total + jnp.dot(prob, values_in[head][:stop], preferred_element_type=f32)
            lses.append(top + jnp.log(summed))
        mixed_ref[start:stop, :] = total.astype(bf16)
        lse_ref[start:stop, :] = jnp.where(lane_ids(block) < HEAD, lses[0], lses[1])


def head_pairs(kv, low):
    kv = kv.astype(f32)
    turned = pltpu.roll(kv, HEAD, 1)
    zero = jnp.zeros_like(kv)
    keys = [jnp.where(low, kv, zero).astype(bf16), jnp.where(low, zero, turned).astype(bf16)]
    values_in = [jnp.where(low, turned, zero).astype(bf16), jnp.where(low, zero, kv).astype(bf16)]
    return keys, values_in


def causal(rows, columns, start):
    return lax.broadcasted_iota(jnp.int32, (rows, columns), 1) <= start + lax.broadcasted_iota(
        jnp.int32, (rows, columns), 0
    )


def attention_backward_kernel(
    rot_ref, grad_ref, lse_ref, cos_ref, sin_ref, out_ref, key_acc, value_acc
):
    seq_len = rot_ref.shape[0]
    lane = lane_ids(seq_len)
    first = (lane & (2 * HALF - 1)) < HALF
    low = lane < HEAD
    cosine, sine = cos_ref[...], sin_ref[...]
    keys, values_in = head_pairs(rot_ref[:, LANES:], low)
    key_acc[...] = jnp.zeros_like(key_acc)
    value_acc[...] = jnp.zeros_like(value_acc)
    block = min(BLOCK, seq_len)
    for start in range(0, seq_len, block):
        stop = start + block
        allowed = causal(block, stop, start)
        query = rot_ref[start:stop, :LANES]
        grad = grad_ref[start:stop, :]
        query_grad = jnp.zeros((block, LANES), f32)
        for head in (0, 1):
            scores = contract(query, keys[head][:stop], 1, 1) * attn_scale
            log_total = lse_ref[start:stop, head * HEAD : head * HEAD + 1]
            prob = jnp.where(allowed, jnp.exp(jnp.where(allowed, scores - log_total, 0.0)), 0.0)
            prob_grad = contract(grad, values_in[head][:stop], 1, 1)
            row_dot = jnp.sum(prob * prob_grad, axis=1, keepdims=True)
            score_grad = (prob * (prob_grad - row_dot)).astype(bf16)
            query_grad = query_grad + jnp.dot(
                score_grad, keys[head][:stop], preferred_element_type=f32
            )
            key_acc[head, :stop, :] += contract(score_grad, query, 0, 0)
            value_acc[head, :stop, :] += contract(prob.astype(bf16), grad, 0, 0)
        lane_block = (lane_ids(block) & (2 * HALF - 1)) < HALF
        out_ref[start:stop, :LANES] = rope_lanes(
            query_grad * attn_scale, cosine[start:stop], sine[start:stop], lane_block, -1.0
        ).astype(bf16)
    key_grad = (key_acc[0] + pltpu.roll(key_acc[1], HEAD, 1)) * attn_scale
    key_grad = rope_lanes(jnp.where(low, key_grad, 0.0), cosine, sine, first, -1.0)
    value_grad = pltpu.roll(value_acc[0], HEAD, 1) + value_acc[1]
    out_ref[:, LANES:] = jnp.where(low, key_grad, value_grad).astype(bf16)


def by_head(width):
    return lambda seq_len: pl.BlockSpec((seq_len, width), lambda g: (0, g))


def attention_forward(pre, cosine, sine):
    seq_len, width = pre.shape
    groups = width // (2 * LANES)
    whole = pl.BlockSpec((seq_len, LANES), lambda g: (0, 0))
    wide, narrow = by_head(2 * LANES)(seq_len), by_head(LANES)(seq_len)
    return pl.pallas_call(
        attention_forward_kernel,
        grid=(groups,),
        in_specs=[wide, whole, whole],
        out_specs=[narrow, wide, narrow],
        out_shape=[
            jax.ShapeDtypeStruct((seq_len, width // 2), bf16),
            jax.ShapeDtypeStruct((seq_len, width), bf16),
            jax.ShapeDtypeStruct((seq_len, width // 2), f32),
        ],
        cost_estimate=pl.CostEstimate(
            flops=6 * groups * seq_len * seq_len * LANES,
            bytes_accessed=10 * seq_len * width,
            transcendentals=groups * seq_len * seq_len,
        ),
        name="attention_forward",
    )(pre, cosine, sine)


def attention_backward(rot, grad, lse, cosine, sine):
    seq_len, width = rot.shape
    groups = width // (2 * LANES)
    whole = pl.BlockSpec((seq_len, LANES), lambda g: (0, 0))
    wide, narrow = by_head(2 * LANES)(seq_len), by_head(LANES)(seq_len)
    return pl.pallas_call(
        attention_backward_kernel,
        grid=(groups,),
        in_specs=[wide, narrow, narrow, whole, whole],
        out_specs=wide,
        out_shape=jax.ShapeDtypeStruct((seq_len, width), bf16),
        scratch_shapes=[pltpu.VMEM((2, seq_len, LANES), f32)] * 2,
        cost_estimate=pl.CostEstimate(
            flops=16 * groups * seq_len * seq_len * LANES,
            bytes_accessed=10 * seq_len * width,
            transcendentals=groups * seq_len * seq_len,
        ),
        name="attention_backward",
    )(rot, grad, lse, cosine, sine)


def expert_kernel(carried, member_ref, tokens_ref, grad_ref, code_ref, gate_ref, weight_ref, *refs):
    if carried:
        moe_in, normed_in, *refs = refs
    moe_ref, normed_ref, pair_ref, part_ref, both, down, both_acc, down_acc = refs
    step = pl.program_id(0)
    shards_z, members, rows = weight_ref.shape[:3]
    hidden = down.shape[0]
    both_rows = both.shape[0] // (shards_z * members)
    down_rows = hidden // (shards_z * members)

    def places():
        for z in range(shards_z):
            for rel in range(members):
                at = z * members + (member_ref[0] ^ rel)
                yield (
                    z,
                    rel,
                    pl.ds(pl.multiple_of(at * both_rows, both_rows), both_rows),
                    pl.ds(pl.multiple_of(at * down_rows, down_rows), down_rows),
                )

    @pl.when(step == 0)
    def _():
        for z, rel, both_at, down_at in places():
            both[both_at, :] = weight_ref[z, rel, :both_rows, :]
            down[down_at, :] = weight_ref[z, rel, both_rows:, :]
        both_acc[...] = jnp.zeros_like(both_acc)
        down_acc[...] = jnp.zeros_like(down_acc)

    seq_len = tokens_ref.shape[1]
    slot = lax.broadcasted_iota(jnp.int32, (CAP, seq_len), 0)
    match = code_ref[0] == slot
    dispatch = jnp.where(match, 1.0, 0.0).astype(bf16)
    slot_gate = jnp.sum(jnp.where(match, gate_ref[0], 0.0), axis=1, keepdims=True)
    expert_in = jnp.dot(dispatch, tokens_ref[0], preferred_element_type=f32).astype(bf16)
    gate_pre = jnp.dot(expert_in, both[:, :hidden], preferred_element_type=f32)
    up_pre = jnp.dot(expert_in, both[:, hidden:], preferred_element_type=f32)
    sigmoid = 1.0 / (1.0 + jnp.exp(-gate_pre))
    silu = gate_pre * sigmoid
    hidden_act = (silu * up_pre).astype(bf16)
    expert_out = jnp.dot(hidden_act, down[...], preferred_element_type=f32)
    weighted = (slot_gate * expert_out).astype(bf16)
    moe = contract(dispatch, weighted, 0, 0)
    if carried:
        moe = moe + moe_in[0].astype(f32)
    moe_ref[0] = moe.astype(bf16)

    slot_grad = jnp.dot(dispatch, grad_ref[0], preferred_element_type=f32)
    raw_grad = contract(slot_grad.astype(bf16), down[...], 1, 1)
    slot_gate_grad = jnp.sum(hidden_act.astype(f32) * raw_grad, axis=1, keepdims=True)
    pair_ref[0] = jnp.sum(jnp.where(match, slot_gate_grad, 0.0), axis=0, keepdims=True)
    hidden_grad = slot_gate * raw_grad
    gate_grad = (
        hidden_grad * up_pre * sigmoid * (1.0 + gate_pre * (1.0 - sigmoid))
    ).astype(bf16)
    up_grad = (hidden_grad * silu).astype(bf16)
    down_acc[...] += contract(hidden_act, (slot_gate * slot_grad).astype(bf16), 0, 0)
    both_acc[:, :hidden] += contract(expert_in, gate_grad, 0, 0)
    both_acc[:, hidden:] += contract(expert_in, up_grad, 0, 0)
    in_grad = (
        contract(gate_grad, both[:, :hidden], 1, 1) + contract(up_grad, both[:, hidden:], 1, 1)
    ).astype(bf16)
    normed = contract(dispatch, in_grad, 0, 0)
    if carried:
        normed = normed + normed_in[0].astype(f32)
    normed_ref[0] = normed.astype(bf16)

    @pl.when(step == pl.num_programs(0) - 1)
    def _():
        for z, rel, both_at, down_at in places():
            part_ref[z, rel, :both_rows, :] = both_acc[both_at, :].astype(bf16)
            part_ref[z, rel, both_rows:, :] = down_acc[down_at, :].astype(bf16)


def run_expert(member, tokens, grads, code, gate, weight, carry):
    sequences, seq_len, width = tokens.shape
    shards_z, members, rows, both_width = weight.shape
    hidden = both_width // 2
    per_seq = pl.BlockSpec((1, seq_len, width), lambda s: (s, 0, 0))
    per_row = pl.BlockSpec((1, 1, seq_len), lambda s: (s, 0, 0))
    every = pl.BlockSpec(weight.shape, lambda s: (0, 0, 0, 0), pipeline_mode=pl.Buffered(1))
    part = pl.BlockSpec(weight.shape, lambda s: (0, 0, 0, 0))
    slots = sequences * CAP
    return pl.pallas_call(
        functools.partial(expert_kernel, bool(carry)),
        grid=(sequences,),
        in_specs=[
            pl.BlockSpec(memory_space=pltpu.SMEM),
            per_seq,
            per_seq,
            per_row,
            per_row,
            every,
        ]
        + [per_seq] * len(carry),
        out_specs=[per_seq, per_seq, per_row, part],
        out_shape=[
            jax.ShapeDtypeStruct(tokens.shape, bf16),
            jax.ShapeDtypeStruct(tokens.shape, bf16),
            jax.ShapeDtypeStruct((sequences, 1, seq_len), f32),
            jax.ShapeDtypeStruct(weight.shape, bf16),
        ],
        scratch_shapes=[
            pltpu.VMEM((width, both_width), bf16),
            pltpu.VMEM((hidden, width), bf16),
            pltpu.VMEM((width, both_width), f32),
            pltpu.VMEM((hidden, width), f32),
        ],
        compiler_params=pltpu.CompilerParams(vmem_limit_bytes=66_000_000),
        cost_estimate=pl.CostEstimate(
            flops=2 * slots * width * (4 * seq_len + 9 * hidden),
            bytes_accessed=12 * sequences * seq_len * width + 4 * weight.size,
            transcendentals=slots * hidden,
        ),
        name="expert",
    )(member, tokens, grads, code, gate, weight, *carry)


def shards(
    sizes,
    block_input,
    positions,
    expert_ids,
    attn_gain,
    query_weight,
    kv_weight,
    out_weight,
    ffn_gain,
    router_weight,
    gate_weight,
    up_weight,
    down_weight,
    out_grad,
):
    tensor_size, z_size = sizes["tensor"], sizes["z"]
    seq_len = positions.shape[0]
    width = block_input.shape[1]
    shard_rows, groups = kv_weight.shape[:2]
    q_width = query_weight.shape[1]
    wide = 2 * q_width
    expert_count = router_weight.shape[1]
    experts_local = gate_weight.shape[0]
    owned = experts_local // 4
    hidden = gate_weight.shape[2]
    my_y, my_core = lax.axis_index("y"), lax.axis_index("core")
    my_tensor = lax.axis_index("tensor")
    y_first, core_first, tensor_first = my_y == 0, my_core == 0, my_tensor == 0

    def at(values, index):
        return lax.dynamic_index_in_dim(values, index, 0, keepdims=False)

    packed = jnp.concatenate(
        [
            jnp.concatenate([query_weight.reshape(shard_rows, groups, -1), kv_weight], axis=2)
            .reshape(shard_rows, wide),
            out_weight.T,
        ],
        axis=1,
    )
    by_z = lax.all_gather(packed, "z", axis=0, tiled=False)

    experts = jnp.concatenate(
        [jnp.concatenate([gate_weight, up_weight], axis=2), down_weight], axis=1
    )
    rows, both_width = experts.shape[1:]
    grouped = experts.reshape(2, 2, owned, rows, both_width)
    own_y, from_y = at(grouped, my_y), swap(at(grouped, 1 - my_y), "y")
    pieces = [
        at(own_y, my_core),
        swap(at(own_y, 1 - my_core), "core"),
        at(from_y, my_core),
        swap(at(from_y, 1 - my_core), "core"),
    ]
    weights = [
        lax.all_gather(jnp.stack([piece[e] for piece in pieces]), "z", axis=0, tiled=False)
        for e in range(owned)
    ]

    def stacked(mine, theirs, is_first):
        return jnp.stack([jnp.where(is_first, mine, theirs), jnp.where(is_first, theirs, mine)], 1)

    by_y = stacked(by_z, swap(by_z, "y"), y_first)
    other = swap(by_y, "core")
    packed_full = jnp.stack(
        [jnp.where(core_first, by_y, other), jnp.where(core_first, other, by_y)], 2
    ).reshape(width, -1)
    qkv_full, out_full = packed_full[:, :wide], packed_full[:, wide:]

    ids_t = expert_ids.T
    hits = jnp.zeros((expert_count, seq_len), jnp.bool_)
    for k in range(ids_t.shape[0]):
        hits = hits | (ids_t[k][None, :] == jnp.arange(expert_count)[:, None])
    token_ids = jnp.arange(seq_len)
    earlier = (token_ids[:, None] < token_ids[None, :]).astype(bf16)
    rank = jnp.dot(hits.astype(bf16), earlier, preferred_element_type=f32)
    code = jnp.where(hits, jnp.where(rank < CAP, rank, -1.0), -2.0)
    code_y = swap(code, "y")
    codes = jnp.stack([code, code_y, swap(code, "core"), swap(code_y, "core")])

    half_dim = HEAD // 2
    frequency = rope_base ** (-(jnp.arange(half_dim, dtype=f32) * 2.0 / HEAD))
    angles = positions.astype(f32)[:, None] * frequency[None, :]
    cosine = jnp.tile(jnp.cos(angles), (1, 4))
    sine = jnp.tile(jnp.concatenate([-jnp.sin(angles), jnp.sin(angles)], axis=1), (1, 2))

    input_rows = block_input.astype(f32)
    attn_normed = (input_rows * row_scale(input_rows) * attn_gain).astype(bf16)
    attn_tokens = gather_rows(attn_normed, tensor_size)
    grad_rows = out_grad.astype(f32)
    moe_rows = (residual_scale * grad_rows).astype(bf16)
    qkv_full, moe_rows, codes = lax.optimization_barrier((qkv_full, moe_rows, codes))
    moe_grad = gather_group(moe_rows, tensor_size)
    qkv_pre = jnp.dot(attn_tokens, qkv_full, preferred_element_type=f32)
    attn_mixed, qkv_rot, log_totals = attention_forward(qkv_pre, cosine, sine)
    attn_mixed, moe_grad = lax.optimization_barrier((attn_mixed, moe_grad))
    attn_out = scatter_rows(contract(attn_mixed, out_full, 1, 1), tensor_size)
    hidden_state = input_rows + residual_scale * attn_out
    ffn_normed = (hidden_state * row_scale(hidden_state) * ffn_gain).astype(bf16)

    tokens = gather_group(ffn_normed, tensor_size)
    logits = ein("dx,std->sxt", router_weight, tokens)
    chosen = codes > -1.5
    top_logit = jnp.max(jnp.where(chosen, logits, -jnp.inf), axis=1, keepdims=True)
    raised = jnp.where(chosen, jnp.exp(jnp.where(chosen, logits - top_logit, 0.0)), 0.0)
    gates = raised / jnp.sum(raised, axis=1, keepdims=True)
    member = my_y * 2 + my_core
    expert_first = my_tensor * experts_local + member * owned
    code_own = lax.dynamic_slice_in_dim(codes, expert_first, owned, 1).astype(jnp.int32)
    gate_own = lax.dynamic_slice_in_dim(gates, expert_first, owned, 1)

    carry, pairs, parts = (), [], []
    for e in range(owned):
        *carry, pair, part = run_expert(
            member.reshape(1).astype(jnp.int32),
            tokens,
            moe_grad,
            code_own[:, e : e + 1],
            gate_own[:, e : e + 1],
            weights[e],
            carry,
        )
        pairs.append(pair)
        parts.append(lax.psum_scatter(part, "z", scatter_dimension=0, tiled=False))
    moe_parts, normed_parts = carry

    pair_grad = jnp.concatenate(pairs, axis=1)
    pair_core = stacked(pair_grad[:2], swap(pair_grad[2:], "core"), core_first)
    pair_y = in_order(pair_core[0], swap(pair_core[1], "y"), y_first)
    pair_y = pair_y.reshape(experts_local, seq_len)
    if tensor_size == 2:
        local = seq_len // 2
        give = lax.dynamic_slice_in_dim(pair_y, (1 - my_tensor) * local, local, 1)
        keep = lax.dynamic_slice_in_dim(pair_y, my_tensor * local, local, 1)
        pair_all = in_order(keep, swap(give, "tensor"), tensor_first)
    else:
        local = seq_len // tensor_size
        pair_all = lax.all_gather(pair_y, "tensor", axis=0, tiled=True)
        pair_all = lax.dynamic_slice_in_dim(pair_all, my_tensor * local, local, 1)
    gates_local = lax.dynamic_slice_in_dim(gates[0], my_tensor * local, local, 1)
    gate_dot = jnp.sum(gates_local * pair_all, axis=0, keepdims=True)
    logit_low = (gates_local * (pair_all - gate_dot)).astype(bf16)

    normed_local = scatter_group(normed_parts, tensor_size)
    normed_local, moe_parts = lax.optimization_barrier((normed_local, moe_parts))
    normed_local = normed_local + contract(logit_low, router_weight, 0, 1)
    router_part = jnp.dot(logit_low, ffn_normed, preferred_element_type=f32)
    state_grad, ffn_gain_part = norm_backward(normed_local, hidden_state, ffn_gain)
    state_grad = state_grad + grad_rows
    steps = (("core", 2), ("y", 2), ("tensor", tensor_size), ("z", z_size))
    attn_grad_all = gather_rows((residual_scale * state_grad).astype(bf16), tensor_size)
    moe_out = scatter_group(moe_parts, tensor_size)
    block_output = (hidden_state + residual_scale * moe_out).astype(bf16)

    def scatter_dp(part):
        part = part.reshape(z_size, 2, 2, shard_rows, part.shape[1])
        part = jnp.take(part, my_core, axis=2), jnp.take(part, 1 - my_core, axis=2)
        part = part[0].astype(f32) + swap(part[1].astype(bf16), "core").astype(f32)
        part = jnp.take(part, my_y, axis=1), jnp.take(part, 1 - my_y, axis=1)
        part = part[0] + swap(part[1].astype(bf16), "y").astype(f32)
        return lax.psum_scatter(part.astype(bf16), "z", scatter_dimension=0, tiled=False)

    out_sum = scatter_dp(contract(attn_grad_all, attn_mixed, 0, 0))
    mixed_grad = jnp.dot(attn_grad_all, out_full, preferred_element_type=f32).astype(bf16)
    qkv_pre_grad = attention_backward(qkv_rot, mixed_grad, log_totals, cosine, sine)
    qkv_pre_grad, block_output = lax.optimization_barrier((qkv_pre_grad, block_output))
    attn_normed_grad = scatter_rows(contract(qkv_pre_grad, qkv_full, 1, 1), tensor_size)
    qkv_sum = scatter_dp(contract(attn_tokens, qkv_pre_grad, 0, 0))
    input_part, attn_gain_part = norm_backward(attn_normed_grad, input_rows, attn_gain)
    input_grad = (state_grad + input_part).astype(bf16)
    small = jnp.concatenate(
        [router_part, ffn_gain_part[None, :], attn_gain_part[None, :]], axis=0
    )
    small = butterfly_sum(small, steps)

    owners = []
    for part in parts:
        near = stacked(part[0::2], swap(part[1::2], "core"), core_first)
        owners.append(in_order(near[0], swap(near[1], "y"), y_first))
    summed = jnp.stack(owners, axis=1).reshape(experts_local, rows, both_width)
    both_rows = gate_weight.shape[1]
    qkv_sum = qkv_sum.reshape(shard_rows, groups, -1)
    return (
        block_output,
        input_grad,
        small[expert_count + 1],
        qkv_sum[:, :, : 2 * HEAD].reshape(query_weight.shape).astype(f32),
        qkv_sum[:, :, 2 * HEAD :].astype(f32),
        out_sum.T.astype(f32),
        small[expert_count],
        small[:expert_count].T,
        summed[:, :both_rows, :hidden].astype(f32),
        summed[:, :both_rows, hidden:].astype(f32),
        summed[:, both_rows:].astype(f32),
    )


def solution(mesh):
    dp, tensor = mesh.shape["dp"], mesh.shape["tensor"]
    fine = Mesh(mesh.devices.reshape(dp // 4, 2, 2, tensor), ("z", "y", "core", "tensor"))
    rows = ("z", "y", "core")
    every = rows + ("tensor",)
    experts = P("tensor", rows, None)
    return jax.shard_map(
        functools.partial(shards, dict(fine.shape)),
        mesh=fine,
        in_specs=(
            P(every, None),
            P(rows),
            P(rows, None),
            P(),
            P(rows, "tensor"),
            P(rows, "tensor", None),
            P("tensor", rows),
            P(),
            P(),
            experts,
            experts,
            experts,
            P(every, None),
        ),
        out_specs=(
            P(every, None),
            P(every, None),
            P(),
            P(rows, "tensor"),
            P(rows, "tensor", None),
            P("tensor", rows),
            P(),
            P(),
            experts,
            experts,
            experts,
        ),
        check_vma=False,
    )
```

```python
import functools

import jax
import jax.numpy as jnp
from jax import lax
from jax.experimental import pallas as pl
from jax.experimental.pallas import tpu as pltpu
from jax.sharding import Mesh, PartitionSpec as P

CAP = 320
HEAD = 64
HALF = HEAD // 2
LANES = 2 * HEAD
BLOCK = 256
norm_eps = 1e-06
attn_scale = 0.015625
residual_scale = 0.22
rope_base = 10000.0
masked_score = -1e30
f32 = jnp.float32
bf16 = jnp.bfloat16


def row_scale(values):
    return lax.rsqrt(jnp.mean(values * values, axis=-1, keepdims=True) + norm_eps)


def contract(left, right, left_dim, right_dim):
    return lax.dot_general(
        left, right, (((left_dim,), (right_dim,)), ((), ())), preferred_element_type=f32
    )


def ein(spec, *operands):
    return jnp.einsum(spec, *operands, preferred_element_type=f32)


def norm_backward(normed_grad, source, gain):
    scale_rows = row_scale(source)
    unit_rows = source * scale_rows
    scaled_grad = normed_grad * gain
    gain_grad = jnp.sum(normed_grad * unit_rows, axis=0)
    source_grad = scale_rows * (
        scaled_grad - unit_rows * jnp.mean(scaled_grad * unit_rows, axis=-1, keepdims=True)
    )
    return (source_grad, gain_grad)


def together(*values):
    return lax.optimization_barrier(values)


def after(values, *earlier):
    return lax.optimization_barrier((values,) + earlier)[0]


def swap(values, axis):
    return lax.ppermute(values, axis, [(0, 1), (1, 0)])


def butterfly_sum(values, sizes):
    for axis, size in sizes:
        step = 1
        while step < size:
            values = values + lax.ppermute(values, axis, [(i, i ^ step) for i in range(size)])
            step *= 2
    return values


def in_order(mine, theirs, first):
    return jnp.concatenate(
        [jnp.where(first, mine, theirs), jnp.where(first, theirs, mine)], axis=0
    )


def gather_rows(rows, tensor_size):
    if tensor_size != 2:
        return lax.all_gather(rows, "tensor", axis=0, tiled=True)
    return in_order(rows, swap(rows, "tensor"), lax.axis_index("tensor") == 0)


def scatter_rows(values, tensor_size):
    if tensor_size != 2:
        return lax.psum_scatter(
            values.astype(bf16), "tensor", scatter_dimension=0, tiled=True
        ).astype(f32)
    half = values.shape[0] // 2
    me = lax.axis_index("tensor")
    give = lax.dynamic_slice_in_dim(values, (1 - me) * half, half, 0).astype(bf16)
    keep = lax.dynamic_slice_in_dim(values, me * half, half, 0)
    return keep.astype(f32) + swap(give, "tensor").astype(f32)


def gather_group(rows, tensor_size, earlier):
    if tensor_size != 2:
        own = gather_rows(rows, tensor_size)
        across = swap(own, "y")
    else:
        first = lax.axis_index("tensor") == 0
        half = rows.shape[0] // 2
        by_tensor, by_y, _ = together(swap(rows, "tensor"), swap(rows, "y"), earlier)
        own = in_order(rows, by_tensor, first)
        low, high, own_core = together(
            swap(by_y[:half], "tensor"), swap(by_tensor[half:], "y"), swap(own, "core")
        )
        corner = jnp.concatenate([low, high], axis=0)
        across = in_order(by_y, corner, first)
        return jnp.stack([own, across, own_core, swap(across, "core")])
    return jnp.stack([own, across, swap(own, "core"), swap(across, "core")])


def add_core(parts):
    given = swap(parts[2:], "core")
    return (parts[:2].astype(f32) + given.astype(f32)).astype(bf16)


def scatter_group(pair, tensor_size):
    own, across = pair[0].astype(f32), pair[1].astype(f32)
    if tensor_size != 2:
        own = own + swap(across.astype(bf16), "y").astype(f32)
        return scatter_rows(own, tensor_size)
    me = lax.axis_index("tensor")
    rows = own.shape[0] // 2
    half = rows // 2

    def take(values, which):
        return lax.dynamic_slice_in_dim(values, which * rows, rows, 0)

    mine, by_tensor = take(own, me), take(own, 1 - me)
    by_y, corner = take(across, me), take(across, 1 - me).astype(bf16)
    low, high = together(swap(corner[:half], "tensor"), swap(corner[half:], "y"))
    by_y = jnp.concatenate([by_y[:half] + low.astype(f32), by_y[half:]], axis=0)
    by_tensor = jnp.concatenate([by_tensor[:half], by_tensor[half:] + high.astype(f32)], axis=0)
    from_tensor, from_y = together(
        swap(by_tensor.astype(bf16), "tensor"), swap(by_y.astype(bf16), "y")
    )
    return mine + from_tensor.astype(f32) + from_y.astype(f32)


def rope_lanes(values, cosine, sine, first, direction):
    lanes = values.shape[1]
    turned = jnp.where(
        first, pltpu.roll(values, lanes - HALF, 1), pltpu.roll(values, HALF, 1)
    )
    return values * cosine + direction * (turned * sine)


def lane_ids(rows):
    return lax.broadcasted_iota(jnp.int32, (rows, LANES), 1)


def attention_forward_kernel(pre_ref, cos_ref, sin_ref, mixed_ref, rot_ref, lse_ref):
    seq_len = pre_ref.shape[0]
    lane = lane_ids(seq_len)
    first = (lane & (2 * HALF - 1)) < HALF
    low = lane < HEAD
    cosine, sine = cos_ref[...], sin_ref[...]
    query = rope_lanes(pre_ref[:, :LANES], cosine, sine, first, 1.0).astype(bf16)
    kv = pre_ref[:, LANES:]
    kv = jnp.where(low, rope_lanes(kv, cosine, sine, first, 1.0), kv)
    rot_ref[:, :LANES] = query
    rot_ref[:, LANES:] = kv.astype(bf16)
    keys, values_in = head_pairs(kv, low)
    block = min(BLOCK, seq_len)
    for start in range(0, seq_len, block):
        stop = start + block
        allowed = causal(block, stop, start)
        total = jnp.zeros((block, LANES), f32)
        lses = []
        for head in (0, 1):
            scores = (
                contract(query[start:stop], keys[head][:stop], 1, 1) * attn_scale
            )
            scores = jnp.where(allowed, scores, masked_score)
            top = jnp.max(scores, axis=1, keepdims=True)
            raised = jnp.exp(scores - top)
            summed = jnp.sum(raised, axis=1, keepdims=True)
            prob = (raised * (1.0 / summed)).astype(bf16)
            total = total + jnp.dot(prob, values_in[head][:stop], preferred_element_type=f32)
            lses.append(top + jnp.log(summed))
        mixed_ref[start:stop, :] = total.astype(bf16)
        lse_ref[start:stop, :] = jnp.where(lane_ids(block) < HEAD, lses[0], lses[1])


def head_pairs(kv, low):
    kv = kv.astype(f32)
    turned = pltpu.roll(kv, HEAD, 1)
    zero = jnp.zeros_like(kv)
    keys = [jnp.where(low, kv, zero).astype(bf16), jnp.where(low, zero, turned).astype(bf16)]
    values_in = [jnp.where(low, turned, zero).astype(bf16), jnp.where(low, zero, kv).astype(bf16)]
    return keys, values_in


def causal(rows, columns, start):
    return lax.broadcasted_iota(jnp.int32, (rows, columns), 1) <= start + lax.broadcasted_iota(
        jnp.int32, (rows, columns), 0
    )


def attention_backward_kernel(
    rot_ref, grad_ref, lse_ref, cos_ref, sin_ref, out_ref, key_acc, value_acc
):
    seq_len = rot_ref.shape[0]
    lane = lane_ids(seq_len)
    first = (lane & (2 * HALF - 1)) < HALF
    low = lane < HEAD
    cosine, sine = cos_ref[...], sin_ref[...]
    keys, values_in = head_pairs(rot_ref[:, LANES:], low)
    key_acc[...] = jnp.zeros_like(key_acc)
    value_acc[...] = jnp.zeros_like(value_acc)
    block = min(BLOCK, seq_len)
    for start in range(0, seq_len, block):
        stop = start + block
        allowed = causal(block, stop, start)
        query = rot_ref[start:stop, :LANES]
        grad = grad_ref[start:stop, :]
        query_grad = jnp.zeros((block, LANES), f32)
        for head in (0, 1):
            scores = contract(query, keys[head][:stop], 1, 1) * attn_scale
            log_total = lse_ref[start:stop, head * HEAD : head * HEAD + 1]
            prob = jnp.where(allowed, jnp.exp(jnp.where(allowed, scores - log_total, 0.0)), 0.0)
            prob_grad = contract(grad, values_in[head][:stop], 1, 1)
            row_dot = jnp.sum(prob * prob_grad, axis=1, keepdims=True)
            score_grad = (prob * (prob_grad - row_dot)).astype(bf16)
            query_grad = query_grad + jnp.dot(
                score_grad, keys[head][:stop], preferred_element_type=f32
            )
            key_acc[head, :stop, :] += contract(score_grad, query, 0, 0)
            value_acc[head, :stop, :] += contract(prob.astype(bf16), grad, 0, 0)
        lane_block = (lane_ids(block) & (2 * HALF - 1)) < HALF
        out_ref[start:stop, :LANES] = rope_lanes(
            query_grad * attn_scale, cosine[start:stop], sine[start:stop], lane_block, -1.0
        ).astype(bf16)
    key_grad = (key_acc[0] + pltpu.roll(key_acc[1], HEAD, 1)) * attn_scale
    key_grad = rope_lanes(jnp.where(low, key_grad, 0.0), cosine, sine, first, -1.0)
    value_grad = pltpu.roll(value_acc[0], HEAD, 1) + value_acc[1]
    out_ref[:, LANES:] = jnp.where(low, key_grad, value_grad).astype(bf16)


def by_head(width):
    return lambda seq_len: pl.BlockSpec((seq_len, width), lambda g: (0, g))


def attention_forward(pre, cosine, sine):
    seq_len, width = pre.shape
    groups = width // (2 * LANES)
    whole = pl.BlockSpec((seq_len, LANES), lambda g: (0, 0))
    wide, narrow = by_head(2 * LANES)(seq_len), by_head(LANES)(seq_len)
    return pl.pallas_call(
        attention_forward_kernel,
        grid=(groups,),
        in_specs=[wide, whole, whole],
        out_specs=[narrow, wide, narrow],
        out_shape=[
            jax.ShapeDtypeStruct((seq_len, width // 2), bf16),
            jax.ShapeDtypeStruct((seq_len, width), bf16),
            jax.ShapeDtypeStruct((seq_len, width // 2), f32),
        ],
        cost_estimate=pl.CostEstimate(
            flops=6 * groups * seq_len * seq_len * LANES,
            bytes_accessed=10 * seq_len * width,
            transcendentals=groups * seq_len * seq_len,
        ),
        name="attention_forward",
    )(pre, cosine, sine)


def attention_backward(rot, grad, lse, cosine, sine):
    seq_len, width = rot.shape
    groups = width // (2 * LANES)
    whole = pl.BlockSpec((seq_len, LANES), lambda g: (0, 0))
    wide, narrow = by_head(2 * LANES)(seq_len), by_head(LANES)(seq_len)
    return pl.pallas_call(
        attention_backward_kernel,
        grid=(groups,),
        in_specs=[wide, narrow, narrow, whole, whole],
        out_specs=wide,
        out_shape=jax.ShapeDtypeStruct((seq_len, width), bf16),
        scratch_shapes=[pltpu.VMEM((2, seq_len, LANES), f32)] * 2,
        cost_estimate=pl.CostEstimate(
            flops=16 * groups * seq_len * seq_len * LANES,
            bytes_accessed=10 * seq_len * width,
            transcendentals=groups * seq_len * seq_len,
        ),
        name="attention_backward",
    )(rot, grad, lse, cosine, sine)


def expert_kernel(
    carried, shared, member_ref, tokens_ref, grad_ref, code_ref, gate_ref, weight_ref, *refs
):
    if carried:
        moe_in, normed_in, *refs = refs
    if shared:
        refs = refs[1:]
    moe_ref, normed_ref, pair_ref, part_ref, both, down, both_acc, down_acc = refs
    step = pl.program_id(0)
    shards_z, members, rows = weight_ref.shape[0], weight_ref.shape[2], weight_ref.shape[3]
    hidden = down.shape[0]
    both_rows = both.shape[0] // (shards_z * members)
    down_rows = hidden // (shards_z * members)

    def places():
        for z in range(shards_z):
            for rel in range(members):
                at = z * members + (member_ref[0] ^ rel)
                yield (
                    z,
                    rel,
                    pl.ds(pl.multiple_of(at * both_rows, both_rows), both_rows),
                    pl.ds(pl.multiple_of(at * down_rows, down_rows), down_rows),
                )

    @pl.when(step == 0)
    def _():
        for z, rel, both_at, down_at in places():
            both[both_at, :] = weight_ref[z, 0, rel, :both_rows, :]
            down[down_at, :] = weight_ref[z, 0, rel, both_rows:, :]
        both_acc[...] = jnp.zeros_like(both_acc)
        down_acc[...] = jnp.zeros_like(down_acc)

    seq_len = tokens_ref.shape[1]
    slot = lax.broadcasted_iota(jnp.int32, (CAP, seq_len), 0)
    match = code_ref[0] == slot
    dispatch = jnp.where(match, 1.0, 0.0).astype(bf16)
    slot_gate = jnp.sum(jnp.where(match, gate_ref[0], 0.0), axis=1, keepdims=True)
    expert_in = jnp.dot(dispatch, tokens_ref[0], preferred_element_type=f32).astype(bf16)
    gate_pre = jnp.dot(expert_in, both[:, :hidden], preferred_element_type=f32)
    up_pre = jnp.dot(expert_in, both[:, hidden:], preferred_element_type=f32)
    sigmoid = 1.0 / (1.0 + jnp.exp(-gate_pre))
    silu = gate_pre * sigmoid
    hidden_act = (silu * up_pre).astype(bf16)
    expert_out = jnp.dot(hidden_act, down[...], preferred_element_type=f32)
    weighted = (slot_gate * expert_out).astype(bf16)
    moe = contract(dispatch, weighted, 0, 0)
    if carried:
        moe = moe + moe_in[0].astype(f32)
    moe_ref[0] = moe.astype(bf16)

    slot_grad = jnp.dot(dispatch, grad_ref[0], preferred_element_type=f32)
    raw_grad = contract(slot_grad.astype(bf16), down[...], 1, 1)
    slot_gate_grad = jnp.sum(hidden_act.astype(f32) * raw_grad, axis=1, keepdims=True)
    pair_ref[0] = jnp.sum(jnp.where(match, slot_gate_grad, 0.0), axis=0, keepdims=True)
    hidden_grad = slot_gate * raw_grad
    gate_grad = (
        hidden_grad * up_pre * sigmoid * (1.0 + gate_pre * (1.0 - sigmoid))
    ).astype(bf16)
    up_grad = (hidden_grad * silu).astype(bf16)
    down_acc[...] += contract(hidden_act, (slot_gate * slot_grad).astype(bf16), 0, 0)
    both_acc[:, :hidden] += contract(expert_in, gate_grad, 0, 0)
    both_acc[:, hidden:] += contract(expert_in, up_grad, 0, 0)
    in_grad = (
        contract(gate_grad, both[:, :hidden], 1, 1) + contract(up_grad, both[:, hidden:], 1, 1)
    ).astype(bf16)
    normed = contract(dispatch, in_grad, 0, 0)
    if carried:
        normed = normed + normed_in[0].astype(f32)
    normed_ref[0] = normed.astype(bf16)

    @pl.when(step == pl.num_programs(0) - 1)
    def _():
        for z, rel, both_at, down_at in places():
            part_ref[z, 0, rel, :both_rows, :] = both_acc[both_at, :].astype(bf16)
            part_ref[z, 0, rel, both_rows:, :] = down_acc[down_at, :].astype(bf16)


def run_expert(member, tokens, grads, code, gate, weight, place, carry, shared):
    sequences, seq_len, width = tokens.shape
    shards_z, bunch, members, rows, both_width = weight.shape
    hidden = both_width // 2
    per_seq = pl.BlockSpec((1, seq_len, width), lambda s: (s, 0, 0))
    per_row = pl.BlockSpec((1, 1, seq_len), lambda s: (s, 0, 0))
    one = (shards_z, 1, members, rows, both_width)
    every = pl.BlockSpec(one, lambda s: (0, place, 0, 0, 0), pipeline_mode=pl.Buffered(1))
    part = pl.BlockSpec(one, lambda s: (0, place, 0, 0, 0))
    slots = sequences * CAP
    return pl.pallas_call(
        functools.partial(expert_kernel, bool(carry), bool(shared)),
        grid=(sequences,),
        in_specs=[
            pl.BlockSpec(memory_space=pltpu.SMEM),
            per_seq,
            per_seq,
            per_row,
            per_row,
            every,
        ]
        + [per_seq] * len(carry)
        + [pl.BlockSpec(memory_space=pl.ANY)] * len(shared),
        out_specs=[per_seq, per_seq, per_row, part],
        out_shape=[
            jax.ShapeDtypeStruct(tokens.shape, bf16),
            jax.ShapeDtypeStruct(tokens.shape, bf16),
            jax.ShapeDtypeStruct((sequences, 1, seq_len), f32),
            jax.ShapeDtypeStruct(weight.shape, bf16),
        ],
        scratch_shapes=[
            pltpu.VMEM((width, both_width), bf16),
            pltpu.VMEM((hidden, width), bf16),
            pltpu.VMEM((width, both_width), f32),
            pltpu.VMEM((hidden, width), f32),
        ],
        compiler_params=pltpu.CompilerParams(vmem_limit_bytes=66_000_000),
        cost_estimate=pl.CostEstimate(
            flops=2 * slots * width * (4 * seq_len + 9 * hidden),
            bytes_accessed=12 * sequences * seq_len * width + 4 * (weight.size // bunch),
            transcendentals=slots * hidden,
        ),
        name="expert",
        input_output_aliases={6 + len(carry): 3} if shared else {},
    )(member, tokens, grads, code, gate, weight, *carry, *shared)


def shards(
    sizes,
    block_input,
    positions,
    expert_ids,
    attn_gain,
    query_weight,
    kv_weight,
    out_weight,
    ffn_gain,
    router_weight,
    gate_weight,
    up_weight,
    down_weight,
    out_grad,
):
    tensor_size, z_size = sizes["tensor"], sizes["z"]
    seq_len = positions.shape[0]
    width = block_input.shape[1]
    shard_rows, groups = kv_weight.shape[:2]
    q_width = query_weight.shape[1]
    wide = 2 * q_width
    expert_count = router_weight.shape[1]
    experts_local = gate_weight.shape[0]
    owned = experts_local // 4
    hidden = gate_weight.shape[2]
    my_z, my_y, my_core = lax.axis_index("z"), lax.axis_index("y"), lax.axis_index("core")
    my_tensor = lax.axis_index("tensor")
    y_first, core_first, tensor_first = my_y == 0, my_core == 0, my_tensor == 0

    def at(values, index):
        return lax.dynamic_index_in_dim(values, index, 0, keepdims=False)

    def stacked(mine, theirs, is_first, axis=1):
        ordered = [jnp.where(is_first, mine, theirs), jnp.where(is_first, theirs, mine)]
        return jnp.stack(ordered, axis)

    packed = jnp.concatenate(
        [
            jnp.concatenate([query_weight.reshape(shard_rows, groups, -1), kv_weight], axis=2)
            .reshape(shard_rows, wide),
            out_weight.T,
        ],
        axis=1,
    )
    packed_full = lax.all_gather(packed, ("z", "y", "core"), axis=0, tiled=True)

    input_rows = block_input.astype(f32)
    attn_normed = (input_rows * row_scale(input_rows) * attn_gain).astype(bf16)
    attn_tokens = gather_rows(attn_normed, tensor_size)
    grad_rows = out_grad.astype(f32)
    moe_rows = after((residual_scale * grad_rows).astype(bf16), attn_tokens)

    experts = jnp.concatenate(
        [jnp.concatenate([gate_weight, up_weight], axis=2), down_weight], axis=1
    )
    rows, both_width = experts.shape[1:]
    grouped = experts.reshape(2, 2, owned, rows, both_width)
    own_y, give_y = at(grouped, my_y), at(grouped, 1 - my_y)
    from_y = swap(give_y, "y")
    members = jnp.stack(
        [
            at(own_y, my_core),
            swap(at(own_y, 1 - my_core), "core"),
            at(from_y, my_core),
            swap(at(from_y, 1 - my_core), "core"),
        ],
        axis=1,
    )
    moe_own = gather_rows(moe_rows, tensor_size)
    packed_full, attn_tokens, moe_own, members = together(
        packed_full, attn_tokens, moe_own, members
    )
    qkv_full, out_full = packed_full[:, :wide], packed_full[:, wide:]
    bunch = min(2, owned)
    weights = []
    for e in range(0, owned, bunch):
        item = members[e : e + bunch]
        if weights:
            item = after(item, launched)
        launched = item
        weights.append(lax.all_gather(item, "z", axis=0, tiled=False))

    ids_t = expert_ids.T
    hits = jnp.zeros((expert_count, seq_len), jnp.bool_)
    for k in range(ids_t.shape[0]):
        hits = hits | (ids_t[k][None, :] == jnp.arange(expert_count)[:, None])
    token_ids = jnp.arange(seq_len)
    earlier = (token_ids[:, None] < token_ids[None, :]).astype(bf16)
    rank = jnp.dot(hits.astype(bf16), earlier, preferred_element_type=f32)
    code = jnp.where(hits, jnp.where(rank < CAP, rank, -1.0), -2.0)
    code_y = swap(code, "y")
    codes = jnp.stack([code, code_y, swap(code, "core"), swap(code_y, "core")])

    half_dim = HEAD // 2
    frequency = rope_base ** (-(jnp.arange(half_dim, dtype=f32) * 2.0 / HEAD))
    angles = positions.astype(f32)[:, None] * frequency[None, :]
    cosine = jnp.tile(jnp.cos(angles), (1, 4))
    sine = jnp.tile(jnp.concatenate([-jnp.sin(angles), jnp.sin(angles)], axis=1), (1, 2))

    qkv_pre = jnp.dot(attn_tokens, qkv_full, preferred_element_type=f32)
    qkv_pre, moe_own, codes = together(qkv_pre, moe_own, codes)
    moe_across = swap(moe_own, "y")
    attn_mixed, qkv_rot, log_totals = attention_forward(qkv_pre, cosine, sine)
    attn_out = scatter_rows(contract(attn_mixed, out_full, 1, 1), tensor_size)
    attn_out, moe_across = lax.optimization_barrier((attn_out, moe_across))
    moe_grad = jnp.stack([moe_own, moe_across, swap(moe_own, "core"), swap(moe_across, "core")])
    hidden_state = input_rows + residual_scale * attn_out
    ffn_normed = (hidden_state * row_scale(hidden_state) * ffn_gain).astype(bf16)

    tokens = gather_group(ffn_normed, tensor_size, moe_grad)
    logits = ein("dx,std->sxt", router_weight, tokens)
    chosen = codes > -1.5
    top_logit = jnp.max(jnp.where(chosen, logits, -jnp.inf), axis=1, keepdims=True)
    raised = jnp.where(chosen, jnp.exp(jnp.where(chosen, logits - top_logit, 0.0)), 0.0)
    gates = raised / jnp.sum(raised, axis=1, keepdims=True)
    member = my_y * 2 + my_core
    expert_first = my_tensor * experts_local + member * owned
    code_own = lax.dynamic_slice_in_dim(codes, expert_first, owned, 1).astype(jnp.int32)
    gate_own = lax.dynamic_slice_in_dim(gates, expert_first, owned, 1)

    carry, pairs, parts, shared = (), [], [], ()
    for e in range(owned):
        *carry, pair, part = run_expert(
            member.reshape(1).astype(jnp.int32),
            tokens,
            moe_grad,
            code_own[:, e : e + 1],
            gate_own[:, e : e + 1],
            weights[e // bunch],
            e % bunch,
            carry,
            shared,
        )
        pairs.append(pair)
        shared = (part,)
        if (e + 1) % bunch == 0:
            parts.append(lax.psum_scatter(part, "z", scatter_dimension=0, tiled=False))
            shared = ()
    moe_parts, normed_parts = carry

    pair_grad = jnp.concatenate(pairs, axis=1)
    pair_core = stacked(pair_grad[:2], swap(pair_grad[2:], "core"), core_first)
    pair_y = in_order(pair_core[0], swap(pair_core[1], "y"), y_first)
    pair_y = pair_y.reshape(experts_local, seq_len)
    if tensor_size == 2:
        local = seq_len // 2
        give = lax.dynamic_slice_in_dim(pair_y, (1 - my_tensor) * local, local, 1)
        keep = lax.dynamic_slice_in_dim(pair_y, my_tensor * local, local, 1)
        pair_all = in_order(keep, swap(give, "tensor"), tensor_first)
    else:
        local = seq_len // tensor_size
        pair_all = lax.all_gather(pair_y, "tensor", axis=0, tiled=True)
        pair_all = lax.dynamic_slice_in_dim(pair_all, my_tensor * local, local, 1)
    normed_pair, pair_all = together(add_core(normed_parts), pair_all)
    normed_local = scatter_group(normed_pair, tensor_size)

    def core_owners(part):
        part = jnp.moveaxis(part.reshape(bunch, 2, 2, rows, both_width), 2, 0)
        return stacked(part[0], swap(part[1], "core"), core_first, 0)

    def y_owners(part):
        keep, give = part[:, :, 0], part[:, :, 1]
        return stacked(keep, swap(give, "y"), y_first, 0)

    early = parts[:-1]
    normed_local, *early = together(normed_local, *[core_owners(part) for part in early])
    gates_local = lax.dynamic_slice_in_dim(gates[0], my_tensor * local, local, 1)
    gate_dot = jnp.sum(gates_local * pair_all, axis=0, keepdims=True)
    logit_low = (gates_local * (pair_all - gate_dot)).astype(bf16)

    normed_local = normed_local + contract(logit_low, router_weight, 0, 1)
    router_part = jnp.dot(logit_low, ffn_normed, preferred_element_type=f32)
    state_grad, ffn_gain_part = norm_backward(normed_local, hidden_state, ffn_gain)
    state_grad = state_grad + grad_rows
    attn_grad_all = gather_rows((residual_scale * state_grad).astype(bf16), tensor_size)
    moe_pair = add_core(after(moe_parts, normed_pair))
    owners = [y_owners(part) for part in early]
    attn_grad_all, moe_pair, *owners = together(attn_grad_all, moe_pair, *owners)
    if tensor_size == 2:
        local = seq_len // 2
        moe_far = lax.dynamic_slice_in_dim(moe_pair[1], (1 - my_tensor) * local, local, 0)
        moe_near = lax.dynamic_slice_in_dim(moe_pair[1], my_tensor * local, local, 0)
    else:
        moe_far, moe_near = moe_pair[1], jnp.zeros((1, width), bf16)
    moe_far = swap(moe_far, "y")

    def halves(part, mine):
        return at(part, mine), at(part, 1 - mine).astype(bf16)

    def by_dp(part):
        return part.reshape(z_size, 2, 2, shard_rows, part.shape[1])

    def add(keep, given):
        return keep.astype(f32) + given.astype(f32)

    out_part = contract(attn_grad_all, attn_mixed, 0, 0)
    out_keep, out_give = halves(jnp.moveaxis(by_dp(out_part), 2, 0), my_core)
    out_given = swap(out_give, "core")
    mixed_grad = jnp.dot(attn_grad_all, out_full, preferred_element_type=f32).astype(bf16)
    qkv_pre_grad = attention_backward(qkv_rot, mixed_grad, log_totals, cosine, sine)
    qkv_pre_grad, moe_far, out_given = together(qkv_pre_grad, moe_far, out_given)

    out_keep, out_give = halves(jnp.moveaxis(add(out_keep, out_given), 1, 0), my_y)
    attn_part = contract(qkv_pre_grad, qkv_full, 1, 1)
    attn_scattered = scatter_rows(attn_part, tensor_size)
    qkv_part = contract(attn_tokens, qkv_pre_grad, 0, 0)
    qkv_keep, qkv_give = halves(jnp.moveaxis(by_dp(qkv_part), 2, 0), my_core)
    attn_normed_grad, moe_near, qkv_given = together(
        attn_scattered, swap(moe_near, "y"), swap(qkv_give, "core")
    )
    input_part, attn_gain_part = norm_backward(attn_normed_grad, input_rows, attn_gain)
    input_grad = (state_grad + input_part).astype(bf16)
    small = jnp.concatenate(
        [router_part, ffn_gain_part[None, :], attn_gain_part[None, :]], axis=0
    )
    if tensor_size == 2:
        moe_give = lax.dynamic_slice_in_dim(moe_pair[0], (1 - my_tensor) * local, local, 0)
        moe_keep = lax.dynamic_slice_in_dim(moe_pair[0], my_tensor * local, local, 0)
        moe_sum = add(moe_keep, moe_near)
        moe_given = swap(add(moe_give, moe_far).astype(bf16), "tensor")
    else:
        moe_sum = jnp.zeros((local, width), f32)
        moe_given = scatter_rows(add(moe_pair[0], moe_far), tensor_size)
    qkv_keep, qkv_give = halves(jnp.moveaxis(add(qkv_keep, qkv_given), 1, 0), my_y)
    small = butterfly_sum(small, (("core", 2), ("z", z_size)))
    small, qkv_given, out_given = together(small, swap(qkv_give, "y"), swap(out_give, "y"))

    def z_scatter(part):
        step = z_size // 2
        while step:
            keep, give = halves(
                part.reshape(2, -1, shard_rows, part.shape[-1]), (my_z // step) % 2
            )
            pairs = [(i, i ^ step) for i in range(z_size)]
            part = add(keep, lax.ppermute(give, "z", pairs))
            step //= 2
        return part.reshape(shard_rows, part.shape[-1])

    dp_part = jnp.concatenate([add(qkv_keep, qkv_given), add(out_keep, out_given)], axis=-1)
    dp_sum = z_scatter(dp_part)
    small, moe_given, dp_sum = together(butterfly_sum(small, (("y", 2),)), moe_given, dp_sum)
    qkv_sum, out_sum = dp_sum[:, :wide], dp_sum[:, wide:]
    block_output = (hidden_state + residual_scale * add(moe_sum, moe_given)).astype(bf16)
    small = butterfly_sum(small, (("tensor", tensor_size),))
    owners.append(y_owners(core_owners(after(parts[-1], dp_sum))))
    summed = jnp.concatenate(owners, axis=2)
    summed = summed.reshape(experts_local, rows, both_width)
    both_rows = gate_weight.shape[1]
    qkv_sum = qkv_sum.reshape(shard_rows, groups, -1)
    return (
        block_output,
        input_grad,
        small[expert_count + 1],
        qkv_sum[:, :, : 2 * HEAD].reshape(query_weight.shape).astype(f32),
        qkv_sum[:, :, 2 * HEAD :].astype(f32),
        out_sum.T.astype(f32),
        small[expert_count],
        small[:expert_count].T,
        summed[:, :both_rows, :hidden].astype(f32),
        summed[:, :both_rows, hidden:].astype(f32),
        summed[:, both_rows:].astype(f32),
    )


def solution(mesh):
    dp, tensor = mesh.shape["dp"], mesh.shape["tensor"]
    fine = Mesh(mesh.devices.reshape(dp // 4, 2, 2, tensor), ("z", "y", "core", "tensor"))
    rows = ("z", "y", "core")
    every = rows + ("tensor",)
    experts = P("tensor", rows, None)
    return jax.shard_map(
        functools.partial(shards, dict(fine.shape)),
        mesh=fine,
        in_specs=(
            P(every, None),
            P(rows),
            P(rows, None),
            P(),
            P(rows, "tensor"),
            P(rows, "tensor", None),
            P("tensor", rows),
            P(),
            P(),
            experts,
            experts,
            experts,
            P(every, None),
        ),
        out_specs=(
            P(every, None),
            P(every, None),
            P(),
            P(rows, "tensor"),
            P(rows, "tensor", None),
            P("tensor", rows),
            P(),
            P(),
            experts,
            experts,
            experts,
        ),
        check_vma=False,
    )
```

```python
import functools

import jax
import jax.numpy as jnp
from jax import lax
from jax.experimental import pallas as pl
from jax.experimental.pallas import tpu as pltpu
from jax.sharding import Mesh, PartitionSpec as P

CAP = 320
HEAD = 64
HALF = HEAD // 2
LANES = 2 * HEAD
BLOCK = 256
norm_eps = 1e-06
attn_scale = 0.015625
residual_scale = 0.22
rope_base = 10000.0
masked_score = -1e30
f32 = jnp.float32
bf16 = jnp.bfloat16


def row_scale(values):
    return lax.rsqrt(jnp.mean(values * values, axis=-1, keepdims=True) + norm_eps)


def contract(left, right, left_dim, right_dim):
    return lax.dot_general(
        left, right, (((left_dim,), (right_dim,)), ((), ())), preferred_element_type=f32
    )


def ein(spec, *operands):
    return jnp.einsum(spec, *operands, preferred_element_type=f32)


def norm_backward(normed_grad, source, gain):
    scale_rows = row_scale(source)
    unit_rows = source * scale_rows
    scaled_grad = normed_grad * gain
    gain_grad = jnp.sum(normed_grad * unit_rows, axis=0)
    source_grad = scale_rows * (
        scaled_grad - unit_rows * jnp.mean(scaled_grad * unit_rows, axis=-1, keepdims=True)
    )
    return (source_grad, gain_grad)


def together(*values):
    return lax.optimization_barrier(values)


def after(values, *earlier):
    return lax.optimization_barrier((values,) + earlier)[0]


def swap(values, axis):
    return lax.ppermute(values, axis, [(0, 1), (1, 0)])


def butterfly_sum(values, sizes):
    for axis, size in sizes:
        step = 1
        while step < size:
            values = values + lax.ppermute(values, axis, [(i, i ^ step) for i in range(size)])
            step *= 2
    return values


def in_order(mine, theirs, first):
    return jnp.concatenate(
        [jnp.where(first, mine, theirs), jnp.where(first, theirs, mine)], axis=0
    )


def gather_rows(rows, tensor_size):
    if tensor_size != 2:
        return lax.all_gather(rows, "tensor", axis=0, tiled=True)
    return in_order(rows, swap(rows, "tensor"), lax.axis_index("tensor") == 0)


def scatter_rows(values, tensor_size):
    if tensor_size != 2:
        return lax.psum_scatter(
            values.astype(bf16), "tensor", scatter_dimension=0, tiled=True
        ).astype(f32)
    half = values.shape[0] // 2
    me = lax.axis_index("tensor")
    give = lax.dynamic_slice_in_dim(values, (1 - me) * half, half, 0).astype(bf16)
    keep = lax.dynamic_slice_in_dim(values, me * half, half, 0)
    return keep.astype(f32) + swap(give, "tensor").astype(f32)


def gather_group(rows, tensor_size, earlier):
    if tensor_size != 2:
        own = gather_rows(rows, tensor_size)
        across = swap(own, "y")
    else:
        first = lax.axis_index("tensor") == 0
        half = rows.shape[0] // 2
        by_tensor, by_y, _ = together(swap(rows, "tensor"), swap(rows, "y"), earlier)
        own = in_order(rows, by_tensor, first)
        low, high, own_core = together(
            swap(by_y[:half], "tensor"), swap(by_tensor[half:], "y"), swap(own, "core")
        )
        corner = jnp.concatenate([low, high], axis=0)
        across = in_order(by_y, corner, first)
        return jnp.stack([own, across, own_core, swap(across, "core")])
    return jnp.stack([own, across, swap(own, "core"), swap(across, "core")])


def add(keep, given):
    return keep.astype(f32) + given.astype(f32)


def piece(near, given, sequence, which, rows):
    return add(
        lax.dynamic_slice_in_dim(near[sequence], which * rows, rows, 0),
        lax.dynamic_slice_in_dim(given[sequence], which * rows, rows, 0),
    )


def scatter_group(near, given, tensor_size):
    if tensor_size != 2:
        own, across = add(near[0], given[0]), add(near[1], given[1])
        own = own + swap(across.astype(bf16), "y").astype(f32)
        return scatter_rows(own, tensor_size)
    me = lax.axis_index("tensor")
    rows = near.shape[1] // 2
    half = rows // 2
    take = functools.partial(piece, near, given)
    corner = take(1, 1 - me, rows).astype(bf16)
    low, high = swap(corner[:half], "tensor"), swap(corner[half:], "y")
    by_tensor, by_y = take(0, 1 - me, rows), take(1, me, rows)
    first_tensor = swap(by_tensor[:half].astype(bf16), "tensor")
    first_y = swap(by_y[half:].astype(bf16), "y")
    low, high = together(low, high)
    rest_tensor = swap(add(by_tensor[half:], high).astype(bf16), "tensor")
    rest_y = swap(add(by_y[:half], low).astype(bf16), "y")
    first_tensor, first_y, rest_tensor, rest_y = together(
        first_tensor, first_y, rest_tensor, rest_y
    )
    mine = take(0, me, rows)
    return mine + add(
        jnp.concatenate([first_tensor, rest_tensor], axis=0),
        jnp.concatenate([rest_y, first_y], axis=0),
    )


def rope_lanes(values, cosine, sine, first, direction):
    lanes = values.shape[1]
    turned = jnp.where(
        first, pltpu.roll(values, lanes - HALF, 1), pltpu.roll(values, HALF, 1)
    )
    return values * cosine + direction * (turned * sine)


def lane_ids(rows):
    return lax.broadcasted_iota(jnp.int32, (rows, LANES), 1)


def attention_forward_kernel(pre_ref, cos_ref, sin_ref, mixed_ref, rot_ref, lse_ref):
    seq_len = pre_ref.shape[0]
    lane = lane_ids(seq_len)
    first = (lane & (2 * HALF - 1)) < HALF
    low = lane < HEAD
    cosine, sine = cos_ref[...], sin_ref[...]
    query = rope_lanes(pre_ref[:, :LANES], cosine, sine, first, 1.0).astype(bf16)
    kv = pre_ref[:, LANES:]
    kv = jnp.where(low, rope_lanes(kv, cosine, sine, first, 1.0), kv)
    rot_ref[:, :LANES] = query
    rot_ref[:, LANES:] = kv.astype(bf16)
    keys, values_in = head_pairs(kv, low)
    block = min(BLOCK, seq_len)
    for start in range(0, seq_len, block):
        stop = start + block
        allowed = causal(block, stop, start)
        total = jnp.zeros((block, LANES), f32)
        lses = []
        for head in (0, 1):
            scores = (
                contract(query[start:stop], keys[head][:stop], 1, 1) * attn_scale
            )
            scores = jnp.where(allowed, scores, masked_score)
            top = jnp.max(scores, axis=1, keepdims=True)
            raised = jnp.exp(scores - top)
            summed = jnp.sum(raised, axis=1, keepdims=True)
            prob = (raised * (1.0 / summed)).astype(bf16)
            total = total + jnp.dot(prob, values_in[head][:stop], preferred_element_type=f32)
            lses.append(top + jnp.log(summed))
        mixed_ref[start:stop, :] = total.astype(bf16)
        lse_ref[start:stop, :] = jnp.where(lane_ids(block) < HEAD, lses[0], lses[1])


def head_pairs(kv, low):
    kv = kv.astype(f32)
    turned = pltpu.roll(kv, HEAD, 1)
    zero = jnp.zeros_like(kv)
    keys = [jnp.where(low, kv, zero).astype(bf16), jnp.where(low, zero, turned).astype(bf16)]
    values_in = [jnp.where(low, turned, zero).astype(bf16), jnp.where(low, zero, kv).astype(bf16)]
    return keys, values_in


def causal(rows, columns, start):
    return lax.broadcasted_iota(jnp.int32, (rows, columns), 1) <= start + lax.broadcasted_iota(
        jnp.int32, (rows, columns), 0
    )


def attention_backward_kernel(
    rot_ref, grad_ref, lse_ref, cos_ref, sin_ref, out_ref, key_acc, value_acc
):
    seq_len = rot_ref.shape[0]
    lane = lane_ids(seq_len)
    first = (lane & (2 * HALF - 1)) < HALF
    low = lane < HEAD
    cosine, sine = cos_ref[...], sin_ref[...]
    keys, values_in = head_pairs(rot_ref[:, LANES:], low)
    key_acc[...] = jnp.zeros_like(key_acc)
    value_acc[...] = jnp.zeros_like(value_acc)
    block = min(BLOCK, seq_len)
    for start in range(0, seq_len, block):
        stop = start + block
        allowed = causal(block, stop, start)
        query = rot_ref[start:stop, :LANES]
        grad = grad_ref[start:stop, :]
        query_grad = jnp.zeros((block, LANES), f32)
        for head in (0, 1):
            scores = contract(query, keys[head][:stop], 1, 1) * attn_scale
            log_total = lse_ref[start:stop, head * HEAD : head * HEAD + 1]
            prob = jnp.where(allowed, jnp.exp(jnp.where(allowed, scores - log_total, 0.0)), 0.0)
            prob_grad = contract(grad, values_in[head][:stop], 1, 1)
            row_dot = jnp.sum(prob * prob_grad, axis=1, keepdims=True)
            score_grad = (prob * (prob_grad - row_dot)).astype(bf16)
            query_grad = query_grad + jnp.dot(
                score_grad, keys[head][:stop], preferred_element_type=f32
            )
            key_acc[head, :stop, :] += contract(score_grad, query, 0, 0)
            value_acc[head, :stop, :] += contract(prob.astype(bf16), grad, 0, 0)
        lane_block = (lane_ids(block) & (2 * HALF - 1)) < HALF
        out_ref[start:stop, :LANES] = rope_lanes(
            query_grad * attn_scale, cosine[start:stop], sine[start:stop], lane_block, -1.0
        ).astype(bf16)
    key_grad = (key_acc[0] + pltpu.roll(key_acc[1], HEAD, 1)) * attn_scale
    key_grad = rope_lanes(jnp.where(low, key_grad, 0.0), cosine, sine, first, -1.0)
    value_grad = pltpu.roll(value_acc[0], HEAD, 1) + value_acc[1]
    out_ref[:, LANES:] = jnp.where(low, key_grad, value_grad).astype(bf16)


def by_head(width):
    return lambda seq_len: pl.BlockSpec((seq_len, width), lambda g: (0, g))


def attention_forward(pre, cosine, sine):
    seq_len, width = pre.shape
    groups = width // (2 * LANES)
    whole = pl.BlockSpec((seq_len, LANES), lambda g: (0, 0))
    wide, narrow = by_head(2 * LANES)(seq_len), by_head(LANES)(seq_len)
    return pl.pallas_call(
        attention_forward_kernel,
        grid=(groups,),
        in_specs=[wide, whole, whole],
        out_specs=[narrow, wide, narrow],
        out_shape=[
            jax.ShapeDtypeStruct((seq_len, width // 2), bf16),
            jax.ShapeDtypeStruct((seq_len, width), bf16),
            jax.ShapeDtypeStruct((seq_len, width // 2), f32),
        ],
        cost_estimate=pl.CostEstimate(
            flops=6 * groups * seq_len * seq_len * LANES,
            bytes_accessed=10 * seq_len * width,
            transcendentals=groups * seq_len * seq_len,
        ),
        name="attention_forward",
    )(pre, cosine, sine)


def attention_backward(rot, grad, lse, cosine, sine):
    seq_len, width = rot.shape
    groups = width // (2 * LANES)
    whole = pl.BlockSpec((seq_len, LANES), lambda g: (0, 0))
    wide, narrow = by_head(2 * LANES)(seq_len), by_head(LANES)(seq_len)
    return pl.pallas_call(
        attention_backward_kernel,
        grid=(groups,),
        in_specs=[wide, narrow, narrow, whole, whole],
        out_specs=wide,
        out_shape=jax.ShapeDtypeStruct((seq_len, width), bf16),
        scratch_shapes=[pltpu.VMEM((2, seq_len, LANES), f32)] * 2,
        cost_estimate=pl.CostEstimate(
            flops=16 * groups * seq_len * seq_len * LANES,
            bytes_accessed=10 * seq_len * width,
            transcendentals=groups * seq_len * seq_len,
        ),
        name="attention_backward",
    )(rot, grad, lse, cosine, sine)


def expert_kernel(
    carried, shared, last, member_ref, tokens_ref, grad_ref, code_ref, gate_ref, weight_ref, *refs
):
    if carried:
        moe_in, normed_in, *refs = refs
    if shared:
        refs = refs[1:]
    *sum_refs, pair_ref, part_ref, both, down, both_acc, down_acc = refs
    step = pl.program_id(0)

    def put(place, values):
        if not last:
            sum_refs[place][0] = values
            return

        @pl.when(step < 2)
        def _():
            sum_refs[2 * place][0] = values

        @pl.when(step >= 2)
        def _():
            sum_refs[2 * place + 1][0] = values
    shards_z, members, rows = weight_ref.shape[0], weight_ref.shape[2], weight_ref.shape[3]
    hidden = down.shape[0]
    both_rows = both.shape[0] // (shards_z * members)
    down_rows = hidden // (shards_z * members)

    def places():
        for z in range(shards_z):
            for rel in range(members):
                at = z * members + (member_ref[0] ^ rel)
                yield (
                    z,
                    rel,
                    pl.ds(pl.multiple_of(at * both_rows, both_rows), both_rows),
                    pl.ds(pl.multiple_of(at * down_rows, down_rows), down_rows),
                )

    @pl.when(step == 0)
    def _():
        for z, rel, both_at, down_at in places():
            both[both_at, :] = weight_ref[z, 0, rel, :both_rows, :]
            down[down_at, :] = weight_ref[z, 0, rel, both_rows:, :]
        both_acc[...] = jnp.zeros_like(both_acc)
        down_acc[...] = jnp.zeros_like(down_acc)

    seq_len = tokens_ref.shape[1]
    slot = lax.broadcasted_iota(jnp.int32, (CAP, seq_len), 0)
    match = code_ref[0] == slot
    dispatch = jnp.where(match, 1.0, 0.0).astype(bf16)
    slot_gate = jnp.sum(jnp.where(match, gate_ref[0], 0.0), axis=1, keepdims=True)
    expert_in = jnp.dot(dispatch, tokens_ref[0], preferred_element_type=f32).astype(bf16)
    gate_pre = jnp.dot(expert_in, both[:, :hidden], preferred_element_type=f32)
    up_pre = jnp.dot(expert_in, both[:, hidden:], preferred_element_type=f32)
    sigmoid = 1.0 / (1.0 + jnp.exp(-gate_pre))
    silu = gate_pre * sigmoid
    hidden_act = (silu * up_pre).astype(bf16)
    expert_out = jnp.dot(hidden_act, down[...], preferred_element_type=f32)
    weighted = (slot_gate * expert_out).astype(bf16)
    moe = contract(dispatch, weighted, 0, 0)
    if carried:
        moe = moe + moe_in[0].astype(f32)
    put(0, moe.astype(bf16))

    slot_grad = jnp.dot(dispatch, grad_ref[0], preferred_element_type=f32)
    raw_grad = contract(slot_grad.astype(bf16), down[...], 1, 1)
    slot_gate_grad = jnp.sum(hidden_act.astype(f32) * raw_grad, axis=1, keepdims=True)
    pair_ref[0] = jnp.sum(jnp.where(match, slot_gate_grad, 0.0), axis=0, keepdims=True)
    hidden_grad = slot_gate * raw_grad
    gate_grad = (
        hidden_grad * up_pre * sigmoid * (1.0 + gate_pre * (1.0 - sigmoid))
    ).astype(bf16)
    up_grad = (hidden_grad * silu).astype(bf16)
    down_acc[...] += contract(hidden_act, (slot_gate * slot_grad).astype(bf16), 0, 0)
    both_acc[:, :hidden] += contract(expert_in, gate_grad, 0, 0)
    both_acc[:, hidden:] += contract(expert_in, up_grad, 0, 0)
    in_grad = (
        contract(gate_grad, both[:, :hidden], 1, 1) + contract(up_grad, both[:, hidden:], 1, 1)
    ).astype(bf16)
    normed = contract(dispatch, in_grad, 0, 0)
    if carried:
        normed = normed + normed_in[0].astype(f32)
    put(1, normed.astype(bf16))

    @pl.when(step == pl.num_programs(0) - 1)
    def _():
        for z, rel, both_at, down_at in places():
            part_ref[z, 0, rel, :both_rows, :] = both_acc[both_at, :].astype(bf16)
            part_ref[z, 0, rel, both_rows:, :] = down_acc[down_at, :].astype(bf16)


def run_expert(
    member, tokens, grads, code, gate, weight, source, bunch, place, last, carry, shared
):
    sequences, seq_len, width = tokens.shape
    shards_z, held, members, rows, both_width = weight.shape
    hidden = both_width // 2
    per_seq = pl.BlockSpec((1, seq_len, width), lambda s: (s, 0, 0))
    per_row = pl.BlockSpec((1, 1, seq_len), lambda s: (s, 0, 0))
    one = (shards_z, 1, members, rows, both_width)
    every = pl.BlockSpec(one, lambda s: (0, source, 0, 0, 0), pipeline_mode=pl.Buffered(1))
    part = pl.BlockSpec(one, lambda s: (0, place, 0, 0, 0))
    slots = sequences * CAP
    if last:
        near = pl.BlockSpec((1, seq_len, width), lambda s: (jnp.minimum(s, 1), 0, 0))
        far = pl.BlockSpec((1, seq_len, width), lambda s: (jnp.maximum(s - 2, 0), 0, 0))
        sums = [near, far, near, far]
        sum_shapes = [jax.ShapeDtypeStruct((2, seq_len, width), bf16)] * 4
    else:
        sums, sum_shapes = [per_seq] * 2, [jax.ShapeDtypeStruct(tokens.shape, bf16)] * 2
    return pl.pallas_call(
        functools.partial(expert_kernel, bool(carry), bool(shared), last),
        grid=(sequences,),
        in_specs=[
            pl.BlockSpec(memory_space=pltpu.SMEM),
            per_seq,
            per_seq,
            per_row,
            per_row,
            every,
        ]
        + [per_seq] * len(carry)
        + [pl.BlockSpec(memory_space=pl.ANY)] * len(shared),
        out_specs=sums + [per_row, part],
        out_shape=sum_shapes
        + [
            jax.ShapeDtypeStruct((sequences, 1, seq_len), f32),
            jax.ShapeDtypeStruct((shards_z, bunch, members, rows, both_width), bf16),
        ],
        scratch_shapes=[
            pltpu.VMEM((width, both_width), bf16),
            pltpu.VMEM((hidden, width), bf16),
            pltpu.VMEM((width, both_width), f32),
            pltpu.VMEM((hidden, width), f32),
        ],
        compiler_params=pltpu.CompilerParams(vmem_limit_bytes=66_000_000),
        cost_estimate=pl.CostEstimate(
            flops=2 * slots * width * (4 * seq_len + 9 * hidden),
            bytes_accessed=12 * sequences * seq_len * width + 4 * (weight.size // held),
            transcendentals=slots * hidden,
        ),
        name="expert",
        input_output_aliases={6 + len(carry): len(sums) + 1} if shared else {},
    )(member, tokens, grads, code, gate, weight, *carry, *shared)


def shards(
    sizes,
    block_input,
    positions,
    expert_ids,
    attn_gain,
    query_weight,
    kv_weight,
    out_weight,
    ffn_gain,
    router_weight,
    gate_weight,
    up_weight,
    down_weight,
    out_grad,
):
    tensor_size, z_size = sizes["tensor"], sizes["z"]
    seq_len = positions.shape[0]
    width = block_input.shape[1]
    shard_rows, groups = kv_weight.shape[:2]
    q_width = query_weight.shape[1]
    wide = 2 * q_width
    expert_count = router_weight.shape[1]
    experts_local = gate_weight.shape[0]
    owned = experts_local // 4
    hidden = gate_weight.shape[2]
    my_z, my_y, my_core = lax.axis_index("z"), lax.axis_index("y"), lax.axis_index("core")
    my_tensor = lax.axis_index("tensor")
    y_first, core_first, tensor_first = my_y == 0, my_core == 0, my_tensor == 0

    def at(values, index):
        return lax.dynamic_index_in_dim(values, index, 0, keepdims=False)

    def stacked(mine, theirs, is_first, axis=1):
        ordered = [jnp.where(is_first, mine, theirs), jnp.where(is_first, theirs, mine)]
        return jnp.stack(ordered, axis)

    packed = jnp.concatenate(
        [
            jnp.concatenate([query_weight.reshape(shard_rows, groups, -1), kv_weight], axis=2)
            .reshape(shard_rows, wide),
            out_weight.T,
        ],
        axis=1,
    )
    packed_full = lax.all_gather(packed, ("z", "y", "core"), axis=0, tiled=True)

    input_rows = block_input.astype(f32)
    attn_normed = (input_rows * row_scale(input_rows) * attn_gain).astype(bf16)
    attn_tokens = gather_rows(attn_normed, tensor_size)
    grad_rows = out_grad.astype(f32)
    moe_rows = after((residual_scale * grad_rows).astype(bf16), attn_tokens)

    experts = jnp.concatenate(
        [jnp.concatenate([gate_weight, up_weight], axis=2), down_weight], axis=1
    )
    rows, both_width = experts.shape[1:]
    grouped = experts.reshape(2, 2, owned, rows, both_width)
    own_y, give_y = at(grouped, my_y), at(grouped, 1 - my_y)
    from_y = swap(give_y, "y")
    members = jnp.stack(
        [
            at(own_y, my_core),
            swap(at(own_y, 1 - my_core), "core"),
            at(from_y, my_core),
            swap(at(from_y, 1 - my_core), "core"),
        ],
        axis=1,
    )
    moe_own = gather_rows(moe_rows, tensor_size)

    ids_t = expert_ids.T
    hits = jnp.zeros((expert_count, seq_len), jnp.bool_)
    for k in range(ids_t.shape[0]):
        hits = hits | (ids_t[k][None, :] == jnp.arange(expert_count)[:, None])
    token_ids = jnp.arange(seq_len)
    earlier = (token_ids[:, None] < token_ids[None, :]).astype(bf16)
    rank = jnp.dot(hits.astype(bf16), earlier, preferred_element_type=f32)
    code = jnp.where(hits, jnp.where(rank < CAP, rank, -1.0), -2.0)

    half_dim = HEAD // 2
    frequency = rope_base ** (-(jnp.arange(half_dim, dtype=f32) * 2.0 / HEAD))
    angles = positions.astype(f32)[:, None] * frequency[None, :]
    cosine = jnp.tile(jnp.cos(angles), (1, 4))
    sine = jnp.tile(jnp.concatenate([-jnp.sin(angles), jnp.sin(angles)], axis=1), (1, 2))

    packed_full, attn_tokens, moe_own, members, code, cosine, sine = together(
        packed_full, attn_tokens, moe_own, members, code, cosine, sine
    )
    qkv_full, out_full = packed_full[:, :wide], packed_full[:, wide:]
    bunch = min(2, owned)
    weights, launched = [], None
    for start, stop in [(0, bunch)] + [(e, e + 1) for e in range(bunch, owned)]:
        item = members[start:stop]
        if launched is not None:
            item = after(item, launched)
        launched = item
        item = lax.all_gather(item, "z", axis=0, tiled=False)
        weights += [(item, e) for e in range(stop - start)]

    qkv_pre = jnp.dot(attn_tokens, qkv_full, preferred_element_type=f32)
    qkv_pre, moe_own, code_y = together(qkv_pre, moe_own, swap(code, "y"))
    moe_across = swap(moe_own, "y")
    attn_mixed, qkv_rot, log_totals = attention_forward(qkv_pre, cosine, sine)
    attn_out = scatter_rows(contract(attn_mixed, out_full, 1, 1), tensor_size)
    codes = jnp.stack([code, code_y, swap(code, "core"), swap(code_y, "core")])
    attn_out, moe_across, codes = together(attn_out, moe_across, codes)
    moe_grad = jnp.stack([moe_own, moe_across, swap(moe_own, "core"), swap(moe_across, "core")])
    hidden_state = input_rows + residual_scale * attn_out
    ffn_normed = (hidden_state * row_scale(hidden_state) * ffn_gain).astype(bf16)

    tokens = gather_group(ffn_normed, tensor_size, moe_grad)
    logits = ein("dx,std->sxt", router_weight, tokens)
    chosen = codes > -1.5
    top_logit = jnp.max(jnp.where(chosen, logits, -jnp.inf), axis=1, keepdims=True)
    raised = jnp.where(chosen, jnp.exp(jnp.where(chosen, logits - top_logit, 0.0)), 0.0)
    gates = raised / jnp.sum(raised, axis=1, keepdims=True)
    member = my_y * 2 + my_core
    expert_first = my_tensor * experts_local + member * owned
    code_own = lax.dynamic_slice_in_dim(codes, expert_first, owned, 1).astype(jnp.int32)
    gate_own = lax.dynamic_slice_in_dim(gates, expert_first, owned, 1)

    carry, pairs, parts, shared = (), [], [], ()
    for e in range(owned):
        *carry, pair, part = run_expert(
            member.reshape(1).astype(jnp.int32),
            tokens,
            moe_grad,
            code_own[:, e : e + 1],
            gate_own[:, e : e + 1],
            *weights[e],
            bunch,
            e % bunch,
            e + 1 == owned,
            carry,
            shared,
        )
        pairs.append(pair)
        shared = (part,)
        if (e + 1) % bunch == 0:
            parts.append(lax.psum_scatter(part, "z", scatter_dimension=0, tiled=False))
            shared = ()
    moe_near, moe_give, normed_near, normed_give = carry

    pair_grad = jnp.concatenate(pairs, axis=1)
    pair_core = stacked(pair_grad[:2], swap(pair_grad[2:], "core"), core_first)
    pair_y = in_order(pair_core[0], swap(pair_core[1], "y"), y_first)
    pair_y = pair_y.reshape(experts_local, seq_len)
    if tensor_size == 2:
        local = seq_len // 2
        give = lax.dynamic_slice_in_dim(pair_y, (1 - my_tensor) * local, local, 1)
        keep = lax.dynamic_slice_in_dim(pair_y, my_tensor * local, local, 1)
        pair_all = in_order(keep, swap(give, "tensor"), tensor_first)
    else:
        local = seq_len // tensor_size
        pair_all = lax.all_gather(pair_y, "tensor", axis=0, tiled=True)
        pair_all = lax.dynamic_slice_in_dim(pair_all, my_tensor * local, local, 1)
    normed_given, pair_all = together(swap(normed_give, "core"), pair_all)
    normed_local = scatter_group(normed_near, normed_given, tensor_size)

    def core_owners(part):
        part = jnp.moveaxis(part.reshape(bunch, 2, 2, rows, both_width), 2, 0)
        return stacked(part[0], swap(part[1], "core"), core_first, 0)

    def y_owners(part):
        keep, give = part[:, :, 0], part[:, :, 1]
        return stacked(keep, swap(give, "y"), y_first, 0)

    early = parts[:-1]
    moe_given = swap(after(moe_give, normed_given), "core")
    normed_local, moe_given = together(normed_local, moe_given)
    gates_local = lax.dynamic_slice_in_dim(gates[0], my_tensor * local, local, 1)
    gate_dot = jnp.sum(gates_local * pair_all, axis=0, keepdims=True)
    logit_low = (gates_local * (pair_all - gate_dot)).astype(bf16)

    normed_local = normed_local + contract(logit_low, router_weight, 0, 1)
    router_part = jnp.dot(logit_low, ffn_normed, preferred_element_type=f32)
    state_grad, ffn_gain_part = norm_backward(normed_local, hidden_state, ffn_gain)
    state_grad = state_grad + grad_rows
    attn_grad_all = gather_rows((residual_scale * state_grad).astype(bf16), tensor_size)
    if tensor_size == 2:
        local = seq_len // 2
        moe_piece = functools.partial(piece, moe_near, moe_given)
        moe_far = moe_piece(1, 1 - my_tensor, local).astype(bf16)
        moe_own_far = moe_piece(1, my_tensor, local).astype(bf16)
    else:
        moe_far = add(moe_near[1], moe_given[1]).astype(bf16)
        moe_own_far = jnp.zeros((1, width), bf16)
    attn_grad_all, moe_far, moe_own_far = together(
        attn_grad_all, swap(moe_far, "y"), moe_own_far
    )
    early = [core_owners(after(part, attn_grad_all)) for part in early]
    moe_own_far = swap(moe_own_far, "y")

    def halves(part, mine):
        return at(part, mine), at(part, 1 - mine).astype(bf16)

    def by_dp(part):
        return part.reshape(z_size, 2, 2, shard_rows, part.shape[1])

    mixed_grad = jnp.dot(attn_grad_all, out_full, preferred_element_type=f32).astype(bf16)
    qkv_pre_grad = attention_backward(qkv_rot, mixed_grad, log_totals, cosine, sine)
    qkv_pre_grad, moe_own_far = together(qkv_pre_grad, moe_own_far)

    attn_part = contract(qkv_pre_grad, qkv_full, 1, 1)
    attn_scattered = scatter_rows(attn_part, tensor_size)
    tokens_late, grads_late, _ = together(attn_tokens, attn_grad_all, attn_part)
    qkv_part = contract(tokens_late, qkv_pre_grad, 0, 0)
    qkv_keep, qkv_give = halves(jnp.moveaxis(by_dp(qkv_part), 2, 0), my_core)
    out_part = contract(grads_late, attn_mixed, 0, 0)
    out_keep, out_give = halves(jnp.moveaxis(by_dp(out_part), 2, 0), my_core)
    attn_normed_grad, qkv_given, out_given, *owners = together(
        attn_scattered,
        swap(qkv_give, "core"),
        swap(out_give, "core"),
        *[y_owners(part) for part in early],
    )
    input_part, attn_gain_part = norm_backward(attn_normed_grad, input_rows, attn_gain)
    input_grad = (state_grad + input_part).astype(bf16)
    small = jnp.concatenate(
        [router_part, ffn_gain_part[None, :], attn_gain_part[None, :]], axis=0
    )
    if tensor_size == 2:
        moe_sum = add(moe_piece(0, my_tensor, local), moe_own_far)
        moe_given = swap(
            add(moe_piece(0, 1 - my_tensor, local), moe_far).astype(bf16), "tensor"
        )
    else:
        moe_sum = jnp.zeros((local, width), f32)
        moe_given = scatter_rows(add(add(moe_near[0], moe_given[0]), moe_far), tensor_size)
    qkv_keep, qkv_give = halves(jnp.moveaxis(add(qkv_keep, qkv_given), 1, 0), my_y)
    out_keep, out_give = halves(jnp.moveaxis(add(out_keep, out_given), 1, 0), my_y)
    small = butterfly_sum(small, (("core", 2), ("z", z_size)))
    late = core_owners(after(parts[-1], attn_normed_grad))
    small, qkv_given, out_given, moe_given, late = together(
        small, swap(qkv_give, "y"), swap(out_give, "y"), moe_given, late
    )
    dp_sum = jnp.concatenate([add(qkv_keep, qkv_given), add(out_keep, out_given)], axis=-1)
    step = 1
    while step < z_size:
        keep, give = halves(
            jnp.moveaxis(dp_sum.reshape(-1, 2, shard_rows, dp_sum.shape[-1]), 1, 0),
            (my_z // step) % 2,
        )
        dp_sum = add(keep, lax.ppermute(give, "z", [(i, i ^ step) for i in range(z_size)]))
        step *= 2
    dp_sum = dp_sum.reshape(shard_rows, dp_sum.shape[-1])
    late = y_owners(late)
    small, dp_sum = together(butterfly_sum(small, (("y", 2),)), dp_sum)
    qkv_sum, out_sum = dp_sum[:, :wide], dp_sum[:, wide:]
    block_output = (hidden_state + residual_scale * add(moe_sum, moe_given)).astype(bf16)
    small = butterfly_sum(small, (("tensor", tensor_size),))
    owners.append(late)
    summed = jnp.concatenate(owners, axis=2)
    summed = summed.reshape(experts_local, rows, both_width)
    both_rows = gate_weight.shape[1]
    qkv_sum = qkv_sum.reshape(shard_rows, groups, -1)
    return (
        block_output,
        input_grad,
        small[expert_count + 1],
        qkv_sum[:, :, : 2 * HEAD].reshape(query_weight.shape).astype(f32),
        qkv_sum[:, :, 2 * HEAD :].astype(f32),
        out_sum.T.astype(f32),
        small[expert_count],
        small[:expert_count].T,
        summed[:, :both_rows, :hidden].astype(f32),
        summed[:, :both_rows, hidden:].astype(f32),
        summed[:, both_rows:].astype(f32),
    )


def solution(mesh):
    dp, tensor = mesh.shape["dp"], mesh.shape["tensor"]
    fine = Mesh(mesh.devices.reshape(dp // 4, 2, 2, tensor), ("z", "y", "core", "tensor"))
    rows = ("z", "y", "core")
    every = rows + ("tensor",)
    experts = P("tensor", rows, None)
    return jax.shard_map(
        functools.partial(shards, dict(fine.shape)),
        mesh=fine,
        in_specs=(
            P(every, None),
            P(rows),
            P(rows, None),
            P(),
            P(rows, "tensor"),
            P(rows, "tensor", None),
            P("tensor", rows),
            P(),
            P(),
            experts,
            experts,
            experts,
            P(every, None),
        ),
        out_specs=(
            P(every, None),
            P(every, None),
            P(),
            P(rows, "tensor"),
            P(rows, "tensor", None),
            P("tensor", rows),
            P(),
            P(),
            experts,
            experts,
            experts,
        ),
        check_vma=False,
    )
```

```python
import functools

import jax
import jax.numpy as jnp
from jax import lax
from jax.experimental import pallas as pl
from jax.experimental.pallas import tpu as pltpu
from jax.sharding import Mesh, PartitionSpec as P

CAP = 320
HEAD = 64
HALF = HEAD // 2
LANES = 2 * HEAD
BLOCK = 256
norm_eps = 1e-06
attn_scale = 0.015625
residual_scale = 0.22
rope_base = 10000.0
masked_score = -1e30
f32 = jnp.float32
bf16 = jnp.bfloat16


def row_scale(values):
    return lax.rsqrt(jnp.mean(values * values, axis=-1, keepdims=True) + norm_eps)


def contract(left, right, left_dim, right_dim):
    return lax.dot_general(
        left, right, (((left_dim,), (right_dim,)), ((), ())), preferred_element_type=f32
    )


def ein(spec, *operands):
    return jnp.einsum(spec, *operands, preferred_element_type=f32)


def norm_backward(normed_grad, source, gain):
    scale_rows = row_scale(source)
    unit_rows = source * scale_rows
    scaled_grad = normed_grad * gain
    gain_grad = jnp.sum(normed_grad * unit_rows, axis=0)
    source_grad = scale_rows * (
        scaled_grad - unit_rows * jnp.mean(scaled_grad * unit_rows, axis=-1, keepdims=True)
    )
    return (source_grad, gain_grad)


def together(*values):
    return lax.optimization_barrier(values)


def after(values, *earlier):
    return lax.optimization_barrier((values,) + earlier)[0]


def swap(values, axis):
    return lax.ppermute(values, axis, [(0, 1), (1, 0)])


def butterfly_sum(values, sizes):
    for axis, size in sizes:
        step = 1
        while step < size:
            values = values + lax.ppermute(values, axis, [(i, i ^ step) for i in range(size)])
            step *= 2
    return values


def in_order(mine, theirs, first):
    return jnp.concatenate(
        [jnp.where(first, mine, theirs), jnp.where(first, theirs, mine)], axis=0
    )


def gather_rows(rows, tensor_size):
    if tensor_size != 2:
        return lax.all_gather(rows, "tensor", axis=0, tiled=True)
    return in_order(rows, swap(rows, "tensor"), lax.axis_index("tensor") == 0)


def scatter_rows(values, tensor_size):
    if tensor_size != 2:
        return lax.psum_scatter(
            values.astype(bf16), "tensor", scatter_dimension=0, tiled=True
        ).astype(f32)
    half = values.shape[0] // 2
    me = lax.axis_index("tensor")
    give = lax.dynamic_slice_in_dim(values, (1 - me) * half, half, 0).astype(bf16)
    keep = lax.dynamic_slice_in_dim(values, me * half, half, 0)
    return keep.astype(f32) + swap(give, "tensor").astype(f32)


def gather_group(rows, tensor_size, earlier):
    if tensor_size != 2:
        own = gather_rows(rows, tensor_size)
        across = swap(own, "y")
    else:
        first = lax.axis_index("tensor") == 0
        half = rows.shape[0] // 2
        by_tensor, by_y, _ = together(swap(rows, "tensor"), swap(rows, "y"), earlier)
        own = in_order(rows, by_tensor, first)
        low, high, own_core = together(
            swap(by_y[:half], "tensor"), swap(by_tensor[half:], "y"), swap(own, "core")
        )
        corner = jnp.concatenate([low, high], axis=0)
        across = in_order(by_y, corner, first)
        return jnp.stack([own, across, own_core, swap(across, "core")])
    return jnp.stack([own, across, swap(own, "core"), swap(across, "core")])


def add(keep, given):
    return keep.astype(f32) + given.astype(f32)


def piece(near, given, sequence, which, rows):
    start = (jnp.int32(sequence), which.astype(jnp.int32) * rows, jnp.int32(0))
    shape = (1, rows, near.shape[2])
    return add(lax.dynamic_slice(near, start, shape), lax.dynamic_slice(given, start, shape))[0]


def scatter_group(near, given, tensor_size):
    if tensor_size != 2:
        own, across = add(near[0], given[0]), add(near[1], given[1])
        own = own + swap(across.astype(bf16), "y").astype(f32)
        return scatter_rows(own, tensor_size)
    me = lax.axis_index("tensor")
    rows = near.shape[1] // 2
    half = rows // 2
    take = functools.partial(piece, near, given)
    corner = take(1, 1 - me, rows).astype(bf16)
    corner, near, given = together(corner, near, given)
    take = functools.partial(piece, near, given)
    low, high = swap(corner[:half], "tensor"), swap(corner[half:], "y")
    by_tensor, by_y = take(0, 1 - me, rows), take(1, me, rows)
    first_tensor = swap(by_tensor[:half].astype(bf16), "tensor")
    first_y = swap(by_y[half:].astype(bf16), "y")
    low, high = together(low, high)
    rest_tensor = swap(add(by_tensor[half:], high).astype(bf16), "tensor")
    rest_y = swap(add(by_y[:half], low).astype(bf16), "y")
    first_tensor, first_y, rest_tensor, rest_y = together(
        first_tensor, first_y, rest_tensor, rest_y
    )
    mine = take(0, me, rows)
    return mine + add(
        jnp.concatenate([first_tensor, rest_tensor], axis=0),
        jnp.concatenate([rest_y, first_y], axis=0),
    )


def rope_lanes(values, cosine, sine, first, direction):
    lanes = values.shape[1]
    turned = jnp.where(
        first, pltpu.roll(values, lanes - HALF, 1), pltpu.roll(values, HALF, 1)
    )
    return values * cosine + direction * (turned * sine)


def lane_ids(rows):
    return lax.broadcasted_iota(jnp.int32, (rows, LANES), 1)


def attention_forward_kernel(pre_ref, cos_ref, sin_ref, mixed_ref, rot_ref, lse_ref):
    seq_len = pre_ref.shape[0]
    lane = lane_ids(seq_len)
    first = (lane & (2 * HALF - 1)) < HALF
    low = lane < HEAD
    cosine, sine = cos_ref[...], sin_ref[...]
    query = rope_lanes(pre_ref[:, :LANES], cosine, sine, first, 1.0).astype(bf16)
    kv = pre_ref[:, LANES:]
    kv = jnp.where(low, rope_lanes(kv, cosine, sine, first, 1.0), kv)
    rot_ref[:, :LANES] = query
    rot_ref[:, LANES:] = kv.astype(bf16)
    keys, values_in = head_pairs(kv, low)
    block = min(BLOCK, seq_len)
    for start in range(0, seq_len, block):
        stop = start + block
        allowed = causal(block, stop, start)
        total = jnp.zeros((block, LANES), f32)
        lses = []
        for head in (0, 1):
            scores = (
                contract(query[start:stop], keys[head][:stop], 1, 1) * attn_scale
            )
            scores = jnp.where(allowed, scores, masked_score)
            top = jnp.max(scores, axis=1, keepdims=True)
            raised = jnp.exp(scores - top)
            summed = jnp.sum(raised, axis=1, keepdims=True)
            prob = (raised * (1.0 / summed)).astype(bf16)
            total = total + jnp.dot(prob, values_in[head][:stop], preferred_element_type=f32)
            lses.append(top + jnp.log(summed))
        mixed_ref[start:stop, :] = total.astype(bf16)
        lse_ref[start:stop, :] = jnp.where(lane_ids(block) < HEAD, lses[0], lses[1])


def head_pairs(kv, low):
    kv = kv.astype(f32)
    turned = pltpu.roll(kv, HEAD, 1)
    zero = jnp.zeros_like(kv)
    keys = [jnp.where(low, kv, zero).astype(bf16), jnp.where(low, zero, turned).astype(bf16)]
    values_in = [jnp.where(low, turned, zero).astype(bf16), jnp.where(low, zero, kv).astype(bf16)]
    return keys, values_in


def causal(rows, columns, start):
    return lax.broadcasted_iota(jnp.int32, (rows, columns), 1) <= start + lax.broadcasted_iota(
        jnp.int32, (rows, columns), 0
    )


def attention_backward_kernel(
    rot_ref, grad_ref, lse_ref, cos_ref, sin_ref, out_ref, key_acc, value_acc
):
    seq_len = rot_ref.shape[0]
    lane = lane_ids(seq_len)
    first = (lane & (2 * HALF - 1)) < HALF
    low = lane < HEAD
    cosine, sine = cos_ref[...], sin_ref[...]
    keys, values_in = head_pairs(rot_ref[:, LANES:], low)
    key_acc[...] = jnp.zeros_like(key_acc)
    value_acc[...] = jnp.zeros_like(value_acc)
    block = min(BLOCK, seq_len)
    for start in range(0, seq_len, block):
        stop = start + block
        allowed = causal(block, stop, start)
        query = rot_ref[start:stop, :LANES]
        grad = grad_ref[start:stop, :]
        query_grad = jnp.zeros((block, LANES), f32)
        for head in (0, 1):
            scores = contract(query, keys[head][:stop], 1, 1) * attn_scale
            log_total = lse_ref[start:stop, head * HEAD : head * HEAD + 1]
            prob = jnp.where(allowed, jnp.exp(jnp.where(allowed, scores - log_total, 0.0)), 0.0)
            prob_grad = contract(grad, values_in[head][:stop], 1, 1)
            row_dot = jnp.sum(prob * prob_grad, axis=1, keepdims=True)
            score_grad = (prob * (prob_grad - row_dot)).astype(bf16)
            query_grad = query_grad + jnp.dot(
                score_grad, keys[head][:stop], preferred_element_type=f32
            )
            key_acc[head, :stop, :] += contract(score_grad, query, 0, 0)
            value_acc[head, :stop, :] += contract(prob.astype(bf16), grad, 0, 0)
        lane_block = (lane_ids(block) & (2 * HALF - 1)) < HALF
        out_ref[start:stop, :LANES] = rope_lanes(
            query_grad * attn_scale, cosine[start:stop], sine[start:stop], lane_block, -1.0
        ).astype(bf16)
    key_grad = (key_acc[0] + pltpu.roll(key_acc[1], HEAD, 1)) * attn_scale
    key_grad = rope_lanes(jnp.where(low, key_grad, 0.0), cosine, sine, first, -1.0)
    value_grad = pltpu.roll(value_acc[0], HEAD, 1) + value_acc[1]
    out_ref[:, LANES:] = jnp.where(low, key_grad, value_grad).astype(bf16)


def by_head(width):
    return lambda seq_len: pl.BlockSpec((seq_len, width), lambda g: (0, g))


def attention_forward(pre, cosine, sine):
    seq_len, width = pre.shape
    groups = width // (2 * LANES)
    whole = pl.BlockSpec((seq_len, LANES), lambda g: (0, 0))
    wide, narrow = by_head(2 * LANES)(seq_len), by_head(LANES)(seq_len)
    return pl.pallas_call(
        attention_forward_kernel,
        grid=(groups,),
        in_specs=[wide, whole, whole],
        out_specs=[narrow, wide, narrow],
        out_shape=[
            jax.ShapeDtypeStruct((seq_len, width // 2), bf16),
            jax.ShapeDtypeStruct((seq_len, width), bf16),
            jax.ShapeDtypeStruct((seq_len, width // 2), f32),
        ],
        cost_estimate=pl.CostEstimate(
            flops=6 * groups * seq_len * seq_len * LANES,
            bytes_accessed=10 * seq_len * width,
            transcendentals=groups * seq_len * seq_len,
        ),
        name="attention_forward",
    )(pre, cosine, sine)


def attention_backward(rot, grad, lse, cosine, sine):
    seq_len, width = rot.shape
    groups = width // (2 * LANES)
    whole = pl.BlockSpec((seq_len, LANES), lambda g: (0, 0))
    wide, narrow = by_head(2 * LANES)(seq_len), by_head(LANES)(seq_len)
    return pl.pallas_call(
        attention_backward_kernel,
        grid=(groups,),
        in_specs=[wide, narrow, narrow, whole, whole],
        out_specs=wide,
        out_shape=jax.ShapeDtypeStruct((seq_len, width), bf16),
        scratch_shapes=[pltpu.VMEM((2, seq_len, LANES), f32)] * 2,
        cost_estimate=pl.CostEstimate(
            flops=16 * groups * seq_len * seq_len * LANES,
            bytes_accessed=10 * seq_len * width,
            transcendentals=groups * seq_len * seq_len,
        ),
        name="attention_backward",
    )(rot, grad, lse, cosine, sine)


def expert_kernel(
    carried, shared, last, member_ref, tokens_ref, grad_ref, code_ref, gate_ref, weight_ref, *refs
):
    if carried:
        moe_in, normed_in, *refs = refs
    if shared:
        refs = refs[1:]
    *sum_refs, pair_ref, part_ref, both, down, both_acc, down_acc = refs
    step = pl.program_id(0)

    def put(place, values):
        if not last:
            sum_refs[place][0] = values
            return

        sum_refs[2 * place][0] = values
        sum_refs[2 * place + 1][0] = values
    shards_z, members, rows = weight_ref.shape[0], weight_ref.shape[2], weight_ref.shape[3]
    hidden = down.shape[0]
    both_rows = both.shape[0] // (shards_z * members)
    down_rows = hidden // (shards_z * members)

    def places():
        for z in range(shards_z):
            for rel in range(members):
                at = z * members + (member_ref[0] ^ rel)
                yield (
                    z,
                    rel,
                    pl.ds(pl.multiple_of(at * both_rows, both_rows), both_rows),
                    pl.ds(pl.multiple_of(at * down_rows, down_rows), down_rows),
                )

    @pl.when(step == 0)
    def _():
        for z, rel, both_at, down_at in places():
            both[both_at, :] = weight_ref[z, 0, rel, :both_rows, :]
            down[down_at, :] = weight_ref[z, 0, rel, both_rows:, :]
        both_acc[...] = jnp.zeros_like(both_acc)
        down_acc[...] = jnp.zeros_like(down_acc)

    seq_len = tokens_ref.shape[1]
    slot = lax.broadcasted_iota(jnp.int32, (CAP, seq_len), 0)
    match = code_ref[0] == slot
    dispatch = jnp.where(match, 1.0, 0.0).astype(bf16)
    slot_gate = jnp.sum(jnp.where(match, gate_ref[0], 0.0), axis=1, keepdims=True)
    expert_in = jnp.dot(dispatch, tokens_ref[0], preferred_element_type=f32).astype(bf16)
    gate_pre = jnp.dot(expert_in, both[:, :hidden], preferred_element_type=f32)
    up_pre = jnp.dot(expert_in, both[:, hidden:], preferred_element_type=f32)
    sigmoid = 1.0 / (1.0 + jnp.exp(-gate_pre))
    silu = gate_pre * sigmoid
    hidden_act = (silu * up_pre).astype(bf16)
    expert_out = jnp.dot(hidden_act, down[...], preferred_element_type=f32)
    weighted = (slot_gate * expert_out).astype(bf16)
    moe = contract(dispatch, weighted, 0, 0)
    if carried:
        moe = moe + moe_in[0].astype(f32)
    put(0, moe.astype(bf16))

    slot_grad = jnp.dot(dispatch, grad_ref[0], preferred_element_type=f32)
    raw_grad = contract(slot_grad.astype(bf16), down[...], 1, 1)
    slot_gate_grad = jnp.sum(hidden_act.astype(f32) * raw_grad, axis=1, keepdims=True)
    pair_ref[0] = jnp.sum(jnp.where(match, slot_gate_grad, 0.0), axis=0, keepdims=True)
    hidden_grad = slot_gate * raw_grad
    gate_grad = (
        hidden_grad * up_pre * sigmoid * (1.0 + gate_pre * (1.0 - sigmoid))
    ).astype(bf16)
    up_grad = (hidden_grad * silu).astype(bf16)
    down_acc[...] += contract(hidden_act, (slot_gate * slot_grad).astype(bf16), 0, 0)
    both_acc[:, :hidden] += contract(expert_in, gate_grad, 0, 0)
    both_acc[:, hidden:] += contract(expert_in, up_grad, 0, 0)
    in_grad = (
        contract(gate_grad, both[:, :hidden], 1, 1) + contract(up_grad, both[:, hidden:], 1, 1)
    ).astype(bf16)
    normed = contract(dispatch, in_grad, 0, 0)
    if carried:
        normed = normed + normed_in[0].astype(f32)
    put(1, normed.astype(bf16))

    @pl.when(step == pl.num_programs(0) - 1)
    def _():
        for z, rel, both_at, down_at in places():
            part_ref[z, 0, rel, :both_rows, :] = both_acc[both_at, :].astype(bf16)
            part_ref[z, 0, rel, both_rows:, :] = down_acc[down_at, :].astype(bf16)


def run_expert(
    member, tokens, grads, code, gate, weight, source, bunch, place, last, carry, shared
):
    sequences, seq_len, width = tokens.shape
    shards_z, held, members, rows, both_width = weight.shape
    hidden = both_width // 2
    per_seq = pl.BlockSpec((1, seq_len, width), lambda s: (s, 0, 0))
    per_row = pl.BlockSpec((1, 1, seq_len), lambda s: (s, 0, 0))
    one = (shards_z, 1, members, rows, both_width)
    every = pl.BlockSpec(one, lambda s: (0, source, 0, 0, 0), pipeline_mode=pl.Buffered(1))
    part = pl.BlockSpec(one, lambda s: (0, place, 0, 0, 0))
    slots = sequences * CAP
    if last:
        near = pl.BlockSpec((1, seq_len, width), lambda s: (jnp.minimum(s, 2), 0, 0))
        far = pl.BlockSpec((1, seq_len, width), lambda s: (jnp.maximum(s - 2, 0), 0, 0))
        sums = [near, far, near, far]
        sum_shapes = [
            jax.ShapeDtypeStruct((count, seq_len, width), bf16) for count in (3, 2, 3, 2)
        ]
    else:
        sums, sum_shapes = [per_seq] * 2, [jax.ShapeDtypeStruct(tokens.shape, bf16)] * 2
    return pl.pallas_call(
        functools.partial(expert_kernel, bool(carry), bool(shared), last),
        grid=(sequences,),
        in_specs=[
            pl.BlockSpec(memory_space=pltpu.SMEM),
            per_seq,
            per_seq,
            per_row,
            per_row,
            every,
        ]
        + [per_seq] * len(carry)
        + [pl.BlockSpec(memory_space=pl.ANY)] * len(shared),
        out_specs=sums + [per_row, part],
        out_shape=sum_shapes
        + [
            jax.ShapeDtypeStruct((sequences, 1, seq_len), f32),
            jax.ShapeDtypeStruct((shards_z, bunch, members, rows, both_width), bf16),
        ],
        scratch_shapes=[
            pltpu.VMEM((width, both_width), bf16),
            pltpu.VMEM((hidden, width), bf16),
            pltpu.VMEM((width, both_width), f32),
            pltpu.VMEM((hidden, width), f32),
        ],
        compiler_params=pltpu.CompilerParams(vmem_limit_bytes=66_000_000),
        cost_estimate=pl.CostEstimate(
            flops=2 * slots * width * (4 * seq_len + 9 * hidden),
            bytes_accessed=12 * sequences * seq_len * width + 4 * (weight.size // held),
            transcendentals=slots * hidden,
        ),
        name="expert",
        input_output_aliases={6 + len(carry): len(sums) + 1} if shared else {},
    )(member, tokens, grads, code, gate, weight, *carry, *shared)


def shards(
    sizes,
    block_input,
    positions,
    expert_ids,
    attn_gain,
    query_weight,
    kv_weight,
    out_weight,
    ffn_gain,
    router_weight,
    gate_weight,
    up_weight,
    down_weight,
    out_grad,
):
    tensor_size, z_size = sizes["tensor"], sizes["z"]
    seq_len = positions.shape[0]
    width = block_input.shape[1]
    shard_rows, groups = kv_weight.shape[:2]
    q_width = query_weight.shape[1]
    wide = 2 * q_width
    expert_count = router_weight.shape[1]
    experts_local = gate_weight.shape[0]
    owned = experts_local // 4
    hidden = gate_weight.shape[2]
    my_z, my_y, my_core = lax.axis_index("z"), lax.axis_index("y"), lax.axis_index("core")
    my_tensor = lax.axis_index("tensor")
    y_first, core_first, tensor_first = my_y == 0, my_core == 0, my_tensor == 0

    def at(values, index):
        return lax.dynamic_index_in_dim(values, index, 0, keepdims=False)

    def stacked(mine, theirs, is_first, axis=1):
        ordered = [jnp.where(is_first, mine, theirs), jnp.where(is_first, theirs, mine)]
        return jnp.stack(ordered, axis)

    packed = jnp.concatenate(
        [
            jnp.concatenate([query_weight.reshape(shard_rows, groups, -1), kv_weight], axis=2)
            .reshape(shard_rows, wide),
            out_weight.T,
        ],
        axis=1,
    )
    packed_full = lax.all_gather(packed, ("z", "y", "core"), axis=0, tiled=True)

    input_rows = block_input.astype(f32)
    attn_normed = (input_rows * row_scale(input_rows) * attn_gain).astype(bf16)
    attn_tokens = gather_rows(attn_normed, tensor_size)
    grad_rows = out_grad.astype(f32)
    moe_rows = after((residual_scale * grad_rows).astype(bf16), attn_tokens)

    experts = jnp.concatenate(
        [jnp.concatenate([gate_weight, up_weight], axis=2), down_weight], axis=1
    )
    rows, both_width = experts.shape[1:]
    grouped = experts.reshape(2, 2, owned, rows, both_width)
    own_y, give_y = at(grouped, my_y), at(grouped, 1 - my_y)
    from_y = swap(give_y, "y")
    members = jnp.stack(
        [
            at(own_y, my_core),
            swap(at(own_y, 1 - my_core), "core"),
            at(from_y, my_core),
            swap(at(from_y, 1 - my_core), "core"),
        ],
        axis=1,
    )
    moe_own = gather_rows(moe_rows, tensor_size)

    ids_t = expert_ids.T
    hits = jnp.zeros((expert_count, seq_len), jnp.bool_)
    for k in range(ids_t.shape[0]):
        hits = hits | (ids_t[k][None, :] == jnp.arange(expert_count)[:, None])
    token_ids = jnp.arange(seq_len)
    earlier = (token_ids[:, None] < token_ids[None, :]).astype(bf16)
    rank = jnp.dot(hits.astype(bf16), earlier, preferred_element_type=f32)
    code = jnp.where(hits, jnp.where(rank < CAP, rank, -1.0), -2.0)

    half_dim = HEAD // 2
    frequency = rope_base ** (-(jnp.arange(half_dim, dtype=f32) * 2.0 / HEAD))
    angles = positions.astype(f32)[:, None] * frequency[None, :]
    cosine = jnp.tile(jnp.cos(angles), (1, 4))
    sine = jnp.tile(jnp.concatenate([-jnp.sin(angles), jnp.sin(angles)], axis=1), (1, 2))

    packed_full, attn_tokens, moe_own, members, code, cosine, sine = together(
        packed_full, attn_tokens, moe_own, members, code, cosine, sine
    )
    qkv_full, out_full = packed_full[:, :wide], packed_full[:, wide:]
    bunch = min(2, owned)
    weights, launched = [], None
    for start, stop in [(0, bunch)] + [(e, e + 1) for e in range(bunch, owned)]:
        item = members[start:stop]
        if launched is not None:
            item = after(item, launched)
        launched = item
        item = lax.all_gather(item, "z", axis=0, tiled=False)
        weights += [(item, e) for e in range(stop - start)]

    qkv_pre = jnp.dot(attn_tokens, qkv_full, preferred_element_type=f32)
    qkv_pre, moe_own, code_y = together(qkv_pre, moe_own, swap(code, "y"))
    moe_across = swap(moe_own, "y")
    attn_mixed, qkv_rot, log_totals = attention_forward(qkv_pre, cosine, sine)
    attn_out = scatter_rows(contract(attn_mixed, out_full, 1, 1), tensor_size)
    codes = jnp.stack([code, code_y, swap(code, "core"), swap(code_y, "core")])
    attn_out, moe_across, codes = together(attn_out, moe_across, codes)
    moe_grad = jnp.stack([moe_own, moe_across, swap(moe_own, "core"), swap(moe_across, "core")])
    hidden_state = input_rows + residual_scale * attn_out
    ffn_normed = (hidden_state * row_scale(hidden_state) * ffn_gain).astype(bf16)

    tokens = gather_group(ffn_normed, tensor_size, moe_grad)
    logits = ein("dx,std->sxt", router_weight, tokens)
    chosen = codes > -1.5
    top_logit = jnp.max(jnp.where(chosen, logits, -jnp.inf), axis=1, keepdims=True)
    raised = jnp.where(chosen, jnp.exp(jnp.where(chosen, logits - top_logit, 0.0)), 0.0)
    gates = raised / jnp.sum(raised, axis=1, keepdims=True)
    member = my_y * 2 + my_core
    expert_first = my_tensor * experts_local + member * owned
    code_own = lax.dynamic_slice_in_dim(codes, expert_first, owned, 1).astype(jnp.int32)
    gate_own = lax.dynamic_slice_in_dim(gates, expert_first, owned, 1)

    carry, pairs, parts, shared = (), [], [], ()
    for e in range(owned):
        *carry, pair, part = run_expert(
            member.reshape(1).astype(jnp.int32),
            tokens,
            moe_grad,
            code_own[:, e : e + 1],
            gate_own[:, e : e + 1],
            *weights[e],
            bunch,
            e % bunch,
            e + 1 == owned,
            carry,
            shared,
        )
        pairs.append(pair)
        shared = (part,)
        if (e + 1) % bunch == 0:
            parts.append(lax.psum_scatter(part, "z", scatter_dimension=0, tiled=False))
            shared = ()
    moe_near, moe_give, normed_near, normed_give = carry

    pair_grad = jnp.concatenate(pairs, axis=1)
    pair_given = swap(pair_grad[2:], "core")
    normed_give = after(normed_give, pair_given)
    pair_core = stacked(pair_grad[:2], pair_given, core_first)
    pair_y = in_order(pair_core[0], swap(pair_core[1], "y"), y_first)
    pair_y = pair_y.reshape(experts_local, seq_len)
    if tensor_size == 2:
        local = seq_len // 2
        give = lax.dynamic_slice_in_dim(pair_y, (1 - my_tensor) * local, local, 1)
        keep = lax.dynamic_slice_in_dim(pair_y, my_tensor * local, local, 1)
        pair_all = in_order(keep, swap(give, "tensor"), tensor_first)
    else:
        local = seq_len // tensor_size
        pair_all = lax.all_gather(pair_y, "tensor", axis=0, tiled=True)
        pair_all = lax.dynamic_slice_in_dim(pair_all, my_tensor * local, local, 1)
    normed_given, pair_all = together(swap(normed_give, "core"), pair_all)
    normed_local = scatter_group(normed_near, normed_given, tensor_size)

    def core_owners(part):
        part = jnp.moveaxis(part.reshape(bunch, 2, 2, rows, both_width), 2, 0)
        return stacked(part[0], swap(part[1], "core"), core_first, 0)

    def y_owners(part):
        keep, give = part[:, :, 0], part[:, :, 1]
        return stacked(keep, swap(give, "y"), y_first, 0)

    early = parts[:-1]
    moe_given = swap(after(moe_give, normed_given), "core")
    normed_local, moe_given = together(normed_local, moe_given)
    gates_local = lax.dynamic_slice_in_dim(gates[0], my_tensor * local, local, 1)
    gate_dot = jnp.sum(gates_local * pair_all, axis=0, keepdims=True)
    logit_low = (gates_local * (pair_all - gate_dot)).astype(bf16)

    normed_local = normed_local + contract(logit_low, router_weight, 0, 1)
    router_part = jnp.dot(logit_low, ffn_normed, preferred_element_type=f32)
    state_grad, ffn_gain_part = norm_backward(normed_local, hidden_state, ffn_gain)
    state_grad = state_grad + grad_rows
    attn_grad_all = gather_rows((residual_scale * state_grad).astype(bf16), tensor_size)
    if tensor_size == 2:
        local = seq_len // 2
        moe_piece = functools.partial(piece, moe_near, moe_given)
        moe_far = moe_piece(1, 1 - my_tensor, local).astype(bf16)
        moe_far, moe_given = together(moe_far, moe_given)
        moe_piece = functools.partial(piece, moe_near, moe_given)
        moe_own_far = moe_piece(1, my_tensor, local).astype(bf16)
    else:
        moe_far = add(moe_near[1], moe_given[1]).astype(bf16)
        moe_own_far = jnp.zeros((1, width), bf16)
    attn_grad_all, moe_far, moe_own_far = together(
        attn_grad_all, swap(moe_far, "y"), moe_own_far
    )
    early = [core_owners(after(part, attn_grad_all)) for part in early]
    moe_own_far = swap(moe_own_far, "y")

    def halves(part, mine):
        return at(part, mine), at(part, 1 - mine).astype(bf16)

    def by_dp(part):
        return part.reshape(z_size, 2, 2, shard_rows, part.shape[1])

    mixed_grad = jnp.dot(attn_grad_all, out_full, preferred_element_type=f32).astype(bf16)
    qkv_pre_grad = attention_backward(qkv_rot, mixed_grad, log_totals, cosine, sine)
    qkv_pre_grad, moe_own_far, *early = together(qkv_pre_grad, moe_own_far, *early)

    attn_part = contract(qkv_pre_grad, qkv_full, 1, 1)
    attn_scattered = scatter_rows(attn_part, tensor_size)
    tokens_late, grads_late, _ = together(attn_tokens, attn_grad_all, attn_part)
    qkv_part = contract(tokens_late, qkv_pre_grad, 0, 0)
    qkv_keep, qkv_give = halves(jnp.moveaxis(by_dp(qkv_part), 2, 0), my_core)
    out_part = contract(grads_late, attn_mixed, 0, 0)
    out_keep, out_give = halves(jnp.moveaxis(by_dp(out_part), 2, 0), my_core)
    attn_normed_grad, qkv_given, out_given, *owners = together(
        attn_scattered,
        swap(qkv_give, "core"),
        swap(out_give, "core"),
        *[y_owners(after(part, qkv_pre_grad)) for part in early],
    )
    input_part, attn_gain_part = norm_backward(attn_normed_grad, input_rows, attn_gain)
    input_grad = (state_grad + input_part).astype(bf16)
    small = jnp.concatenate(
        [router_part, ffn_gain_part[None, :], attn_gain_part[None, :]], axis=0
    )
    if tensor_size == 2:
        moe_sum = add(moe_piece(0, my_tensor, local), moe_own_far)
        moe_given = swap(
            add(moe_piece(0, 1 - my_tensor, local), moe_far).astype(bf16), "tensor"
        )
    else:
        moe_sum = jnp.zeros((local, width), f32)
        moe_given = scatter_rows(add(add(moe_near[0], moe_given[0]), moe_far), tensor_size)
    qkv_keep, qkv_give = halves(jnp.moveaxis(add(qkv_keep, qkv_given), 1, 0), my_y)
    out_keep, out_give = halves(jnp.moveaxis(add(out_keep, out_given), 1, 0), my_y)
    small = butterfly_sum(small, (("core", 2), ("tensor", tensor_size)))
    small, qkv_given, out_given, moe_given = together(
        small, swap(qkv_give, "y"), swap(out_give, "y"), moe_given
    )
    late = core_owners(after(parts[-1], small))
    dp_sum = jnp.concatenate([add(qkv_keep, qkv_given), add(out_keep, out_given)], axis=-1)

    def z_pairs(step):
        return [(i, i ^ step) for i in range(z_size)]

    def z_halve(part, step):
        part = jnp.moveaxis(part.reshape(-1, 2, shard_rows, part.shape[-1]), 1, 0)
        keep, give = halves(part, (my_z // step) % 2)
        return add(keep, lax.ppermute(give, "z", z_pairs(step)))

    small = butterfly_sum(small, (("y", 2),))
    step = 1
    while step < z_size:
        if 2 * step == z_size:
            dp_sum, small, late = together(dp_sum, small, late)
        dp_sum = z_halve(dp_sum, step)
        small = small + lax.ppermute(small, "z", z_pairs(step))
        step *= 2
    dp_sum = dp_sum.reshape(shard_rows, dp_sum.shape[-1])
    late = y_owners(late)
    qkv_sum, out_sum = dp_sum[:, :wide], dp_sum[:, wide:]
    block_output = (hidden_state + residual_scale * add(moe_sum, moe_given)).astype(bf16)
    owners.append(late)
    summed = jnp.concatenate(owners, axis=2)
    summed = summed.reshape(experts_local, rows, both_width)
    both_rows = gate_weight.shape[1]
    qkv_sum = qkv_sum.reshape(shard_rows, groups, -1)
    return (
        block_output,
        input_grad,
        small[expert_count + 1],
        qkv_sum[:, :, : 2 * HEAD].reshape(query_weight.shape).astype(f32),
        qkv_sum[:, :, 2 * HEAD :].astype(f32),
        out_sum.T.astype(f32),
        small[expert_count],
        small[:expert_count].T,
        summed[:, :both_rows, :hidden].astype(f32),
        summed[:, :both_rows, hidden:].astype(f32),
        summed[:, both_rows:].astype(f32),
    )


def solution(mesh):
    dp, tensor = mesh.shape["dp"], mesh.shape["tensor"]
    fine = Mesh(mesh.devices.reshape(dp // 4, 2, 2, tensor), ("z", "y", "core", "tensor"))
    rows = ("z", "y", "core")
    every = rows + ("tensor",)
    experts = P("tensor", rows, None)
    return jax.shard_map(
        functools.partial(shards, dict(fine.shape)),
        mesh=fine,
        in_specs=(
            P(every, None),
            P(rows),
            P(rows, None),
            P(),
            P(rows, "tensor"),
            P(rows, "tensor", None),
            P("tensor", rows),
            P(),
            P(),
            experts,
            experts,
            experts,
            P(every, None),
        ),
        out_specs=(
            P(every, None),
            P(every, None),
            P(),
            P(rows, "tensor"),
            P(rows, "tensor", None),
            P("tensor", rows),
            P(),
            P(),
            experts,
            experts,
            experts,
        ),
        check_vma=False,
    )
```

```python
import functools

import jax
import jax.numpy as jnp
from jax import lax
from jax.experimental import pallas as pl
from jax.experimental.pallas import tpu as pltpu
from jax.sharding import Mesh, PartitionSpec as P

CAP = 320
HEAD = 64
HALF = HEAD // 2
LANES = 2 * HEAD
BLOCK = 256
norm_eps = 1e-06
attn_scale = 0.015625
residual_scale = 0.22
rope_base = 10000.0
masked_score = -1e30
f32 = jnp.float32
bf16 = jnp.bfloat16


def row_scale(values):
    return lax.rsqrt(jnp.mean(values * values, axis=-1, keepdims=True) + norm_eps)


def contract(left, right, left_dim, right_dim):
    return lax.dot_general(
        left, right, (((left_dim,), (right_dim,)), ((), ())), preferred_element_type=f32
    )


def ein(spec, *operands):
    return jnp.einsum(spec, *operands, preferred_element_type=f32)


def norm_backward(normed_grad, source, gain):
    scale_rows = row_scale(source)
    unit_rows = source * scale_rows
    scaled_grad = normed_grad * gain
    gain_grad = jnp.sum(normed_grad * unit_rows, axis=0)
    source_grad = scale_rows * (
        scaled_grad - unit_rows * jnp.mean(scaled_grad * unit_rows, axis=-1, keepdims=True)
    )
    return (source_grad, gain_grad)


def together(*values):
    return lax.optimization_barrier(values)


def after(values, *earlier):
    return lax.optimization_barrier((values,) + earlier)[0]


def swap(values, axis):
    return lax.ppermute(values, axis, [(0, 1), (1, 0)])


def butterfly_sum(values, sizes):
    for axis, size in sizes:
        step = 1
        while step < size:
            values = values + lax.ppermute(values, axis, [(i, i ^ step) for i in range(size)])
            step *= 2
    return values


def in_order(mine, theirs, first):
    return jnp.concatenate(
        [jnp.where(first, mine, theirs), jnp.where(first, theirs, mine)], axis=0
    )


def gather_rows(rows, tensor_size):
    if tensor_size != 2:
        return lax.all_gather(rows, "tensor", axis=0, tiled=True)
    return in_order(rows, swap(rows, "tensor"), lax.axis_index("tensor") == 0)


def scatter_rows(values, tensor_size):
    if tensor_size != 2:
        return lax.psum_scatter(
            values.astype(bf16), "tensor", scatter_dimension=0, tiled=True
        ).astype(f32)
    half = values.shape[0] // 2
    me = lax.axis_index("tensor")
    give = lax.dynamic_slice_in_dim(values, (1 - me) * half, half, 0).astype(bf16)
    keep = lax.dynamic_slice_in_dim(values, me * half, half, 0)
    return keep.astype(f32) + swap(give, "tensor").astype(f32)


def gather_group(rows, tensor_size, earlier):
    if tensor_size != 2:
        own = gather_rows(rows, tensor_size)
        across = swap(own, "y")
    else:
        first = lax.axis_index("tensor") == 0
        half = rows.shape[0] // 2
        by_tensor, by_y, _ = together(swap(rows, "tensor"), swap(rows, "y"), earlier)
        own = in_order(rows, by_tensor, first)
        low, high, own_core = together(
            swap(by_y[:half], "tensor"), swap(by_tensor[half:], "y"), swap(own, "core")
        )
        corner = jnp.concatenate([low, high], axis=0)
        across = in_order(by_y, corner, first)
        return jnp.stack([own, across, own_core, swap(across, "core")])
    return jnp.stack([own, across, swap(own, "core"), swap(across, "core")])


def add(keep, given):
    return keep.astype(f32) + given.astype(f32)


def piece(near, given, sequence, which, rows):
    start = (jnp.int32(sequence), which.astype(jnp.int32) * rows, jnp.int32(0))
    shape = (1, rows, near.shape[2])
    return add(lax.dynamic_slice(near, start, shape), lax.dynamic_slice(given, start, shape))[0]


def scatter_group(near, given, tensor_size):
    if tensor_size != 2:
        own, across = add(near[0], given[0]), add(near[1], given[1])
        own = own + swap(across.astype(bf16), "y").astype(f32)
        return scatter_rows(own, tensor_size)
    me = lax.axis_index("tensor")
    rows = near.shape[1] // 2
    half = rows // 2
    take = functools.partial(piece, near, given)
    corner = take(1, 1 - me, rows).astype(bf16)
    corner, near, given = together(corner, near, given)
    take = functools.partial(piece, near, given)
    low, high = swap(corner[:half], "tensor"), swap(corner[half:], "y")
    by_tensor, by_y = take(0, 1 - me, rows), take(1, me, rows)
    first_tensor = swap(by_tensor[:half].astype(bf16), "tensor")
    first_y = swap(by_y[half:].astype(bf16), "y")
    low, high = together(low, high)
    rest_tensor = swap(add(by_tensor[half:], high).astype(bf16), "tensor")
    rest_y = swap(add(by_y[:half], low).astype(bf16), "y")
    first_tensor, first_y, rest_tensor, rest_y = together(
        first_tensor, first_y, rest_tensor, rest_y
    )
    mine = take(0, me, rows)
    return mine + add(
        jnp.concatenate([first_tensor, rest_tensor], axis=0),
        jnp.concatenate([rest_y, first_y], axis=0),
    )


def rope_lanes(values, cosine, sine, first, direction):
    lanes = values.shape[1]
    turned = jnp.where(
        first, pltpu.roll(values, lanes - HALF, 1), pltpu.roll(values, HALF, 1)
    )
    return values * cosine + direction * (turned * sine)


def lane_ids(rows):
    return lax.broadcasted_iota(jnp.int32, (rows, LANES), 1)


def attention_forward_kernel(pre_ref, cos_ref, sin_ref, mixed_ref, rot_ref, lse_ref):
    seq_len = pre_ref.shape[0]
    lane = lane_ids(seq_len)
    first = (lane & (2 * HALF - 1)) < HALF
    low = lane < HEAD
    cosine, sine = cos_ref[...], sin_ref[...]
    query = rope_lanes(pre_ref[:, :LANES], cosine, sine, first, 1.0).astype(bf16)
    kv = pre_ref[:, LANES:]
    kv = jnp.where(low, rope_lanes(kv, cosine, sine, first, 1.0), kv)
    rot_ref[:, :LANES] = query
    rot_ref[:, LANES:] = kv.astype(bf16)
    keys, values_in = head_pairs(kv, low)
    block = min(BLOCK, seq_len)
    for start in range(0, seq_len, block):
        stop = start + block
        allowed = causal(block, stop, start)
        total = jnp.zeros((block, LANES), f32)
        lses = []
        for head in (0, 1):
            scores = (
                contract(query[start:stop], keys[head][:stop], 1, 1) * attn_scale
            )
            scores = jnp.where(allowed, scores, masked_score)
            top = jnp.max(scores, axis=1, keepdims=True)
            raised = jnp.exp(scores - top)
            summed = jnp.sum(raised, axis=1, keepdims=True)
            prob = (raised * (1.0 / summed)).astype(bf16)
            total = total + jnp.dot(prob, values_in[head][:stop], preferred_element_type=f32)
            lses.append(top + jnp.log(summed))
        mixed_ref[start:stop, :] = total.astype(bf16)
        lse_ref[start:stop, :] = jnp.where(lane_ids(block) < HEAD, lses[0], lses[1])


def head_pairs(kv, low):
    kv = kv.astype(f32)
    turned = pltpu.roll(kv, HEAD, 1)
    zero = jnp.zeros_like(kv)
    keys = [jnp.where(low, kv, zero).astype(bf16), jnp.where(low, zero, turned).astype(bf16)]
    values_in = [jnp.where(low, turned, zero).astype(bf16), jnp.where(low, zero, kv).astype(bf16)]
    return keys, values_in


def causal(rows, columns, start):
    return lax.broadcasted_iota(jnp.int32, (rows, columns), 1) <= start + lax.broadcasted_iota(
        jnp.int32, (rows, columns), 0
    )


def attention_backward_kernel(
    rot_ref, grad_ref, lse_ref, cos_ref, sin_ref, out_ref, key_acc, value_acc
):
    seq_len = rot_ref.shape[0]
    lane = lane_ids(seq_len)
    first = (lane & (2 * HALF - 1)) < HALF
    low = lane < HEAD
    cosine, sine = cos_ref[...], sin_ref[...]
    keys, values_in = head_pairs(rot_ref[:, LANES:], low)
    key_acc[...] = jnp.zeros_like(key_acc)
    value_acc[...] = jnp.zeros_like(value_acc)
    block = min(BLOCK, seq_len)
    for start in range(0, seq_len, block):
        stop = start + block
        allowed = causal(block, stop, start)
        query = rot_ref[start:stop, :LANES]
        grad = grad_ref[start:stop, :]
        query_grad = jnp.zeros((block, LANES), f32)
        for head in (0, 1):
            scores = contract(query, keys[head][:stop], 1, 1) * attn_scale
            log_total = lse_ref[start:stop, head * HEAD : head * HEAD + 1]
            prob = jnp.where(allowed, jnp.exp(jnp.where(allowed, scores - log_total, 0.0)), 0.0)
            prob_grad = contract(grad, values_in[head][:stop], 1, 1)
            row_dot = jnp.sum(prob * prob_grad, axis=1, keepdims=True)
            score_grad = (prob * (prob_grad - row_dot)).astype(bf16)
            query_grad = query_grad + jnp.dot(
                score_grad, keys[head][:stop], preferred_element_type=f32
            )
            key_acc[head, :stop, :] += contract(score_grad, query, 0, 0)
            value_acc[head, :stop, :] += contract(prob.astype(bf16), grad, 0, 0)
        lane_block = (lane_ids(block) & (2 * HALF - 1)) < HALF
        out_ref[start:stop, :LANES] = rope_lanes(
            query_grad * attn_scale, cosine[start:stop], sine[start:stop], lane_block, -1.0
        ).astype(bf16)
    key_grad = (key_acc[0] + pltpu.roll(key_acc[1], HEAD, 1)) * attn_scale
    key_grad = rope_lanes(jnp.where(low, key_grad, 0.0), cosine, sine, first, -1.0)
    value_grad = pltpu.roll(value_acc[0], HEAD, 1) + value_acc[1]
    out_ref[:, LANES:] = jnp.where(low, key_grad, value_grad).astype(bf16)


def by_head(width):
    return lambda seq_len: pl.BlockSpec((seq_len, width), lambda g: (0, g))


def attention_forward(pre, cosine, sine):
    seq_len, width = pre.shape
    groups = width // (2 * LANES)
    whole = pl.BlockSpec((seq_len, LANES), lambda g: (0, 0))
    wide, narrow = by_head(2 * LANES)(seq_len), by_head(LANES)(seq_len)
    return pl.pallas_call(
        attention_forward_kernel,
        grid=(groups,),
        in_specs=[wide, whole, whole],
        out_specs=[narrow, wide, narrow],
        out_shape=[
            jax.ShapeDtypeStruct((seq_len, width // 2), bf16),
            jax.ShapeDtypeStruct((seq_len, width), bf16),
            jax.ShapeDtypeStruct((seq_len, width // 2), f32),
        ],
        cost_estimate=pl.CostEstimate(
            flops=6 * groups * seq_len * seq_len * LANES,
            bytes_accessed=10 * seq_len * width,
            transcendentals=groups * seq_len * seq_len,
        ),
        name="attention_forward",
    )(pre, cosine, sine)


def attention_backward(rot, grad, lse, cosine, sine):
    seq_len, width = rot.shape
    groups = width // (2 * LANES)
    whole = pl.BlockSpec((seq_len, LANES), lambda g: (0, 0))
    wide, narrow = by_head(2 * LANES)(seq_len), by_head(LANES)(seq_len)
    return pl.pallas_call(
        attention_backward_kernel,
        grid=(groups,),
        in_specs=[wide, narrow, narrow, whole, whole],
        out_specs=wide,
        out_shape=jax.ShapeDtypeStruct((seq_len, width), bf16),
        scratch_shapes=[pltpu.VMEM((2, seq_len, LANES), f32)] * 2,
        cost_estimate=pl.CostEstimate(
            flops=16 * groups * seq_len * seq_len * LANES,
            bytes_accessed=10 * seq_len * width,
            transcendentals=groups * seq_len * seq_len,
        ),
        name="attention_backward",
    )(rot, grad, lse, cosine, sine)


def expert_kernel(
    carried, shared, last, member_ref, tokens_ref, grad_ref, code_ref, gate_ref, weight_ref, *refs
):
    if carried:
        moe_in, normed_in, *refs = refs
    if shared:
        refs = refs[1:]
    *sum_refs, pair_ref, part_ref, both, down, both_acc, down_acc = refs
    step = pl.program_id(0)

    def put(place, values):
        if not last:
            sum_refs[place][0] = values
            return

        sum_refs[2 * place][0] = values
        sum_refs[2 * place + 1][0] = values
    shards_z, members, rows = weight_ref.shape[0], weight_ref.shape[2], weight_ref.shape[3]
    hidden = down.shape[0]
    both_rows = both.shape[0] // (shards_z * members)
    down_rows = hidden // (shards_z * members)

    def places():
        for z in range(shards_z):
            for rel in range(members):
                at = z * members + (member_ref[0] ^ rel)
                yield (
                    z,
                    rel,
                    pl.ds(pl.multiple_of(at * both_rows, both_rows), both_rows),
                    pl.ds(pl.multiple_of(at * down_rows, down_rows), down_rows),
                )

    @pl.when(step == 0)
    def _():
        for z, rel, both_at, down_at in places():
            both[both_at, :] = weight_ref[z, 0, rel, :both_rows, :]
            down[down_at, :] = weight_ref[z, 0, rel, both_rows:, :]
        both_acc[...] = jnp.zeros_like(both_acc)
        down_acc[...] = jnp.zeros_like(down_acc)

    seq_len = tokens_ref.shape[1]
    slot = lax.broadcasted_iota(jnp.int32, (CAP, seq_len), 0)
    match = code_ref[0] == slot
    dispatch = jnp.where(match, 1.0, 0.0).astype(bf16)
    slot_gate = jnp.sum(jnp.where(match, gate_ref[0], 0.0), axis=1, keepdims=True)
    expert_in = jnp.dot(dispatch, tokens_ref[0], preferred_element_type=f32).astype(bf16)
    gate_pre = jnp.dot(expert_in, both[:, :hidden], preferred_element_type=f32)
    up_pre = jnp.dot(expert_in, both[:, hidden:], preferred_element_type=f32)
    sigmoid = 1.0 / (1.0 + jnp.exp(-gate_pre))
    silu = gate_pre * sigmoid
    hidden_act = (silu * up_pre).astype(bf16)
    expert_out = jnp.dot(hidden_act, down[...], preferred_element_type=f32)
    weighted = (slot_gate * expert_out).astype(bf16)
    moe = contract(dispatch, weighted, 0, 0)
    if carried:
        moe = moe + moe_in[0].astype(f32)
    put(0, moe.astype(bf16))

    slot_grad = jnp.dot(dispatch, grad_ref[0], preferred_element_type=f32)
    raw_grad = contract(slot_grad.astype(bf16), down[...], 1, 1)
    slot_gate_grad = jnp.sum(hidden_act.astype(f32) * raw_grad, axis=1, keepdims=True)
    pair_ref[0] = jnp.sum(jnp.where(match, slot_gate_grad, 0.0), axis=0, keepdims=True)
    hidden_grad = slot_gate * raw_grad
    gate_grad = (
        hidden_grad * up_pre * sigmoid * (1.0 + gate_pre * (1.0 - sigmoid))
    ).astype(bf16)
    up_grad = (hidden_grad * silu).astype(bf16)
    down_acc[...] += contract(hidden_act, (slot_gate * slot_grad).astype(bf16), 0, 0)
    both_acc[:, :hidden] += contract(expert_in, gate_grad, 0, 0)
    both_acc[:, hidden:] += contract(expert_in, up_grad, 0, 0)
    in_grad = (
        contract(gate_grad, both[:, :hidden], 1, 1) + contract(up_grad, both[:, hidden:], 1, 1)
    ).astype(bf16)
    normed = contract(dispatch, in_grad, 0, 0)
    if carried:
        normed = normed + normed_in[0].astype(f32)
    put(1, normed.astype(bf16))

    @pl.when(step == pl.num_programs(0) - 1)
    def _():
        for z, rel, both_at, down_at in places():
            part_ref[z, 0, rel, :both_rows, :] = both_acc[both_at, :].astype(bf16)
            part_ref[z, 0, rel, both_rows:, :] = down_acc[down_at, :].astype(bf16)


def run_expert(
    member, tokens, grads, code, gate, weight, source, bunch, place, last, carry, shared
):
    sequences, seq_len, width = tokens.shape
    shards_z, held, members, rows, both_width = weight.shape
    hidden = both_width // 2
    per_seq = pl.BlockSpec((1, seq_len, width), lambda s: (s, 0, 0))
    per_row = pl.BlockSpec((1, 1, seq_len), lambda s: (s, 0, 0))
    one = (shards_z, 1, members, rows, both_width)
    every = pl.BlockSpec(one, lambda s: (0, source, 0, 0, 0), pipeline_mode=pl.Buffered(1))
    part = pl.BlockSpec(one, lambda s: (0, place, 0, 0, 0))
    slots = sequences * CAP
    if last:
        near = pl.BlockSpec((1, seq_len, width), lambda s: (jnp.minimum(s, 2), 0, 0))
        far = pl.BlockSpec((1, seq_len, width), lambda s: (jnp.maximum(s - 2, 0), 0, 0))
        sums = [near, far, near, far]
        sum_shapes = [
            jax.ShapeDtypeStruct((count, seq_len, width), bf16) for count in (3, 2, 3, 2)
        ]
    else:
        sums, sum_shapes = [per_seq] * 2, [jax.ShapeDtypeStruct(tokens.shape, bf16)] * 2
    return pl.pallas_call(
        functools.partial(expert_kernel, bool(carry), bool(shared), last),
        grid=(sequences,),
        in_specs=[
            pl.BlockSpec(memory_space=pltpu.SMEM),
            per_seq,
            per_seq,
            per_row,
            per_row,
            every,
        ]
        + [per_seq] * len(carry)
        + [pl.BlockSpec(memory_space=pl.ANY)] * len(shared),
        out_specs=sums + [per_row, part],
        out_shape=sum_shapes
        + [
            jax.ShapeDtypeStruct((sequences, 1, seq_len), f32),
            jax.ShapeDtypeStruct((shards_z, bunch, members, rows, both_width), bf16),
        ],
        scratch_shapes=[
            pltpu.VMEM((width, both_width), bf16),
            pltpu.VMEM((hidden, width), bf16),
            pltpu.VMEM((width, both_width), f32),
            pltpu.VMEM((hidden, width), f32),
        ],
        compiler_params=pltpu.CompilerParams(vmem_limit_bytes=66_000_000),
        cost_estimate=pl.CostEstimate(
            flops=2 * slots * width * (4 * seq_len + 9 * hidden),
            bytes_accessed=12 * sequences * seq_len * width + 4 * (weight.size // held),
            transcendentals=slots * hidden,
        ),
        name="expert",
        input_output_aliases={6 + len(carry): len(sums) + 1} if shared else {},
    )(member, tokens, grads, code, gate, weight, *carry, *shared)


def shards(
    sizes,
    block_input,
    positions,
    expert_ids,
    attn_gain,
    query_weight,
    kv_weight,
    out_weight,
    ffn_gain,
    router_weight,
    gate_weight,
    up_weight,
    down_weight,
    out_grad,
):
    tensor_size, z_size = sizes["tensor"], sizes["z"]
    seq_len = positions.shape[0]
    width = block_input.shape[1]
    shard_rows, groups = kv_weight.shape[:2]
    q_width = query_weight.shape[1]
    wide = 2 * q_width
    expert_count = router_weight.shape[1]
    experts_local = gate_weight.shape[0]
    owned = experts_local // 4
    hidden = gate_weight.shape[2]
    my_z, my_y, my_core = lax.axis_index("z"), lax.axis_index("y"), lax.axis_index("core")
    my_tensor = lax.axis_index("tensor")
    y_first, core_first, tensor_first = my_y == 0, my_core == 0, my_tensor == 0

    def at(values, index):
        return lax.dynamic_index_in_dim(values, index, 0, keepdims=False)

    def stacked(mine, theirs, is_first, axis=1):
        ordered = [jnp.where(is_first, mine, theirs), jnp.where(is_first, theirs, mine)]
        return jnp.stack(ordered, axis)

    qkv_shard = jnp.concatenate(
        [query_weight.reshape(shard_rows, groups, -1), kv_weight], axis=2
    ).reshape(shard_rows, wide)
    qkv_full = lax.all_gather(qkv_shard, ("z", "y", "core"), axis=0, tiled=True)

    out_z, step = out_weight.T[None], 1
    while step < z_size:
        other = lax.ppermute(out_z, "z", [(i, i ^ step) for i in range(z_size)])
        high = (my_z // step) % 2 == 1
        out_z = jnp.concatenate(
            [jnp.where(high, other, out_z), jnp.where(high, out_z, other)], axis=0
        )
        step *= 2

    input_rows = block_input.astype(f32)
    attn_normed = (input_rows * row_scale(input_rows) * attn_gain).astype(bf16)
    attn_tokens = gather_rows(attn_normed, tensor_size)
    grad_rows = out_grad.astype(f32)
    moe_rows = after((residual_scale * grad_rows).astype(bf16), attn_tokens)

    experts = jnp.concatenate(
        [jnp.concatenate([gate_weight, up_weight], axis=2), down_weight], axis=1
    )
    rows, both_width = experts.shape[1:]
    grouped = experts.reshape(2, 2, owned, rows, both_width)
    own_y, give_y = at(grouped, my_y), at(grouped, 1 - my_y)
    bunch = min(2, owned)

    def gather_members(near, far):
        return jnp.stack(
            [
                at(near, my_core),
                swap(at(near, 1 - my_core), "core"),
                at(far, my_core),
                swap(at(far, 1 - my_core), "core"),
            ],
            axis=1,
        )

    first_y = swap(give_y[:, :bunch], "y")
    first_members = gather_members(own_y[:, :bunch], first_y)
    moe_own = gather_rows(moe_rows, tensor_size)

    ids_t = expert_ids.T
    hits = jnp.zeros((expert_count, seq_len), jnp.bool_)
    for k in range(ids_t.shape[0]):
        hits = hits | (ids_t[k][None, :] == jnp.arange(expert_count)[:, None])
    token_ids = jnp.arange(seq_len)
    earlier = (token_ids[:, None] < token_ids[None, :]).astype(bf16)
    rank = jnp.dot(hits.astype(bf16), earlier, preferred_element_type=f32)
    code = jnp.where(hits, jnp.where(rank < CAP, rank, -1.0), -2.0)

    lane = jnp.arange(LANES)
    frequency = rope_base ** (-((lane % HALF).astype(f32) * 2.0 / HEAD))
    angles = positions.astype(f32)[:, None] * frequency[None, :]
    cosine = jnp.cos(angles)
    sine = jnp.sin(angles) * jnp.where(lane % HEAD < HALF, -1.0, 1.0)[None, :]

    later_y = [swap(give_y[:, e : e + 1], "y") for e in range(bunch, owned)]
    out_y = stacked(out_z, swap(out_z, "y"), y_first)
    qkv_full, attn_tokens, moe_own, first_members, code, cosine, sine, out_y, *later_y = together(
        qkv_full, attn_tokens, moe_own, first_members, code, cosine, sine, out_y, *later_y
    )
    qkv_pre = jnp.dot(attn_tokens, qkv_full, preferred_element_type=f32)
    qkv_pre, moe_own, code_y = together(qkv_pre, moe_own, swap(code, "y"))
    members = [first_members] + [
        gather_members(own_y[:, e : e + 1], item)
        for e, item in zip(range(bunch, owned), later_y)
    ]
    weights, launched = [], None
    for item in members:
        if launched is not None:
            item = after(item, launched)
        launched = item
        gathered = lax.all_gather(item, "z", axis=0, tiled=False)
        weights += [(gathered, e) for e in range(item.shape[0])]
    out_other = swap(out_y, "core")
    moe_across = swap(moe_own, "y")
    attn_mixed, qkv_rot, log_totals = attention_forward(qkv_pre, cosine, sine)
    attn_mixed, out_other = together(attn_mixed, out_other)
    out_full = jnp.stack(
        [jnp.where(core_first, out_y, out_other), jnp.where(core_first, out_other, out_y)], 2
    ).reshape(width, -1)
    attn_out = scatter_rows(contract(attn_mixed, out_full, 1, 1), tensor_size)
    codes = jnp.stack([code, code_y, swap(code, "core"), swap(code_y, "core")])
    attn_out, moe_across, codes, _ = together(attn_out, moe_across, codes, launched)
    moe_grad = jnp.stack([moe_own, moe_across, swap(moe_own, "core"), swap(moe_across, "core")])
    hidden_state = input_rows + residual_scale * attn_out
    ffn_normed = (hidden_state * row_scale(hidden_state) * ffn_gain).astype(bf16)

    tokens = gather_group(ffn_normed, tensor_size, moe_grad)
    logits = ein("dx,std->sxt", router_weight, tokens)
    chosen = codes > -1.5
    top_logit = jnp.max(jnp.where(chosen, logits, -jnp.inf), axis=1, keepdims=True)
    raised = jnp.where(chosen, jnp.exp(jnp.where(chosen, logits - top_logit, 0.0)), 0.0)
    gates = raised / jnp.sum(raised, axis=1, keepdims=True)
    member = my_y * 2 + my_core
    expert_first = my_tensor * experts_local + member * owned
    code_own = lax.dynamic_slice_in_dim(codes, expert_first, owned, 1).astype(jnp.int32)
    gate_own = lax.dynamic_slice_in_dim(gates, expert_first, owned, 1)

    carry, pairs, parts, shared = (), [], [], ()
    for e in range(owned):
        *carry, pair, part = run_expert(
            member.reshape(1).astype(jnp.int32),
            tokens,
            moe_grad,
            code_own[:, e : e + 1],
            gate_own[:, e : e + 1],
            *weights[e],
            bunch,
            e % bunch,
            e + 1 == owned,
            carry,
            shared,
        )
        pairs.append(pair)
        shared = (part,)
        if (e + 1) % bunch == 0:
            parts.append(lax.psum_scatter(part, "z", scatter_dimension=0, tiled=False))
            shared = ()
    moe_near, moe_give, normed_near, normed_give = carry

    pair_grad = jnp.concatenate(pairs, axis=1)
    pair_given = swap(pair_grad[2:], "core")
    normed_give = after(normed_give, pair_given)
    pair_core = stacked(pair_grad[:2], pair_given, core_first)
    pair_y = in_order(pair_core[0], swap(pair_core[1], "y"), y_first)
    pair_y = pair_y.reshape(experts_local, seq_len)
    if tensor_size == 2:
        local = seq_len // 2
        give = lax.dynamic_slice_in_dim(pair_y, (1 - my_tensor) * local, local, 1)
        keep = lax.dynamic_slice_in_dim(pair_y, my_tensor * local, local, 1)
        pair_all = in_order(keep, swap(give, "tensor"), tensor_first)
    else:
        local = seq_len // tensor_size
        pair_all = lax.all_gather(pair_y, "tensor", axis=0, tiled=True)
        pair_all = lax.dynamic_slice_in_dim(pair_all, my_tensor * local, local, 1)
    normed_given, pair_all = together(swap(normed_give, "core"), pair_all)
    normed_local = scatter_group(normed_near, normed_given, tensor_size)

    def core_owners(part):
        part = jnp.moveaxis(part.reshape(bunch, 2, 2, rows, both_width), 2, 0)
        return stacked(part[0], swap(part[1], "core"), core_first, 0)

    def y_owners(part):
        keep, give = part[:, :, 0], part[:, :, 1]
        return stacked(keep, swap(give, "y"), y_first, 0)

    early = parts[:-1]
    moe_given = swap(after(moe_give, normed_given), "core")
    normed_local, moe_given = together(normed_local, moe_given)
    gates_local = lax.dynamic_slice_in_dim(gates[0], my_tensor * local, local, 1)
    gate_dot = jnp.sum(gates_local * pair_all, axis=0, keepdims=True)
    logit_low = (gates_local * (pair_all - gate_dot)).astype(bf16)

    normed_local = normed_local + contract(logit_low, router_weight, 0, 1)
    router_part = jnp.dot(logit_low, ffn_normed, preferred_element_type=f32)
    state_grad, ffn_gain_part = norm_backward(normed_local, hidden_state, ffn_gain)
    state_grad = state_grad + grad_rows
    attn_grad_all = gather_rows((residual_scale * state_grad).astype(bf16), tensor_size)
    if tensor_size == 2:
        local = seq_len // 2
        moe_piece = functools.partial(piece, moe_near, moe_given)
        moe_far = moe_piece(1, 1 - my_tensor, local).astype(bf16)
        moe_far, moe_given = together(moe_far, moe_given)
        moe_piece = functools.partial(piece, moe_near, moe_given)
        moe_own_far = moe_piece(1, my_tensor, local).astype(bf16)
    else:
        moe_far = add(moe_near[1], moe_given[1]).astype(bf16)
        moe_own_far = jnp.zeros((1, width), bf16)
    attn_grad_all, moe_far, moe_own_far = together(
        attn_grad_all, swap(moe_far, "y"), moe_own_far
    )
    early = [core_owners(after(part, attn_grad_all)) for part in early]
    moe_own_far = swap(moe_own_far, "y")

    def halves(part, mine):
        return at(part, mine), at(part, 1 - mine).astype(bf16)

    def by_dp(part):
        return part.reshape(z_size, 2, 2, shard_rows, part.shape[1])

    mixed_grad = jnp.dot(attn_grad_all, out_full, preferred_element_type=f32).astype(bf16)
    qkv_pre_grad = attention_backward(qkv_rot, mixed_grad, log_totals, cosine, sine)
    qkv_pre_grad, moe_own_far, *early = together(qkv_pre_grad, moe_own_far, *early)

    attn_part = contract(qkv_pre_grad, qkv_full, 1, 1)
    attn_scattered = scatter_rows(attn_part, tensor_size)
    tokens_late, grads_late, _ = together(attn_tokens, attn_grad_all, attn_part)
    qkv_part = contract(tokens_late, qkv_pre_grad, 0, 0)
    qkv_keep, qkv_give = halves(jnp.moveaxis(by_dp(qkv_part), 2, 0), my_core)
    out_part = contract(grads_late, attn_mixed, 0, 0)
    out_keep, out_give = halves(jnp.moveaxis(by_dp(out_part), 2, 0), my_core)
    attn_normed_grad, qkv_given, out_given, *owners = together(
        attn_scattered,
        swap(qkv_give, "core"),
        swap(out_give, "core"),
        *[y_owners(after(part, qkv_pre_grad)) for part in early],
    )
    input_part, attn_gain_part = norm_backward(attn_normed_grad, input_rows, attn_gain)
    input_grad = (state_grad + input_part).astype(bf16)
    small = jnp.concatenate(
        [router_part, ffn_gain_part[None, :], attn_gain_part[None, :]], axis=0
    )
    if tensor_size == 2:
        moe_sum = add(moe_piece(0, my_tensor, local), moe_own_far)
        moe_given = swap(
            add(moe_piece(0, 1 - my_tensor, local), moe_far).astype(bf16), "tensor"
        )
    else:
        moe_sum = jnp.zeros((local, width), f32)
        moe_given = scatter_rows(add(add(moe_near[0], moe_given[0]), moe_far), tensor_size)
    qkv_keep, qkv_give = halves(jnp.moveaxis(add(qkv_keep, qkv_given), 1, 0), my_y)
    out_keep, out_give = halves(jnp.moveaxis(add(out_keep, out_given), 1, 0), my_y)
    small = butterfly_sum(small, (("core", 2), ("tensor", tensor_size)))
    small, qkv_given, out_given, moe_given = together(
        small, swap(qkv_give, "y"), swap(out_give, "y"), moe_given
    )
    late = core_owners(after(parts[-1], small))
    dp_sum = jnp.concatenate([add(qkv_keep, qkv_given), add(out_keep, out_given)], axis=-1)

    def z_pairs(step):
        return [(i, i ^ step) for i in range(z_size)]

    def z_halve(part, step):
        part = jnp.moveaxis(part.reshape(-1, 2, shard_rows, part.shape[-1]), 1, 0)
        keep, give = halves(part, (my_z // step) % 2)
        return add(keep, lax.ppermute(give, "z", z_pairs(step)))

    small = butterfly_sum(small, (("y", 2),))
    step = 1
    while step < z_size:
        if 2 * step == z_size:
            dp_sum, small, late = together(dp_sum, small, late)
        dp_sum = z_halve(dp_sum, step)
        small = small + lax.ppermute(small, "z", z_pairs(step))
        step *= 2
    dp_sum = dp_sum.reshape(shard_rows, dp_sum.shape[-1])
    late = y_owners(late)
    qkv_sum, out_sum = dp_sum[:, :wide], dp_sum[:, wide:]
    block_output = (hidden_state + residual_scale * add(moe_sum, moe_given)).astype(bf16)
    owners.append(late)
    summed = jnp.concatenate(owners, axis=2)
    summed = summed.reshape(experts_local, rows, both_width)
    both_rows = gate_weight.shape[1]
    qkv_sum = qkv_sum.reshape(shard_rows, groups, -1)
    return (
        block_output,
        input_grad,
        small[expert_count + 1],
        qkv_sum[:, :, : 2 * HEAD].reshape(query_weight.shape).astype(f32),
        qkv_sum[:, :, 2 * HEAD :].astype(f32),
        out_sum.T.astype(f32),
        small[expert_count],
        small[:expert_count].T,
        summed[:, :both_rows, :hidden].astype(f32),
        summed[:, :both_rows, hidden:].astype(f32),
        summed[:, both_rows:].astype(f32),
    )


def solution(mesh):
    dp, tensor = mesh.shape["dp"], mesh.shape["tensor"]
    fine = Mesh(mesh.devices.reshape(dp // 4, 2, 2, tensor), ("z", "y", "core", "tensor"))
    rows = ("z", "y", "core")
    every = rows + ("tensor",)
    experts = P("tensor", rows, None)
    return jax.shard_map(
        functools.partial(shards, dict(fine.shape)),
        mesh=fine,
        in_specs=(
            P(every, None),
            P(rows),
            P(rows, None),
            P(),
            P(rows, "tensor"),
            P(rows, "tensor", None),
            P("tensor", rows),
            P(),
            P(),
            experts,
            experts,
            experts,
            P(every, None),
        ),
        out_specs=(
            P(every, None),
            P(every, None),
            P(),
            P(rows, "tensor"),
            P(rows, "tensor", None),
            P("tensor", rows),
            P(),
            P(),
            experts,
            experts,
            experts,
        ),
        check_vma=False,
    )
```

```python
import functools

import jax
import jax.numpy as jnp
from jax import lax
from jax.experimental import pallas as pl
from jax.experimental.pallas import tpu as pltpu
from jax.sharding import Mesh, PartitionSpec as P

CAP = 320
HEAD = 64
HALF = HEAD // 2
LANES = 2 * HEAD
BLOCK = 256
norm_eps = 1e-06
attn_scale = 0.015625
residual_scale = 0.22
rope_base = 10000.0
masked_score = -1e30
f32 = jnp.float32
bf16 = jnp.bfloat16


def row_scale(values):
    return lax.rsqrt(jnp.mean(values * values, axis=-1, keepdims=True) + norm_eps)


def contract(left, right, left_dim, right_dim):
    return lax.dot_general(
        left, right, (((left_dim,), (right_dim,)), ((), ())), preferred_element_type=f32
    )


def ein(spec, *operands):
    return jnp.einsum(spec, *operands, preferred_element_type=f32)


def norm_backward(normed_grad, source, gain):
    scale_rows = row_scale(source)
    unit_rows = source * scale_rows
    scaled_grad = normed_grad * gain
    gain_grad = jnp.sum(normed_grad * unit_rows, axis=0)
    source_grad = scale_rows * (
        scaled_grad - unit_rows * jnp.mean(scaled_grad * unit_rows, axis=-1, keepdims=True)
    )
    return (source_grad, gain_grad)


def together(*values):
    return lax.optimization_barrier(values)


def after(values, *earlier):
    return lax.optimization_barrier((values,) + earlier)[0]


def swap(values, axis):
    return lax.ppermute(values, axis, [(0, 1), (1, 0)])


def butterfly_sum(values, sizes):
    for axis, size in sizes:
        step = 1
        while step < size:
            values = values + lax.ppermute(values, axis, [(i, i ^ step) for i in range(size)])
            step *= 2
    return values


def in_order(mine, theirs, first):
    return jnp.concatenate(
        [jnp.where(first, mine, theirs), jnp.where(first, theirs, mine)], axis=0
    )


def gather_rows(rows, tensor_size):
    if tensor_size != 2:
        return lax.all_gather(rows, "tensor", axis=0, tiled=True)
    return in_order(rows, swap(rows, "tensor"), lax.axis_index("tensor") == 0)


def scatter_rows(values, tensor_size):
    if tensor_size != 2:
        return lax.psum_scatter(
            values.astype(bf16), "tensor", scatter_dimension=0, tiled=True
        ).astype(f32)
    half = values.shape[0] // 2
    me = lax.axis_index("tensor")
    give = lax.dynamic_slice_in_dim(values, (1 - me) * half, half, 0).astype(bf16)
    keep = lax.dynamic_slice_in_dim(values, me * half, half, 0)
    return keep.astype(f32) + swap(give, "tensor").astype(f32)


def gather_group(rows, tensor_size, earlier):
    if tensor_size != 2:
        own = gather_rows(rows, tensor_size)
        across = swap(own, "y")
    else:
        first = lax.axis_index("tensor") == 0
        half = rows.shape[0] // 2
        by_tensor, by_y, _ = together(swap(rows, "tensor"), swap(rows, "y"), earlier)
        own = in_order(rows, by_tensor, first)
        low, high, own_core = together(
            swap(by_y[:half], "tensor"), swap(by_tensor[half:], "y"), swap(own, "core")
        )
        corner = jnp.concatenate([low, high], axis=0)
        across = in_order(by_y, corner, first)
        return jnp.stack([own, across, own_core, swap(across, "core")])
    return jnp.stack([own, across, swap(own, "core"), swap(across, "core")])


def add(keep, given):
    return keep.astype(f32) + given.astype(f32)


def piece(near, given, sequence, which, rows):
    start = (jnp.int32(sequence), which.astype(jnp.int32) * rows, jnp.int32(0))
    shape = (1, rows, near.shape[2])
    return add(lax.dynamic_slice(near, start, shape), lax.dynamic_slice(given, start, shape))[0]


def scatter_group(near, given, tensor_size):
    if tensor_size != 2:
        own, across = add(near[0], given[0]), add(near[1], given[1])
        own = own + swap(across.astype(bf16), "y").astype(f32)
        return scatter_rows(own, tensor_size)
    me = lax.axis_index("tensor")
    rows = near.shape[1] // 2
    half = rows // 2
    take = functools.partial(piece, near, given)
    corner = take(1, 1 - me, rows).astype(bf16)
    corner, near, given = together(corner, near, given)
    take = functools.partial(piece, near, given)
    low, high = swap(corner[:half], "tensor"), swap(corner[half:], "y")
    by_tensor, by_y = take(0, 1 - me, rows), take(1, me, rows)
    first_tensor = swap(by_tensor[:half].astype(bf16), "tensor")
    first_y = swap(by_y[half:].astype(bf16), "y")
    low, high = together(low, high)
    rest_tensor = swap(add(by_tensor[half:], high).astype(bf16), "tensor")
    rest_y = swap(add(by_y[:half], low).astype(bf16), "y")
    first_tensor, first_y, rest_tensor, rest_y = together(
        first_tensor, first_y, rest_tensor, rest_y
    )
    mine = take(0, me, rows)
    return mine + add(
        jnp.concatenate([first_tensor, rest_tensor], axis=0),
        jnp.concatenate([rest_y, first_y], axis=0),
    )


def rope_lanes(values, cosine, sine, first, direction):
    lanes = values.shape[1]
    turned = jnp.where(
        first, pltpu.roll(values, lanes - HALF, 1), pltpu.roll(values, HALF, 1)
    )
    return values * cosine + direction * (turned * sine)


def lane_ids(rows):
    return lax.broadcasted_iota(jnp.int32, (rows, LANES), 1)


def attention_forward_kernel(pre_ref, cos_ref, sin_ref, mixed_ref, rot_ref, lse_ref):
    seq_len = pre_ref.shape[0]
    lane = lane_ids(seq_len)
    first = (lane & (2 * HALF - 1)) < HALF
    low = lane < HEAD
    cosine, sine = cos_ref[...], sin_ref[...]
    query = rope_lanes(pre_ref[:, :LANES], cosine, sine, first, 1.0).astype(bf16)
    kv = pre_ref[:, LANES:]
    kv = jnp.where(low, rope_lanes(kv, cosine, sine, first, 1.0), kv)
    rot_ref[:, :LANES] = query
    rot_ref[:, LANES:] = kv.astype(bf16)
    keys, values_in = head_pairs(kv, low)
    block = min(BLOCK, seq_len)
    for start in range(0, seq_len, block):
        stop = start + block
        total = jnp.zeros((block, LANES), f32)
        lses = []
        for head in (0, 1):
            scores = (
                contract(query[start:stop], keys[head][:stop], 1, 1) * attn_scale
            )
            scores = causal_scores(scores, start)
            top = jnp.max(scores, axis=1, keepdims=True)
            raised = jnp.exp(scores - top)
            summed = jnp.sum(raised, axis=1, keepdims=True)
            prob = (raised * (1.0 / summed)).astype(bf16)
            total = total + jnp.dot(prob, values_in[head][:stop], preferred_element_type=f32)
            lses.append(top + jnp.log(summed))
        mixed_ref[start:stop, :] = total.astype(bf16)
        lse_ref[start:stop, :] = jnp.where(lane_ids(block) < HEAD, lses[0], lses[1])


def head_pairs(kv, low):
    kv = kv.astype(f32)
    turned = pltpu.roll(kv, HEAD, 1)
    zero = jnp.zeros_like(kv)
    keys = [jnp.where(low, kv, zero).astype(bf16), jnp.where(low, zero, turned).astype(bf16)]
    values_in = [jnp.where(low, turned, zero).astype(bf16), jnp.where(low, zero, kv).astype(bf16)]
    return keys, values_in


def causal_scores(scores, start):
    rows = scores.shape[0]
    last = jnp.where(causal(rows, rows, 0), scores[:, start:], masked_score)
    return last if start == 0 else jnp.concatenate([scores[:, :start], last], axis=1)


def causal(rows, columns, start):
    return lax.broadcasted_iota(jnp.int32, (rows, columns), 1) <= start + lax.broadcasted_iota(
        jnp.int32, (rows, columns), 0
    )


def attention_backward_kernel(
    rot_ref, grad_ref, lse_ref, cos_ref, sin_ref, out_ref, key_acc, value_acc
):
    seq_len = rot_ref.shape[0]
    lane = lane_ids(seq_len)
    first = (lane & (2 * HALF - 1)) < HALF
    low = lane < HEAD
    cosine, sine = cos_ref[...], sin_ref[...]
    keys, values_in = head_pairs(rot_ref[:, LANES:], low)
    key_acc[...] = jnp.zeros_like(key_acc)
    value_acc[...] = jnp.zeros_like(value_acc)
    block = min(BLOCK, seq_len)
    for start in range(0, seq_len, block):
        stop = start + block
        query = rot_ref[start:stop, :LANES]
        grad = grad_ref[start:stop, :]
        query_grad = jnp.zeros((block, LANES), f32)
        for head in (0, 1):
            scores = contract(query, keys[head][:stop], 1, 1) * attn_scale
            log_total = lse_ref[start:stop, head * HEAD : head * HEAD + 1]
            prob = jnp.exp(causal_scores(scores, start) - log_total)
            prob_grad = contract(grad, values_in[head][:stop], 1, 1)
            row_dot = jnp.sum(prob * prob_grad, axis=1, keepdims=True)
            score_grad = (prob * (prob_grad - row_dot)).astype(bf16)
            query_grad = query_grad + jnp.dot(
                score_grad, keys[head][:stop], preferred_element_type=f32
            )
            key_acc[head, :stop, :] += contract(score_grad, query, 0, 0)
            value_acc[head, :stop, :] += contract(prob.astype(bf16), grad, 0, 0)
        lane_block = (lane_ids(block) & (2 * HALF - 1)) < HALF
        out_ref[start:stop, :LANES] = rope_lanes(
            query_grad * attn_scale, cosine[start:stop], sine[start:stop], lane_block, -1.0
        ).astype(bf16)
    key_grad = (key_acc[0] + pltpu.roll(key_acc[1], HEAD, 1)) * attn_scale
    key_grad = rope_lanes(jnp.where(low, key_grad, 0.0), cosine, sine, first, -1.0)
    value_grad = pltpu.roll(value_acc[0], HEAD, 1) + value_acc[1]
    out_ref[:, LANES:] = jnp.where(low, key_grad, value_grad).astype(bf16)


def by_head(width):
    return lambda seq_len: pl.BlockSpec((seq_len, width), lambda g: (0, g))


def attention_forward(pre, cosine, sine):
    seq_len, width = pre.shape
    groups = width // (2 * LANES)
    whole = pl.BlockSpec((seq_len, LANES), lambda g: (0, 0))
    wide, narrow = by_head(2 * LANES)(seq_len), by_head(LANES)(seq_len)
    return pl.pallas_call(
        attention_forward_kernel,
        grid=(groups,),
        in_specs=[wide, whole, whole],
        out_specs=[narrow, wide, narrow],
        out_shape=[
            jax.ShapeDtypeStruct((seq_len, width // 2), bf16),
            jax.ShapeDtypeStruct((seq_len, width), bf16),
            jax.ShapeDtypeStruct((seq_len, width // 2), f32),
        ],
        cost_estimate=pl.CostEstimate(
            flops=6 * groups * seq_len * seq_len * LANES,
            bytes_accessed=10 * seq_len * width,
            transcendentals=groups * seq_len * seq_len,
        ),
        name="attention_forward",
    )(pre, cosine, sine)


def attention_backward(rot, grad, lse, cosine, sine):
    seq_len, width = rot.shape
    groups = width // (2 * LANES)
    whole = pl.BlockSpec((seq_len, LANES), lambda g: (0, 0))
    wide, narrow = by_head(2 * LANES)(seq_len), by_head(LANES)(seq_len)
    return pl.pallas_call(
        attention_backward_kernel,
        grid=(groups,),
        in_specs=[wide, narrow, narrow, whole, whole],
        out_specs=wide,
        out_shape=jax.ShapeDtypeStruct((seq_len, width), bf16),
        scratch_shapes=[pltpu.VMEM((2, seq_len, LANES), f32)] * 2,
        cost_estimate=pl.CostEstimate(
            flops=16 * groups * seq_len * seq_len * LANES,
            bytes_accessed=10 * seq_len * width,
            transcendentals=groups * seq_len * seq_len,
        ),
        name="attention_backward",
    )(rot, grad, lse, cosine, sine)


def expert_kernel(
    carried, shared, last, member_ref, tokens_ref, grad_ref, code_ref, gate_ref, weight_ref, *refs
):
    if carried:
        moe_in, normed_in, *refs = refs
    if shared:
        refs = refs[1:]
    *sum_refs, pair_ref, part_ref, both, down, both_acc, down_acc = refs
    step = pl.program_id(0)

    def put(place, values):
        if not last:
            sum_refs[place][0] = values
            return

        sum_refs[2 * place][0] = values
        sum_refs[2 * place + 1][0] = values
    shards_z, members, rows = weight_ref.shape[0], weight_ref.shape[2], weight_ref.shape[3]
    hidden = down.shape[0]
    both_rows = both.shape[0] // (shards_z * members)
    down_rows = hidden // (shards_z * members)

    def places():
        for z in range(shards_z):
            for rel in range(members):
                at = z * members + (member_ref[0] ^ rel)
                yield (
                    z,
                    rel,
                    pl.ds(pl.multiple_of(at * both_rows, both_rows), both_rows),
                    pl.ds(pl.multiple_of(at * down_rows, down_rows), down_rows),
                )

    @pl.when(step == 0)
    def _():
        for z, rel, both_at, down_at in places():
            both[both_at, :] = weight_ref[z, 0, rel, :both_rows, :]
            down[down_at, :] = weight_ref[z, 0, rel, both_rows:, :]
        both_acc[...] = jnp.zeros_like(both_acc)
        down_acc[...] = jnp.zeros_like(down_acc)

    seq_len = tokens_ref.shape[1]
    slot = lax.broadcasted_iota(jnp.int32, (CAP, seq_len), 0)
    match = code_ref[0] == slot
    dispatch = jnp.where(match, 1.0, 0.0).astype(bf16)
    slot_gate = jnp.sum(jnp.where(match, gate_ref[0], 0.0), axis=1, keepdims=True)
    expert_in = jnp.dot(dispatch, tokens_ref[0], preferred_element_type=f32).astype(bf16)
    gate_pre = jnp.dot(expert_in, both[:, :hidden], preferred_element_type=f32)
    up_pre = jnp.dot(expert_in, both[:, hidden:], preferred_element_type=f32)
    sigmoid = 1.0 / (1.0 + jnp.exp(-gate_pre))
    silu = gate_pre * sigmoid
    hidden_act = (silu * up_pre).astype(bf16)
    expert_out = jnp.dot(hidden_act, down[...], preferred_element_type=f32)
    weighted = (slot_gate * expert_out).astype(bf16)
    moe = contract(dispatch, weighted, 0, 0)
    if carried:
        moe = moe + moe_in[0].astype(f32)
    put(0, moe.astype(bf16))

    slot_grad = jnp.dot(dispatch, grad_ref[0], preferred_element_type=f32)
    raw_grad = contract(slot_grad.astype(bf16), down[...], 1, 1)
    slot_gate_grad = jnp.sum(hidden_act.astype(f32) * raw_grad, axis=1, keepdims=True)
    pair_ref[0] = jnp.sum(jnp.where(match, slot_gate_grad, 0.0), axis=0, keepdims=True)
    hidden_grad = slot_gate * raw_grad
    gate_grad = (
        hidden_grad * up_pre * sigmoid * (1.0 + gate_pre * (1.0 - sigmoid))
    ).astype(bf16)
    up_grad = (hidden_grad * silu).astype(bf16)
    down_acc[...] += contract(hidden_act, (slot_gate * slot_grad).astype(bf16), 0, 0)
    both_acc[:, :hidden] += contract(expert_in, gate_grad, 0, 0)
    both_acc[:, hidden:] += contract(expert_in, up_grad, 0, 0)
    in_grad = (
        contract(gate_grad, both[:, :hidden], 1, 1) + contract(up_grad, both[:, hidden:], 1, 1)
    ).astype(bf16)
    normed = contract(dispatch, in_grad, 0, 0)
    if carried:
        normed = normed + normed_in[0].astype(f32)
    put(1, normed.astype(bf16))

    @pl.when(step == pl.num_programs(0) - 1)
    def _():
        for z, rel, both_at, down_at in places():
            part_ref[z, 0, rel, :both_rows, :] = both_acc[both_at, :].astype(bf16)
            part_ref[z, 0, rel, both_rows:, :] = down_acc[down_at, :].astype(bf16)


def run_expert(
    member, tokens, grads, code, gate, weight, source, bunch, place, last, carry, shared
):
    sequences, seq_len, width = tokens.shape
    shards_z, held, members, rows, both_width = weight.shape
    hidden = both_width // 2
    per_seq = pl.BlockSpec((1, seq_len, width), lambda s: (s, 0, 0))
    per_row = pl.BlockSpec((1, 1, seq_len), lambda s: (s, 0, 0))
    one = (shards_z, 1, members, rows, both_width)
    every = pl.BlockSpec(one, lambda s: (0, source, 0, 0, 0), pipeline_mode=pl.Buffered(1))
    part = pl.BlockSpec(one, lambda s: (0, place, 0, 0, 0))
    slots = sequences * CAP
    if last:
        near = pl.BlockSpec((1, seq_len, width), lambda s: (jnp.minimum(s, 2), 0, 0))
        far = pl.BlockSpec((1, seq_len, width), lambda s: (jnp.maximum(s - 2, 0), 0, 0))
        sums = [near, far, near, far]
        sum_shapes = [
            jax.ShapeDtypeStruct((count, seq_len, width), bf16) for count in (3, 2, 3, 2)
        ]
    else:
        sums, sum_shapes = [per_seq] * 2, [jax.ShapeDtypeStruct(tokens.shape, bf16)] * 2
    return pl.pallas_call(
        functools.partial(expert_kernel, bool(carry), bool(shared), last),
        grid=(sequences,),
        in_specs=[
            pl.BlockSpec(memory_space=pltpu.SMEM),
            per_seq,
            per_seq,
            per_row,
            per_row,
            every,
        ]
        + [per_seq] * len(carry)
        + [pl.BlockSpec(memory_space=pl.ANY)] * len(shared),
        out_specs=sums + [per_row, part],
        out_shape=sum_shapes
        + [
            jax.ShapeDtypeStruct((sequences, 1, seq_len), f32),
            jax.ShapeDtypeStruct((shards_z, bunch, members, rows, both_width), bf16),
        ],
        scratch_shapes=[
            pltpu.VMEM((width, both_width), bf16),
            pltpu.VMEM((hidden, width), bf16),
            pltpu.VMEM((width, both_width), f32),
            pltpu.VMEM((hidden, width), f32),
        ],
        compiler_params=pltpu.CompilerParams(vmem_limit_bytes=66_000_000),
        cost_estimate=pl.CostEstimate(
            flops=2 * slots * width * (4 * seq_len + 9 * hidden),
            bytes_accessed=12 * sequences * seq_len * width + 4 * (weight.size // held),
            transcendentals=slots * hidden,
        ),
        name="expert",
        input_output_aliases={6 + len(carry): len(sums) + 1} if shared else {},
    )(member, tokens, grads, code, gate, weight, *carry, *shared)


def shards(
    sizes,
    block_input,
    positions,
    expert_ids,
    attn_gain,
    query_weight,
    kv_weight,
    out_weight,
    ffn_gain,
    router_weight,
    gate_weight,
    up_weight,
    down_weight,
    out_grad,
):
    tensor_size, z_size = sizes["tensor"], sizes["z"]
    seq_len = positions.shape[0]
    width = block_input.shape[1]
    shard_rows, groups = kv_weight.shape[:2]
    q_width = query_weight.shape[1]
    wide = 2 * q_width
    expert_count = router_weight.shape[1]
    experts_local = gate_weight.shape[0]
    owned = experts_local // 4
    hidden = gate_weight.shape[2]
    my_z, my_y, my_core = lax.axis_index("z"), lax.axis_index("y"), lax.axis_index("core")
    my_tensor = lax.axis_index("tensor")
    y_first, core_first, tensor_first = my_y == 0, my_core == 0, my_tensor == 0

    def at(values, index):
        return lax.dynamic_index_in_dim(values, index, 0, keepdims=False)

    def stacked(mine, theirs, is_first, axis=1):
        ordered = [jnp.where(is_first, mine, theirs), jnp.where(is_first, theirs, mine)]
        return jnp.stack(ordered, axis)

    qkv_shard = jnp.concatenate(
        [query_weight.reshape(shard_rows, groups, -1), kv_weight], axis=2
    ).reshape(shard_rows, wide)
    qkv_full = lax.all_gather(qkv_shard, ("z", "y", "core"), axis=0, tiled=True)

    out_z, step = out_weight.T[None], 1
    while step < z_size:
        other = lax.ppermute(out_z, "z", [(i, i ^ step) for i in range(z_size)])
        high = (my_z // step) % 2 == 1
        out_z = jnp.concatenate(
            [jnp.where(high, other, out_z), jnp.where(high, out_z, other)], axis=0
        )
        step *= 2

    input_rows = block_input.astype(f32)
    attn_normed = (input_rows * row_scale(input_rows) * attn_gain).astype(bf16)
    attn_tokens = gather_rows(attn_normed, tensor_size)
    grad_rows = out_grad.astype(f32)
    moe_rows = after((residual_scale * grad_rows).astype(bf16), attn_tokens)

    experts = jnp.concatenate(
        [jnp.concatenate([gate_weight, up_weight], axis=2), down_weight], axis=1
    )
    rows, both_width = experts.shape[1:]
    grouped = experts.reshape(2, 2, owned, rows, both_width)
    own_y, give_y = at(grouped, my_y), at(grouped, 1 - my_y)
    bunch = min(2, owned)

    def gather_members(near, far):
        return jnp.stack(
            [
                at(near, my_core),
                swap(at(near, 1 - my_core), "core"),
                at(far, my_core),
                swap(at(far, 1 - my_core), "core"),
            ],
            axis=1,
        )

    first_y = swap(give_y[:, :bunch], "y")
    first_members = gather_members(own_y[:, :bunch], first_y)
    moe_own = gather_rows(moe_rows, tensor_size)

    ids_t = expert_ids.T
    hits = jnp.zeros((expert_count, seq_len), jnp.bool_)
    for k in range(ids_t.shape[0]):
        hits = hits | (ids_t[k][None, :] == jnp.arange(expert_count)[:, None])
    token_ids = jnp.arange(seq_len)
    earlier = (token_ids[:, None] < token_ids[None, :]).astype(bf16)
    rank = jnp.dot(hits.astype(bf16), earlier, preferred_element_type=f32)
    code = jnp.where(hits, jnp.where(rank < CAP, rank, -1.0), -2.0)

    lane = jnp.arange(LANES)
    frequency = rope_base ** (-((lane % HALF).astype(f32) * 2.0 / HEAD))
    angles = positions.astype(f32)[:, None] * frequency[None, :]
    cosine = jnp.cos(angles)
    sine = jnp.sin(angles) * jnp.where(lane % HEAD < HALF, -1.0, 1.0)[None, :]

    later_y = [swap(give_y[:, e : e + 1], "y") for e in range(bunch, owned)]
    out_y = stacked(out_z, swap(out_z, "y"), y_first)
    qkv_full, attn_tokens, moe_own, first_members, code, cosine, sine, out_y, *later_y = together(
        qkv_full, attn_tokens, moe_own, first_members, code, cosine, sine, out_y, *later_y
    )
    qkv_pre = jnp.dot(attn_tokens, qkv_full, preferred_element_type=f32)
    qkv_pre, moe_own, code_y = together(qkv_pre, moe_own, swap(code, "y"))
    members = [first_members] + [
        gather_members(own_y[:, e : e + 1], item)
        for e, item in zip(range(bunch, owned), later_y)
    ]
    weights, launched = [], None
    for item in members:
        if launched is not None:
            item = after(item, launched)
        launched = item
        gathered = lax.all_gather(item, "z", axis=0, tiled=False)
        weights += [(gathered, e) for e in range(item.shape[0])]
    out_other = swap(out_y, "core")
    moe_across = swap(moe_own, "y")
    attn_mixed, qkv_rot, log_totals = attention_forward(qkv_pre, cosine, sine)
    attn_mixed, out_other = together(attn_mixed, out_other)
    out_full = jnp.stack(
        [jnp.where(core_first, out_y, out_other), jnp.where(core_first, out_other, out_y)], 2
    ).reshape(width, -1)
    attn_out = scatter_rows(contract(attn_mixed, out_full, 1, 1), tensor_size)
    codes = jnp.stack([code, code_y, swap(code, "core"), swap(code_y, "core")])
    attn_out, moe_across, codes, _ = together(attn_out, moe_across, codes, launched)
    moe_grad = jnp.stack([moe_own, moe_across, swap(moe_own, "core"), swap(moe_across, "core")])
    hidden_state = input_rows + residual_scale * attn_out
    ffn_normed = (hidden_state * row_scale(hidden_state) * ffn_gain).astype(bf16)

    tokens = gather_group(ffn_normed, tensor_size, moe_grad)
    logits = ein("dx,std->sxt", router_weight, tokens)
    chosen = codes > -1.5
    top_logit = jnp.max(jnp.where(chosen, logits, -jnp.inf), axis=1, keepdims=True)
    raised = jnp.where(chosen, jnp.exp(jnp.where(chosen, logits - top_logit, 0.0)), 0.0)
    gates = raised / jnp.sum(raised, axis=1, keepdims=True)
    member = my_y * 2 + my_core
    expert_first = my_tensor * experts_local + member * owned
    code_own = lax.dynamic_slice_in_dim(codes, expert_first, owned, 1).astype(jnp.int32)
    gate_own = lax.dynamic_slice_in_dim(gates, expert_first, owned, 1)

    carry, pairs, parts, shared = (), [], [], ()
    for e in range(owned):
        *carry, pair, part = run_expert(
            member.reshape(1).astype(jnp.int32),
            tokens,
            moe_grad,
            code_own[:, e : e + 1],
            gate_own[:, e : e + 1],
            *weights[e],
            bunch,
            e % bunch,
            e + 1 == owned,
            carry,
            shared,
        )
        pairs.append(pair)
        shared = (part,)
        if (e + 1) % bunch == 0:
            parts.append(lax.psum_scatter(part, "z", scatter_dimension=0, tiled=False))
            shared = ()
    moe_near, moe_give, normed_near, normed_give = carry

    pair_grad = jnp.concatenate(pairs, axis=1)
    pair_given = swap(pair_grad[2:], "core")
    normed_give = after(normed_give, pair_given)
    pair_core = stacked(pair_grad[:2], pair_given, core_first)
    pair_y = in_order(pair_core[0], swap(pair_core[1], "y"), y_first)
    pair_y = pair_y.reshape(experts_local, seq_len)
    if tensor_size == 2:
        local = seq_len // 2
        give = lax.dynamic_slice_in_dim(pair_y, (1 - my_tensor) * local, local, 1)
        keep = lax.dynamic_slice_in_dim(pair_y, my_tensor * local, local, 1)
        pair_all = in_order(keep, swap(give, "tensor"), tensor_first)
    else:
        local = seq_len // tensor_size
        pair_all = lax.all_gather(pair_y, "tensor", axis=0, tiled=True)
        pair_all = lax.dynamic_slice_in_dim(pair_all, my_tensor * local, local, 1)
    normed_given, pair_all = together(swap(normed_give, "core"), pair_all)
    normed_local = scatter_group(normed_near, normed_given, tensor_size)

    def core_owners(part):
        part = jnp.moveaxis(part.reshape(bunch, 2, 2, rows, both_width), 2, 0)
        return stacked(part[0], swap(part[1], "core"), core_first, 0)

    def y_owners(part):
        keep, give = part[:, :, 0], part[:, :, 1]
        return stacked(keep, swap(give, "y"), y_first, 0)

    early = parts[:-1]
    moe_given = swap(after(moe_give, normed_given), "core")
    normed_local, moe_given = together(normed_local, moe_given)
    gates_local = lax.dynamic_slice_in_dim(gates[0], my_tensor * local, local, 1)
    gate_dot = jnp.sum(gates_local * pair_all, axis=0, keepdims=True)
    logit_low = (gates_local * (pair_all - gate_dot)).astype(bf16)

    normed_local = normed_local + contract(logit_low, router_weight, 0, 1)
    router_part = jnp.dot(logit_low, ffn_normed, preferred_element_type=f32)
    state_grad, ffn_gain_part = norm_backward(normed_local, hidden_state, ffn_gain)
    state_grad = state_grad + grad_rows
    attn_grad_all = gather_rows((residual_scale * state_grad).astype(bf16), tensor_size)
    if tensor_size == 2:
        local = seq_len // 2
        moe_piece = functools.partial(piece, moe_near, moe_given)
        moe_far = moe_piece(1, 1 - my_tensor, local).astype(bf16)
        moe_far, moe_given = together(moe_far, moe_given)
        moe_piece = functools.partial(piece, moe_near, moe_given)
        moe_own_far = moe_piece(1, my_tensor, local).astype(bf16)
    else:
        moe_far = add(moe_near[1], moe_given[1]).astype(bf16)
        moe_own_far = jnp.zeros((1, width), bf16)
    attn_grad_all, moe_far, moe_own_far = together(
        attn_grad_all, swap(moe_far, "y"), moe_own_far
    )
    early = [core_owners(after(part, attn_grad_all)) for part in early]
    moe_own_far = swap(moe_own_far, "y")

    def halves(part, mine):
        return at(part, mine), at(part, 1 - mine).astype(bf16)

    def by_dp(part):
        return part.reshape(z_size, 2, 2, shard_rows, part.shape[1])

    mixed_grad = jnp.dot(attn_grad_all, out_full, preferred_element_type=f32).astype(bf16)
    qkv_pre_grad = attention_backward(qkv_rot, mixed_grad, log_totals, cosine, sine)
    qkv_pre_grad, moe_own_far, *early = together(qkv_pre_grad, moe_own_far, *early)

    attn_part = contract(qkv_pre_grad, qkv_full, 1, 1)
    attn_scattered = scatter_rows(attn_part, tensor_size)
    tokens_late, grads_late, _ = together(attn_tokens, attn_grad_all, attn_part)
    qkv_part = contract(tokens_late, qkv_pre_grad, 0, 0)
    qkv_keep, qkv_give = halves(jnp.moveaxis(by_dp(qkv_part), 2, 0), my_core)
    out_part = contract(grads_late, attn_mixed, 0, 0)
    out_keep, out_give = halves(jnp.moveaxis(by_dp(out_part), 2, 0), my_core)
    attn_normed_grad, qkv_given, out_given, *owners = together(
        attn_scattered,
        swap(qkv_give, "core"),
        swap(out_give, "core"),
        *[y_owners(after(part, qkv_pre_grad)) for part in early],
    )
    input_part, attn_gain_part = norm_backward(attn_normed_grad, input_rows, attn_gain)
    input_grad = (state_grad + input_part).astype(bf16)
    small = jnp.concatenate(
        [router_part, ffn_gain_part[None, :], attn_gain_part[None, :]], axis=0
    )
    if tensor_size == 2:
        moe_sum = add(moe_piece(0, my_tensor, local), moe_own_far)
        moe_given = swap(
            add(moe_piece(0, 1 - my_tensor, local), moe_far).astype(bf16), "tensor"
        )
    else:
        moe_sum = jnp.zeros((local, width), f32)
        moe_given = scatter_rows(add(add(moe_near[0], moe_given[0]), moe_far), tensor_size)
    qkv_keep, qkv_give = halves(jnp.moveaxis(add(qkv_keep, qkv_given), 1, 0), my_y)
    out_keep, out_give = halves(jnp.moveaxis(add(out_keep, out_given), 1, 0), my_y)
    small = butterfly_sum(small, (("core", 2), ("tensor", tensor_size)))
    small, qkv_given, out_given, moe_given = together(
        small, swap(qkv_give, "y"), swap(out_give, "y"), moe_given
    )
    late = core_owners(after(parts[-1], small))
    dp_sum = jnp.concatenate([add(qkv_keep, qkv_given), add(out_keep, out_given)], axis=-1)

    def z_pairs(step):
        return [(i, i ^ step) for i in range(z_size)]

    def z_halve(part, step):
        part = jnp.moveaxis(part.reshape(-1, 2, shard_rows, part.shape[-1]), 1, 0)
        keep, give = halves(part, (my_z // step) % 2)
        return add(keep, lax.ppermute(give, "z", z_pairs(step)))

    small = butterfly_sum(small, (("y", 2),))
    step = 1
    while step < z_size:
        if 2 * step == z_size:
            dp_sum, small, late = together(dp_sum, small, late)
        dp_sum = z_halve(dp_sum, step)
        small = small + lax.ppermute(small, "z", z_pairs(step))
        step *= 2
    dp_sum = dp_sum.reshape(shard_rows, dp_sum.shape[-1])
    late = y_owners(late)
    qkv_sum, out_sum = dp_sum[:, :wide], dp_sum[:, wide:]
    block_output = (hidden_state + residual_scale * add(moe_sum, moe_given)).astype(bf16)
    owners.append(late)
    summed = jnp.concatenate(owners, axis=2)
    summed = summed.reshape(experts_local, rows, both_width)
    both_rows = gate_weight.shape[1]
    qkv_sum = qkv_sum.reshape(shard_rows, groups, -1)
    return (
        block_output,
        input_grad,
        small[expert_count + 1],
        qkv_sum[:, :, : 2 * HEAD].reshape(query_weight.shape).astype(f32),
        qkv_sum[:, :, 2 * HEAD :].astype(f32),
        out_sum.T.astype(f32),
        small[expert_count],
        small[:expert_count].T,
        summed[:, :both_rows, :hidden].astype(f32),
        summed[:, :both_rows, hidden:].astype(f32),
        summed[:, both_rows:].astype(f32),
    )


def solution(mesh):
    dp, tensor = mesh.shape["dp"], mesh.shape["tensor"]
    fine = Mesh(mesh.devices.reshape(dp // 4, 2, 2, tensor), ("z", "y", "core", "tensor"))
    rows = ("z", "y", "core")
    every = rows + ("tensor",)
    experts = P("tensor", rows, None)
    return jax.shard_map(
        functools.partial(shards, dict(fine.shape)),
        mesh=fine,
        in_specs=(
            P(every, None),
            P(rows),
            P(rows, None),
            P(),
            P(rows, "tensor"),
            P(rows, "tensor", None),
            P("tensor", rows),
            P(),
            P(),
            experts,
            experts,
            experts,
            P(every, None),
        ),
        out_specs=(
            P(every, None),
            P(every, None),
            P(),
            P(rows, "tensor"),
            P(rows, "tensor", None),
            P("tensor", rows),
            P(),
            P(),
            experts,
            experts,
            experts,
        ),
        check_vma=False,
    )
```
